32 devices in a mesh: dom: 8 (over y, x, core), rep: 4 (over z).
Axes of the slice: x: 2, y: 2, z: 4, core: 2. Of those that a mesh axis runs over, the one named last changes fastest.
Arguments:
- feature_grid: bfloat16 [8, 32, 32768], P('dom'), may hold values from -6 to 6
- fine_in: bfloat16 [8, 64, 32], P('dom'), may hold values from -1 to 1
- fine_mid: bfloat16 [8, 2, 64, 64], P('dom'), may hold values from -0.75 to 0.75
- fine_out: bfloat16 [8, 64], P('dom'), may hold values from -0.75 to 0.75
- prop_in: bfloat16 [8, 16, 32], P('dom'), may hold values from -1 to 1
- prop_out: bfloat16 [8, 16], P('dom'), may hold values from -1.5 to 1.5
- sample_cells: int32 [8, 4, 8, 2048], P('dom', 'rep'), may hold values from 0 to 31710, as said below
- sample_geometry: bfloat16 [4, 8, 4, 8, 2048], P(None, 'dom', 'rep'), may hold values from 0 to 1, as said below
- slot_ray: int32 [8, 4, 8, 32], P('dom', 'rep'), may hold values from 0 to 255, as said below
- slot_rank: int32 [8, 4, 8, 32], P('dom', 'rep'), may hold values from 0 to 7, as said below
- bucket_count: int32 [8, 4, 8], P('dom', 'rep'), may hold values from 1 to 32, as said below
Outputs:
- ray_loss: float32 [8, 4, 256], P('dom', 'rep')
- prop_in_grad: float32 [8, 16, 32], P('dom')
- prop_out_grad: float32 [8, 16], P('dom')
The draws below stay inside these ranges and needn't reach their ends.
Inputs may be any that keep to these rules, and one draw needn't show every extreme that they name: `sample_cells`: each base cell's three coordinates lie in 0 to 30, so all eight corners are inside the grid. `sample_geometry`: rows 0 to 2 lie in 0 to 1; row 3 is positive. `slot_ray`: within one bucket the rays are distinct. `slot_rank`: live segments of one ray on one device have distinct ranks. `bucket_count`: the live slots of a bucket are its first ones; in every draw one partition receives full buckets from every device.
All inputs are finite; a program needn't handle non-finite values.
Results may differ from the reference program's by a relative error of at most 0.0024.
Values may be sent and summed in bfloat16 or wider, within the bound.
No kernel may reach another device: no remote copies, remote signals or barrier semaphores. Data moves between devices by JAX's collectives and lax.ppermute only.
A program may use at most 192 MiB of HBM per device.

```python
import math
import jax
import jax.numpy as jnp
from jax import lax

S = 64
GR = 32
F = 32
FH = 64
MIDS = 2
PH = 16
CAP = 32
RAY_DEV = 256
N_DOM = 8
N_REP = 4


def draw_sample_cells(key, part):
    array_shape = (N_DOM, N_REP, N_DOM, CAP * S)
    coord_x = jax.random.randint(jax.random.fold_in(key, 1), array_shape, 0, GR - 1)
    coord_y = jax.random.randint(jax.random.fold_in(key, 2), array_shape, 0, GR - 1)
    coord_z = jax.random.randint(jax.random.fold_in(key, 3), array_shape, 0, GR - 1)
    return ((coord_x * GR + coord_y) * GR + coord_z).astype(jnp.int32)


def draw_sample_geometry(key, part):
    array_shape = (N_DOM, N_REP, N_DOM, CAP * S)
    offsets = jax.random.uniform(jax.random.fold_in(key, 4), (3,) + array_shape, jnp.float32)
    lowest, highest = (0.004, 0.02)
    spacing = jnp.exp(jax.random.uniform(jax.random.fold_in(key, 5), (1,) + array_shape, jnp.float32, math.log(lowest), math.log(highest)))
    return jnp.concatenate([offsets, spacing], axis=0).astype(jnp.bfloat16)


def segment_plan(key):
    heaviest = jax.random.randint(jax.random.fold_in(key, 11), (), 0, N_DOM)
    counts = jax.random.randint(jax.random.fold_in(key, 12), (N_DOM, N_REP, N_DOM), 1, max(2, 5 * CAP // 8))
    column = jnp.arange(N_DOM)[None, None, :]
    counts = jnp.where(column == heaviest, CAP, counts).astype(jnp.int32)
    scores = jax.random.randint(jax.random.fold_in(key, 13), (N_DOM, N_REP, N_DOM, RAY_DEV), 0, 2 ** 20) * RAY_DEV + jnp.arange(RAY_DEV)
    ray_ids = jnp.argsort(scores, axis=-1)[..., :CAP].astype(jnp.int32)
    shifts = jax.random.randint(jax.random.fold_in(key, 14), (N_DOM, N_REP, 1, RAY_DEV), 0, N_DOM)
    shifts = jnp.broadcast_to(shifts, (N_DOM, N_REP, N_DOM, RAY_DEV))
    rank_ids = (jnp.take_along_axis(shifts, ray_ids, axis=-1) + column[..., None]) % N_DOM
    return (ray_ids, rank_ids.astype(jnp.int32), counts)


def draw_slot_ray(key, part):
    return segment_plan(key)[0]


def draw_slot_rank(key, part):
    return segment_plan(key)[1]


def draw_bucket_count(key, part):
    return segment_plan(key)[2]


def shard_levels(stream_key, dims, cuts, smallest, high):
    level, own = 1.0, jax.random.fold_in(stream_key, 6)
    for dim, blocks in cuts:
        heights = jnp.exp(jax.random.uniform(jax.random.fold_in(own, dim), (blocks,), jnp.float32, smallest / len(cuts), high / len(cuts)))
        level = level * jnp.repeat(heights, dims[dim] // blocks).reshape([-1 if axis == dim else 1 for axis in range(len(dims))])
    return level


def noise(own_key, extent, scale, reach, split=(), held_as=jnp.bfloat16):
    entries = scale * jax.random.normal(own_key, extent, jnp.float32)
    if split:
        entries = entries * shard_levels(own_key, extent, split, -0.22, 0.18)
    return jnp.clip(entries, -reach, reach).astype(held_as)


def setup_inputs(seed: int = 0) -> dict:
    keys = jax.random.split(jax.random.key(seed), 12)
    feature_grid = noise(keys[0], (N_DOM, F, GR ** 3), 1.0, 6.0, ((0, 8),))
    fine_in = noise(keys[1], (N_DOM, FH, F), F ** -0.5, 1.0, ((0, 8),))
    fine_mid = noise(keys[2], (N_DOM, MIDS, FH, FH), FH ** -0.5, 0.75, ((0, 8),))
    fine_out = noise(keys[3], (N_DOM, FH), FH ** -0.5, 0.75, ((0, 8),))
    prop_in = noise(keys[4], (N_DOM, PH, F), F ** -0.5, 1.0, ((0, 8),))
    prop_out = noise(keys[5], (N_DOM, PH), PH ** -0.5, 1.5, ((0, 8),))
    sample_cells = draw_sample_cells(jax.random.fold_in(keys[11], 71), 0)
    sample_geometry = draw_sample_geometry(jax.random.fold_in(keys[11], 71), 0)
    slot_ray = draw_slot_ray(jax.random.fold_in(keys[11], 71), 0)
    slot_rank = draw_slot_rank(jax.random.fold_in(keys[11], 71), 0)
    bucket_count = draw_bucket_count(jax.random.fold_in(keys[11], 71), 0)
    return {"feature_grid": feature_grid, "fine_in": fine_in, "fine_mid": fine_mid, "fine_out": fine_out, "prop_in": prop_in, "prop_out": prop_out, "sample_cells": sample_cells, "sample_geometry": sample_geometry, "slot_ray": slot_ray, "slot_rank": slot_rank, "bucket_count": bucket_count}


distill_weight = 50.0

def interpolate(feature_grid, cell_index, geometry):
    offsets = geometry[:3].astype(jnp.float32)
    summed = jnp.zeros((feature_grid.shape[0], cell_index.shape[0]), jnp.float32)
    for corner in range(8):
        step_x = corner // 4
        step_y = corner // 2 % 2
        step_z = corner % 2
        shifted = cell_index + (step_x * GR + step_y) * GR + step_z
        factor = (offsets[0] if step_x else 1.0 - offsets[0]) * (offsets[1] if step_y else 1.0 - offsets[1]) * (offsets[2] if step_z else 1.0 - offsets[2])
        summed = summed + jnp.take(feature_grid, shifted, axis=1).astype(jnp.float32) * factor
    return summed.astype(jnp.bfloat16)

def fine_density(fine_in, fine_mid, fine_out, features):
    hidden_units = jax.nn.relu(jnp.dot(fine_in, features, preferred_element_type=jnp.float32)).astype(jnp.bfloat16)
    for layer_index in range(fine_mid.shape[0]):
        hidden_units = jax.nn.relu(jnp.dot(fine_mid[layer_index], hidden_units, preferred_element_type=jnp.float32)).astype(jnp.bfloat16)
    return jax.nn.softplus(jnp.dot(fine_out, hidden_units, preferred_element_type=jnp.float32))

def proposal_parts(prop_in, prop_out, features):
    pre_hidden = jnp.dot(prop_in, features, preferred_element_type=jnp.float32)
    hidden_units = jax.nn.relu(pre_hidden).astype(jnp.bfloat16)
    logits = jnp.dot(prop_out, hidden_units, preferred_element_type=jnp.float32)
    return (pre_hidden, hidden_units, logits)

def proposal_grads(prop_in, prop_out, features, sigma_grad):
    pre_hidden, hidden_units, logits = proposal_parts(prop_in, prop_out, features)
    logit_grad = (sigma_grad * jax.nn.sigmoid(logits)).astype(jnp.bfloat16)
    out_grad = jnp.dot(hidden_units, logit_grad, preferred_element_type=jnp.float32)
    spread = prop_out[:, None].astype(jnp.float32) * logit_grad[None, :].astype(jnp.float32)
    hidden_grad = jnp.where(pre_hidden > 0, spread, jnp.float32(0.0)).astype(jnp.bfloat16)
    in_grad = lax.dot_general(hidden_grad, features, (((1,), (1,)), ((), ())), preferred_element_type=jnp.float32)
    return (in_grad, out_grad)

def absorbed(sigma, spacing):
    optical = sigma * spacing
    depth_sum = jnp.cumsum(optical, axis=-2)
    return (jnp.exp(optical - depth_sum) - jnp.exp(-depth_sum), -depth_sum[..., -1, :])

def proposal_terms(sigma, fine_absorbed, spacing):
    prop_absorbed, log_prop = absorbed(sigma, spacing)
    return (lax.optimization_barrier(jnp.sum(prop_absorbed * prop_absorbed, axis=-2)), lax.optimization_barrier(jnp.sum(prop_absorbed * fine_absorbed, axis=-2)), log_prop)

def segment_stats(prop_sigma, fine_sigma, spacing):
    fine_absorbed, log_fine = absorbed(fine_sigma, spacing)
    sum_aa, sum_ab, log_prop = proposal_terms(prop_sigma, fine_absorbed, spacing)
    sum_bb = lax.optimization_barrier(jnp.sum(fine_absorbed * fine_absorbed, axis=-2))
    return (log_prop, log_fine, sum_aa, sum_ab, sum_bb)

def spread_sum(values, ray_table, rank_table, matrix):
    per_ray = lax.dot_general(ray_table, rank_table * values[None, :], (((1,), (1,)), ((), ())), precision=lax.Precision.HIGHEST)
    per_ray = jnp.dot(per_ray, matrix, precision=lax.Precision.HIGHEST)
    spread = lax.dot_general(per_ray, ray_table, (((0,), (0,)), ((), ())), precision=lax.Precision.HIGHEST)
    return lax.optimization_barrier(jnp.sum(spread * rank_table, axis=0))

def ray_side(log_prop, log_fine, sum_aa, sum_ab, sum_bb, ray_ids, rank_ids, counts):
    part_count, capacity = ray_ids.shape
    live_mask = (jnp.arange(capacity)[None, :] < counts[:, None]).astype(jnp.float32).reshape(-1)
    ray_flat = ray_ids.reshape(-1)
    rank_flat = rank_ids.reshape(-1)
    ray_table = (jnp.arange(RAY_DEV)[:, None] == ray_flat[None, :]).astype(jnp.float32)
    rank_table = (jnp.arange(part_count)[:, None] == rank_flat[None, :]).astype(jnp.float32)
    later = (jnp.arange(part_count)[:, None] < jnp.arange(part_count)[None, :]).astype(jnp.float32)
    entry_prop = jnp.exp(spread_sum(log_prop.reshape(-1) * live_mask, ray_table, rank_table, later)) * live_mask
    entry_fine = jnp.exp(spread_sum(log_fine.reshape(-1) * live_mask, ray_table, rank_table, later)) * live_mask
    flat_aa = sum_aa.reshape(-1)
    flat_ab = sum_ab.reshape(-1)
    flat_bb = sum_bb.reshape(-1)
    seg_loss = entry_prop * entry_prop * flat_aa - 2.0 * entry_prop * entry_fine * flat_ab + entry_fine * entry_fine * flat_bb
    slot_grad = distill_weight * (entry_prop * flat_aa - entry_fine * flat_ab) * entry_prop
    carried = spread_sum(slot_grad, ray_table, rank_table, later.T) * live_mask
    ray_loss = 0.5 * distill_weight * jnp.dot(ray_table, seg_loss, precision=lax.Precision.HIGHEST)
    coef_aa = 0.5 * distill_weight * entry_prop * entry_prop
    coef_ab = -distill_weight * entry_prop * entry_fine
    return (jnp.stack([coef_aa, coef_ab, carried]).reshape(3, part_count, capacity), ray_loss)

def reference(feature_grid, fine_in, fine_mid, fine_out, prop_in, prop_out, sample_cells, sample_geometry, slot_ray, slot_rank, bucket_count):
    owner_geometry = jnp.transpose(sample_geometry, (0, 3, 2, 1, 4))
    owners = jnp.arange(N_DOM * N_REP, dtype=jnp.int32)

    def owner_inputs(owner_index):
        part_id = owner_index // N_REP
        replica = owner_index % N_REP
        cell_index = sample_cells[part_id, replica].reshape(-1)
        geometry = owner_geometry[:, part_id, replica].reshape(4, -1)
        features = interpolate(feature_grid[part_id], cell_index, geometry)
        spacing = geometry[3].astype(jnp.float32).reshape(N_DOM, S, CAP)
        return (part_id, features, spacing)

    def owner_forward(owner_index):
        part_id, features, spacing = owner_inputs(owner_index)
        fine_sigma = fine_density(fine_in[part_id], fine_mid[part_id], fine_out[part_id], features)
        prop_sigma = jax.nn.softplus(proposal_parts(prop_in[part_id], prop_out[part_id], features)[2])
        stats = segment_stats(prop_sigma.reshape(N_DOM, S, CAP), fine_sigma.reshape(N_DOM, S, CAP), spacing)
        return (jnp.stack(stats), fine_sigma)
    stats, fine_all = lax.map(owner_forward, owners)
    ray_stats = jnp.transpose(stats.reshape(N_DOM, N_REP, 5, N_DOM, CAP), (3, 1, 2, 0, 4)).reshape(N_DOM * N_REP, 5, N_DOM, CAP)

    def ray_device(packed):
        stat_block, ray_ids, rank_ids, counts = packed
        return ray_side(stat_block[0], stat_block[1], stat_block[2], stat_block[3], stat_block[4], ray_ids, rank_ids, counts)
    factors, losses = lax.map(ray_device, (ray_stats, slot_ray.reshape(-1, N_DOM, CAP), slot_rank.reshape(-1, N_DOM, CAP), bucket_count.reshape(-1, N_DOM)))
    owner_factors = jnp.transpose(factors.reshape(N_DOM, N_REP, 3, N_DOM, CAP), (3, 1, 2, 0, 4)).reshape(N_DOM * N_REP, 3, N_DOM, CAP)

    def owner_backward(packed):
        owner_index, fine_sigma, factor = packed
        part_id, features, spacing = owner_inputs(owner_index)
        prop_sigma = jax.nn.softplus(proposal_parts(prop_in[part_id], prop_out[part_id], features)[2])
        fine_absorbed = absorbed(fine_sigma.reshape(N_DOM, S, CAP), spacing)[0]
        terms_value, pullback = jax.vjp(lambda sigma: proposal_terms(sigma, fine_absorbed, spacing), prop_sigma.reshape(N_DOM, S, CAP))
        sigma_grad = pullback((factor[0], factor[1], factor[2]))[0]
        return proposal_grads(prop_in[part_id], prop_out[part_id], features, sigma_grad.reshape(-1))
    in_grads, out_grads = lax.map(owner_backward, (owners, fine_all, owner_factors))
    return (losses.reshape(N_DOM, N_REP, RAY_DEV), in_grads.reshape(N_DOM, N_REP, PH, F).sum(axis=1), out_grads.reshape(N_DOM, N_REP, PH).sum(axis=1))
```

```python
import functools

import jax
import jax.numpy as jnp
from jax import lax
from jax.experimental import pallas as pl
from jax.experimental.pallas import tpu as pltpu
from jax.sharding import PartitionSpec as P

GR = 32
RAY_DEV = 256
LANES = 128
BLOCK = 256

distill_weight = 50.0
F32 = jnp.float32
BF16 = jnp.bfloat16


def dot(a, b):
    return lax.dot_general(a, b, (((1,), (0,)), ((), ())), preferred_element_type=F32)


def dot_nt(a, b):
    return lax.dot_general(a, b, (((1,), (1,)), ((), ())), preferred_element_type=F32)


def split3(x):
    hi = x.astype(BF16)
    rest = x - hi.astype(F32)
    mid = rest.astype(BF16)
    low = (rest - mid.astype(F32)).astype(BF16)
    return [hi, mid, low]


def gather_kernel(idx_ref, grid_ref, out_ref, table, shifted, near_a, far_a, near_b, far_b):
    step = pl.program_id(0)
    steps = pl.num_programs(0)
    cells = grid_ref.shape[1]
    plane = GR * GR
    width = out_ref.shape[1]
    blocks = width // BLOCK
    rows = lax.broadcasted_iota(jnp.int32, (BLOCK, BLOCK), 0)
    cols = lax.broadcasted_iota(jnp.int32, (BLOCK, BLOCK), 1)
    eye = (rows == cols).astype(BF16)

    def gather(block, near, far):
        row = block // blocks
        start = (block % blocks) * BLOCK
        for u in range(BLOCK):
            k = idx_ref[row, start + u]
            near[u : u + 1, :] = table[pl.ds(k, 1), :]
            far[u : u + 1, :] = table[pl.ds(k + 1, 1), :]

    @pl.when(step == 0)
    def _():
        span = 2048

        def shift(b, carry):
            c0 = pl.multiple_of(b * span, span)
            x = grid_ref[:, pl.ds(c0, span + LANES)]
            shifted[:, pl.ds(c0, span)] = x[:, GR : GR + span]
            return carry

        lax.fori_loop(0, cells // span - 1, shift, 0)
        last = grid_ref[:, cells - span :]
        shifted[:, cells - span :] = jnp.concatenate([last[:, GR:], last[:, :GR]], axis=1)

        def build(b, carry):
            c0 = pl.multiple_of(b * BLOCK, BLOCK)
            x = jnp.concatenate(
                [
                    grid_ref[:, pl.ds(c0, BLOCK)],
                    shifted[:, pl.ds(c0, BLOCK)],
                    grid_ref[:, pl.ds(c0 + plane, BLOCK)],
                    shifted[:, pl.ds(c0 + plane, BLOCK)],
                ],
                axis=0,
            )
            table[pl.ds(c0, BLOCK), :] = dot_nt(eye, x)
            return carry

        lax.fori_loop(0, (cells - plane) // BLOCK, build, 0, unroll=4)
        gather(0, near_a, far_a)

    def turn(j, near, far):
        d = jnp.concatenate([near[...].astype(BF16), far[...].astype(BF16)], axis=1)
        t = dot_nt(eye, d)
        out_ref[:, pl.ds(pl.multiple_of(j * BLOCK, BLOCK), BLOCK)] = t.astype(BF16)

    final = steps * blocks - 1

    def pair(i, carry):
        first = step * blocks + 2 * i
        gather(first + 1, near_b, far_b)
        turn(2 * i, near_a, far_a)
        gather(jnp.minimum(first + 2, final), near_a, far_a)
        turn(2 * i + 1, near_b, far_b)
        return carry

    lax.fori_loop(0, blocks // 2, pair, 0)


def gather_corners(cells, grid):
    parts, width = cells.shape
    features, total = grid.shape
    return pl.pallas_call(
        gather_kernel,
        grid=(parts,),
        out_shape=jax.ShapeDtypeStruct((8 * features, parts * width), BF16),
        in_specs=[
            pl.BlockSpec(memory_space=pltpu.SMEM),
            pl.BlockSpec((features, total), lambda q: (0, 0), pipeline_mode=pl.Buffered(1)),
        ],
        out_specs=pl.BlockSpec((8 * features, width), lambda q: (0, q)),
        scratch_shapes=[
            pltpu.VMEM((total, LANES), F32),
            pltpu.VMEM((features, total), BF16),
        ]
        + [pltpu.VMEM((BLOCK, LANES), F32)] * 4,
        compiler_params=pltpu.CompilerParams(vmem_limit_bytes=40 * 1024 * 1024),
        name="gather_corners",
    )(cells, grid)


def lane_fold(x, cap):
    shift = LANES // 2
    while shift >= cap:
        x = x + pltpu.roll(x, shift, 1)
        shift //= 2
    return x


def running(pieces, cap):
    lane = lax.broadcasted_iota(jnp.int32, pieces[0].shape, 1)
    carry = jnp.zeros_like(pieces[0])
    out = []
    for x in pieces:
        y = x
        shift = cap
        while shift < LANES:
            y = y + jnp.where(lane >= shift, pltpu.roll(y, shift, 1), 0.0)
            shift *= 2
        out.append(carry + y)
        carry = carry + lane_fold(x, cap)
    return out, carry


def trailing(pieces, cap):
    lane = lax.broadcasted_iota(jnp.int32, pieces[0].shape, 1)
    carry = jnp.zeros_like(pieces[0])
    out = []
    for x in reversed(pieces):
        y = x
        shift = cap
        while shift < LANES:
            y = y + jnp.where(lane < LANES - shift, pltpu.roll(y, LANES - shift, 1), 0.0)
            shift *= 2
        out.append(carry + y)
        carry = carry + lane_fold(x, cap)
    return out[::-1]


def softplus(x):
    return jnp.maximum(x, 0.0) + jnp.log1p(jnp.exp(-jnp.abs(x)))


def pieces_of(x):
    return [x[:, v * LANES : (v + 1) * LANES] for v in range(x.shape[1] // LANES)]


def forward_kernel(
    cap, corners_ref, geometry_ref, first_ref, mid_ref, head_ref,
    saved_ref, dense_ref, summary_ref, weights, fine_logit, prop_logit,
):
    step = pl.program_id(0)
    features = corners_ref.shape[0] // 8
    hidden = mid_ref.shape[1]
    width = corners_ref.shape[1]

    @pl.when(step == 0)
    def _():
        g = [geometry_ref[j].astype(F32) for j in range(3)]
        for corner in range(8):
            bits = (corner // 4, corner // 2 % 2, corner % 2)
            w = [x if bit else 1.0 - x for x, bit in zip(g, bits)]
            weights[corner] = w[0] * w[1] * w[2]

    feats = []
    for v in range(width // BLOCK):
        at = v * BLOCK
        total = jnp.zeros((features, BLOCK), F32)
        for corner in range(8):
            place = (corner % 2) * 4 + corner // 2
            x = corners_ref[place * features : (place + 1) * features, at : at + BLOCK].astype(F32)
            total = total + x * weights[corner, pl.ds(step, 1), at : at + BLOCK]
        feats.append(total.astype(BF16))
    feat = jnp.concatenate(feats, axis=1)
    both = jnp.maximum(dot(first_ref[...], feat), 0.0).astype(BF16)
    h = both[:hidden]
    ph = both[hidden:]
    for layer in range(mid_ref.shape[0]):
        h = jnp.maximum(dot(mid_ref[layer], h), 0.0).astype(BF16)
    logits = dot(head_ref[...], jnp.concatenate([h, ph], axis=0))
    fine_logit[pl.ds(step, 1), :] = logits[0:1]
    prop_logit[pl.ds(step, 1), :] = logits[1:2]
    saved_ref[:features, :] = feat
    saved_ref[features:, :] = ph

    @pl.when(step == pl.num_programs(0) - 1)
    def _():
        space = pieces_of(geometry_ref[3].astype(F32))
        results = []
        for k, ref in enumerate((prop_logit, fine_logit)):
            logit = pieces_of(ref[...])
            optical = [softplus(x) * s for x, s in zip(logit, space)]
            depth, whole = running(optical, cap)
            early = [jnp.exp(o - d) for o, d in zip(optical, depth)]
            absorb = [e - jnp.exp(-d) for e, d in zip(early, depth)]
            results.append((absorb, whole))
            if k == 0:
                slope = [s * jax.nn.sigmoid(x) for x, s in zip(logit, space)]
                dense_ref[0] = jnp.concatenate(early, axis=1)
                dense_ref[3] = jnp.concatenate(slope, axis=1)
        (a, log_prop), (b, log_fine) = results
        dense_ref[1] = jnp.concatenate(a, axis=1)
        dense_ref[2] = jnp.concatenate(b, axis=1)
        sums = [lane_fold(sum(x * y for x, y in zip(s, t)), cap) for s, t in ((a, a), (a, b), (b, b))]
        stats = [-log_prop, -log_fine] + sums
        per = LANES // cap
        group = lax.broadcasted_iota(jnp.int32, stats[0].shape, 1) // cap
        slabs = []
        for s in range(-(-len(stats) // per)):
            slab = jnp.zeros_like(stats[0])
            for k, x in enumerate(stats[s * per : (s + 1) * per]):
                slab = jnp.where(group == k, x, slab)
            slabs.append(slab)
        summary_ref[...] = jnp.concatenate(slabs, axis=1)


def forward(corners, geometry, first, mid, head, cap):
    rows, total = corners.shape
    parts, width = geometry.shape[1:]
    features = rows // 8
    prop_hidden = first.shape[0] - mid.shape[1]
    kept = features + prop_hidden
    stat_lanes = -(-5 // (LANES // cap)) * LANES
    whole = lambda shape: pl.BlockSpec(shape, lambda q: (0,) * len(shape))
    return pl.pallas_call(
        functools.partial(forward_kernel, cap),
        grid=(parts,),
        out_shape=(
            jax.ShapeDtypeStruct((kept, total), BF16),
            jax.ShapeDtypeStruct((4, parts, width), F32),
            jax.ShapeDtypeStruct((parts, stat_lanes), F32),
        ),
        in_specs=[
            pl.BlockSpec((rows, width), lambda q: (0, q)),
            whole(geometry.shape),
            whole(first.shape),
            whole(mid.shape),
            whole(head.shape),
        ],
        out_specs=(
            pl.BlockSpec((kept, width), lambda q: (0, q)),
            whole((4, parts, width)),
            whole((parts, stat_lanes)),
        ),
        scratch_shapes=[
            pltpu.VMEM((8, parts, width), F32),
            pltpu.VMEM((parts, width), F32),
            pltpu.VMEM((parts, width), F32),
        ],
        compiler_params=pltpu.CompilerParams(vmem_limit_bytes=32 * 1024 * 1024),
        name="forward",
    )(corners, geometry, first, mid, head)


def backward_kernel(
    cap, me_ref, stats_ref, key_ref, dense_ref, saved_ref, out_col_ref,
    loss_ref, grad_ref, keys_t, slope_ref, *masks,
):
    me = me_ref[0]
    parts = stats_ref.shape[0]
    slots = key_ref.shape[1]
    per = LANES // cap
    width = dense_ref.shape[2]
    prop_hidden = out_col_ref.shape[0]
    key = key_ref[...]
    live = (key >= 0).astype(F32)
    sub = lax.broadcasted_iota(jnp.int32, (parts, slots), 0)
    keys_t[...] = key.T

    def mask_of(q):
        if isinstance(q, int):
            col = keys_t[:, q : q + 1]
            row = key[q : q + 1]
        else:
            lane = lax.broadcasted_iota(jnp.int32, (slots, parts), 1)
            col = jnp.sum(jnp.where(lane == q, keys_t[...], 0.0), axis=1, keepdims=True)
            row = jnp.sum(jnp.where(sub == q, key, 0.0), axis=0, keepdims=True)
        gap = row - col
        return ((gap > 0) & (gap < parts)).astype(BF16)

    if masks:
        for q in range(parts):
            masks[0][q] = mask_of(q)

    def over(body, init):
        if masks:
            for q in range(parts):
                init = body(q, init)
            return init
        return lax.fori_loop(0, parts, body, init)

    group = lax.broadcasted_iota(jnp.int32, (parts, LANES), 1) // cap

    def flat(j):
        slab = slice((j // per) * LANES, (j // per + 1) * LANES)
        out = []
        for half in range(slots // LANES):
            x = jnp.zeros((parts, LANES), F32)
            for k in range(per):
                piece = stats_ref[half * per + k, :, slab]
                shift = ((k - j % per) * cap) % LANES
                x = jnp.where(group == k, pltpu.roll(piece, shift, 1) if shift else piece, x)
            out.append(x)
        return jnp.concatenate(out, axis=1)

    log_prop, log_fine, sum_aa, sum_ab, sum_bb = [flat(j) for j in range(5)]
    terms = split3(log_prop * live) + split3(log_fine * live)
    stacked = jnp.concatenate(terms, axis=0)

    def lead(q, acc):
        m = masks[0][q] if masks else mask_of(q)
        y = dot(stacked, m)
        return tuple(
            jnp.where(sub == q, y[k * parts : (k + 1) * parts], x) for k, x in enumerate(acc)
        )

    zero = jnp.zeros((parts, slots), F32)
    lead_sums = over(lead, (zero,) * 6)
    entry_prop = jnp.exp(lead_sums[0] + lead_sums[1] + lead_sums[2]) * live
    entry_fine = jnp.exp(lead_sums[3] + lead_sums[4] + lead_sums[5]) * live
    seg_loss = (
        entry_prop * entry_prop * sum_aa
        - 2.0 * entry_prop * entry_fine * sum_ab
        + entry_fine * entry_fine * sum_bb
    )
    slot_grad = distill_weight * (entry_prop * sum_aa - entry_fine * sum_ab) * entry_prop
    mine = pl.ds(pl.multiple_of(me * cap, cap), cap)
    grads = jnp.concatenate(split3(slot_grad), axis=0)
    sub_cap = lax.broadcasted_iota(jnp.int32, (parts, cap), 0)

    def tail(q, acc):
        if masks:
            m = masks[0][q, mine, :]
            y = dot_nt(grads, m)
        else:
            y = dot_nt(grads, mask_of(q))
            y = own_lanes(y)
        y = y[:parts] + y[parts : 2 * parts] + y[2 * parts :]
        return jnp.where(sub_cap == q, y, acc)

    def own_lanes(x):
        out = x[:, :cap]
        for p in range(1, parts):
            out = jnp.where(me == p, x[:, p * cap : (p + 1) * cap], out)
        return out

    carried = over(tail, jnp.zeros((parts, cap), F32)) * own_lanes(live)
    coef_aa = own_lanes(0.5 * distill_weight * entry_prop * entry_prop)
    coef_ab = own_lanes(-distill_weight * entry_prop * entry_fine)

    lane_me = lax.broadcasted_iota(jnp.int32, (slots, parts), 1)
    key_col = jnp.sum(jnp.where(lane_me == me, keys_t[...], 0.0), axis=1, keepdims=True)
    ray = lax.broadcasted_iota(jnp.int32, (slots, RAY_DEV), 1).astype(F32)
    rest = key_col - ray * (2.0 * parts)
    hot = ((rest >= 0) & (rest < 2 * parts)).astype(BF16)
    spread = dot(jnp.concatenate(split3(seg_loss), axis=0), hot)
    spread = spread[:parts] + spread[parts : 2 * parts] + spread[2 * parts :]
    sub_ray = lax.broadcasted_iota(jnp.int32, (parts, RAY_DEV), 0)
    loss_ref[...] = (0.5 * distill_weight) * jnp.sum(
        jnp.where(sub_ray == me, spread, 0.0), axis=0, keepdims=True
    )

    tile = lambda x: jnp.concatenate([x] * per, axis=1)
    c_aa, c_ab, c_log = tile(2.0 * coef_aa), tile(coef_ab), tile(carried)
    early, a, b, slope = [pieces_of(dense_ref[k]) for k in range(4)]
    d_absorb = [c_aa * x + c_ab * y for x, y in zip(a, b)]
    back = trailing([d * x for d, x in zip(d_absorb, a)], cap)
    logit_grad = [
        ((d * e - c_log - r) * s).astype(BF16).astype(F32)
        for d, e, r, s in zip(d_absorb, early, back, slope)
    ]
    slope_ref[...] = jnp.concatenate(logit_grad, axis=1)
    features = saved_ref.shape[0] - prop_hidden
    out_col = out_col_ref[...].astype(F32)
    first_row = lax.broadcasted_iota(jnp.int32, (prop_hidden, width), 0) == 0

    def accumulate(q, total):
        at = pl.ds(pl.multiple_of(q * width, width), width)
        row = slope_ref[pl.ds(q, 1), :]
        kept = saved_ref[:, at]
        hidden_grad = jnp.where(kept[features:].astype(F32) > 0, out_col * row, 0.0).astype(BF16)
        alone = jnp.where(first_row, row, 0.0).astype(BF16)
        return total + dot_nt(jnp.concatenate([hidden_grad, alone], axis=0), kept)

    total = jnp.zeros((2 * prop_hidden, saved_ref.shape[0]), F32)
    total = lax.fori_loop(0, parts, accumulate, total)
    grad_ref[...] = total


def backward(me, stats, key, dense, saved, out_col, cap):
    parts, slots = key.shape
    width = dense.shape[2]
    prop_hidden = out_col.shape[0]
    vmem = pl.BlockSpec(memory_space=pltpu.VMEM)
    keep = [pltpu.VMEM((parts, slots, slots), BF16)] if slots <= 256 else []
    return pl.pallas_call(
        functools.partial(backward_kernel, cap),
        out_shape=(
            jax.ShapeDtypeStruct((1, RAY_DEV), F32),
            jax.ShapeDtypeStruct((2 * prop_hidden, saved.shape[0]), F32),
        ),
        in_specs=[pl.BlockSpec(memory_space=pltpu.SMEM)] + [vmem] * 5,
        out_specs=(vmem, vmem),
        scratch_shapes=[pltpu.VMEM((slots, parts), F32), pltpu.VMEM((parts, width), F32)] + keep,
        compiler_params=pltpu.CompilerParams(vmem_limit_bytes=48 * 1024 * 1024),
        name="backward",
    )(me, stats, key, dense, saved, out_col)


def sum_replicas(x):
    count = lax.axis_size("rep")
    if count != 4:
        return lax.psum(x, "rep")
    other = [lax.ppermute(x, "rep", [(i, i ^ s) for i in range(count)]) for s in (1, 2, 3)]
    return (x + other[0]) + (other[1] + other[2])


def on_device(
    feature_grid,
    fine_in,
    fine_mid,
    fine_out,
    prop_in,
    prop_out,
    sample_cells,
    sample_geometry,
    slot_ray,
    slot_rank,
    bucket_count,
):
    parts = lax.axis_size("dom")
    cap = slot_ray.shape[3]
    width = sample_cells.shape[3]
    features = feature_grid.shape[1]
    prop_hidden = prop_in.shape[1]
    slots = parts * cap

    live = jnp.arange(cap)[None, :] < bucket_count[0, 0][:, None]
    ray = jnp.where(live, slot_ray[0, 0], -1).reshape(-1)
    marks = jnp.concatenate([ray, slot_rank[0, 0].reshape(-1)]).astype(BF16)
    extra = -(-2 * slots // width)
    marks = jnp.pad(marks, (0, extra * width - 2 * slots)).reshape(extra, 1, width)
    outgoing = jnp.concatenate(
        [sample_geometry[:, 0, 0], jnp.broadcast_to(marks, (extra, parts, width))], axis=0
    )
    arrived = lax.all_to_all(outgoing, "dom", split_axis=1, concat_axis=1, tiled=True)

    corners = gather_corners(sample_cells[0, 0], feature_grid[0])

    geometry = arrived[:4]
    marks = jnp.moveaxis(arrived[4:], 0, 1).reshape(parts, extra * width)[:, : 2 * slots].astype(F32)
    key = marks[:, :slots] * (2.0 * parts) + marks[:, slots:]
    first = jnp.concatenate([fine_in[0], prop_in[0]], axis=0)
    head = jnp.concatenate(
        [
            jnp.pad(fine_out, ((0, 0), (0, prop_hidden))),
            jnp.pad(prop_out, ((0, 0), (fine_out.shape[1], 0))),
        ],
        axis=0,
    )
    head = jnp.pad(head, ((0, 6), (0, 0)))
    saved, dense, summary = forward(corners, geometry, first, fine_mid[0], head, cap)

    stats = lax.all_to_all(
        jnp.broadcast_to(summary[None], (parts,) + summary.shape),
        "dom", split_axis=0, concat_axis=0, tiled=True,
    )
    me = lax.axis_index("dom").reshape(1).astype(jnp.int32)
    ray_loss, grads = backward(me, stats, key, dense, saved, prop_out.reshape(-1, 1), cap)
    sums = sum_replicas(grads)
    in_sum = sums[:prop_hidden, :features]
    out_sum = sums[prop_hidden, features:]
    return (ray_loss.reshape(1, 1, -1), in_sum[None], out_sum[None])


def solution(mesh):
    return jax.shard_map(
        on_device,
        mesh=mesh,
        in_specs=(
            P("dom", None, None),
            P("dom", None, None),
            P("dom", None, None, None),
            P("dom", None),
            P("dom", None, None),
            P("dom", None),
            P("dom", "rep", None, None),
            P(None, "dom", "rep", None, None),
            P("dom", "rep", None, None),
            P("dom", "rep", None, None),
            P("dom", "rep", None),
        ),
        out_specs=(P("dom", "rep", None), P("dom", None, None), P("dom", None)),
        check_vma=False,
    )
```

```python
import functools

import jax
import jax.numpy as jnp
from jax import lax
from jax.experimental import pallas as pl
from jax.experimental.pallas import tpu as pltpu
from jax.sharding import PartitionSpec as P

GR = 32
RAY_DEV = 256
LANES = 128
BLOCK = 256
BUILD_UNROLL = 31
DEPTH = 4

distill_weight = 50.0
F32 = jnp.float32
BF16 = jnp.bfloat16


def dot(a, b):
    return lax.dot_general(a, b, (((1,), (0,)), ((), ())), preferred_element_type=F32)


def dot_nt(a, b):
    return lax.dot_general(a, b, (((1,), (1,)), ((), ())), preferred_element_type=F32)


def split3(x):
    hi = x.astype(BF16)
    rest = x - hi.astype(F32)
    mid = rest.astype(BF16)
    low = (rest - mid.astype(F32)).astype(BF16)
    return [hi, mid, low]


def stack_rows(arrays, row):
    return jnp.concatenate([x[row : row + 1] for x in arrays], axis=0)


def flatten_slots(x, cap):
    parts = x.shape[0]
    per = LANES // cap
    lane = lax.broadcasted_iota(jnp.int32, (1, LANES), 1)
    wide = jnp.concatenate([x] * per, axis=1)
    out = []
    for first in range(0, parts, per):
        row = wide[first : first + 1]
        for k in range(1, per):
            row = jnp.where(lane // cap == k, wide[first + k : first + k + 1], row)
        out.append(row)
    return jnp.concatenate(out, axis=1)


def pack_kernel(geometry_ref, ray_ref, rank_ref, count_ref, out_ref):
    parts, cap = ray_ref.shape
    width = geometry_ref.shape[2]
    extra = out_ref.shape[1] - 4
    live = lax.broadcasted_iota(jnp.int32, (parts, cap), 1) < count_ref[...]
    ray = jnp.where(live, ray_ref[...], -1).astype(F32)
    marks = jnp.concatenate(
        [flatten_slots(ray, cap), flatten_slots(rank_ref[...].astype(F32), cap)], axis=1
    )
    spare = extra * width - marks.shape[1]
    if spare:
        marks = jnp.concatenate([marks, jnp.zeros((1, spare), F32)], axis=1)
    marks = [marks[:, e * width : (e + 1) * width] for e in range(extra)]
    g = [geometry_ref[j].astype(F32) for j in range(4)]
    for p in range(parts):
        block = [x[p : p + 1] for x in g] + marks
        out_ref[p] = jnp.concatenate(block, axis=0).astype(BF16)


def pack(geometry, ray, rank, count):
    parts, width = geometry.shape[1:]
    extra = -(-2 * ray.size // width)
    vmem = pl.BlockSpec(memory_space=pltpu.VMEM)
    return pl.pallas_call(
        pack_kernel,
        out_shape=jax.ShapeDtypeStruct((parts, 4 + extra, width), BF16),
        in_specs=[vmem] * 4,
        out_specs=vmem,
        name="pack",
    )(geometry, ray, rank, count)


def marks_kernel(cap, me_ref, arrived_ref, key_ref, hot_ref, *mask_ref):
    me = me_ref[0]
    parts = arrived_ref.shape[0]
    slots = parts * cap
    width = arrived_ref.shape[2]
    extra = arrived_ref.shape[1] - 4
    ray, rank = [], []
    for q in range(parts):
        marks = [arrived_ref[q].astype(F32)[4 + e : 5 + e] for e in range(extra)]
        marks = marks[0] if extra == 1 else jnp.concatenate(marks, axis=1)
        ray.append(marks[:, :slots])
        rank.append(marks[:, slots : 2 * slots])
    key = jnp.concatenate(ray, axis=0) * (2.0 * parts) + jnp.concatenate(rank, axis=0)
    key_ref[...] = key
    key_t = key.T
    mine = lax.broadcasted_iota(jnp.int32, (slots, parts), 1) == me
    key_col = jnp.sum(jnp.where(mine, key_t, 0.0), axis=1, keepdims=True)
    ray = lax.broadcasted_iota(jnp.int32, (slots, RAY_DEV), 1).astype(F32)
    rest = key_col - ray * (2.0 * parts)
    hot_ref[...] = ((rest >= 0) & (rest < 2 * parts)).astype(BF16)
    if mask_ref:
        for q in range(parts):
            gap = key[q : q + 1] - key_t[:, q : q + 1]
            mask_ref[0][q] = ((gap > 0) & (gap < parts)).astype(BF16)


def slot_marks(me, arrived, cap):
    parts = arrived.shape[0]
    slots = parts * cap
    vmem = pl.BlockSpec(memory_space=pltpu.VMEM)
    shapes = [
        jax.ShapeDtypeStruct((parts, slots), F32),
        jax.ShapeDtypeStruct((slots, RAY_DEV), BF16),
    ]
    if slots <= 256:
        shapes.append(jax.ShapeDtypeStruct((parts, slots, slots), BF16))
    return pl.pallas_call(
        functools.partial(marks_kernel, cap),
        out_shape=tuple(shapes),
        in_specs=[pl.BlockSpec(memory_space=pltpu.SMEM), vmem],
        out_specs=(vmem,) * len(shapes),
        cost_estimate=pl.CostEstimate(
            flops=parts * slots * slots * 8, bytes_accessed=4 << 20, transcendentals=0
        ),
        name="slot_marks",
    )(me, arrived)


def gather_kernel(idx_ref, grid_ref, out_ref, table, shifted, rows, eye):
    step = pl.program_id(0)
    steps = pl.num_programs(0)
    cells = grid_ref.shape[1]
    plane = GR * GR
    width = out_ref.shape[0] * LANES
    blocks = width // BLOCK

    def unit():
        return jnp.concatenate([eye[0], eye[1]], axis=1)

    def gather(row, block, pair):
        start = row * width
        for u in range(BLOCK):
            k = idx_ref.at[pl.ds(block * BLOCK + u, idx_ref.shape[0] - width + 1)][start]
            pair[2 * u : 2 * u + 2, :] = table[pl.ds(k, 2), :]

    @pl.when(step == 0)
    def _():
        down = lax.broadcasted_iota(jnp.int32, (BLOCK, BLOCK), 0)
        across = lax.broadcasted_iota(jnp.int32, (BLOCK, BLOCK), 1)
        same = (down == across).astype(BF16)
        eye[0] = same[:, :LANES]
        eye[1] = same[:, LANES:]
        span = 2048

        def shift(b, carry):
            c0 = pl.multiple_of(b * span, span)
            x = grid_ref[:, pl.ds(c0, span + LANES)]
            shifted[:, pl.ds(c0, span)] = x[:, GR : GR + span]
            return carry

        lax.fori_loop(0, cells // span - 1, shift, 0)
        last = grid_ref[:, cells - span :]
        shifted[:, cells - span :] = jnp.concatenate([last[:, GR:], last[:, :GR]], axis=1)

        def build(b, carry):
            c0 = pl.multiple_of(b * 2 * BLOCK, 2 * BLOCK)
            x = jnp.concatenate(
                [
                    ref[:, pl.ds(c0 + half * BLOCK + across, BLOCK)]
                    for half in range(2)
                    for across in (0, plane)
                    for ref in (grid_ref, shifted)
                ],
                axis=0,
            )
            table[pl.ds(c0, BLOCK), :] = x[:LANES].T.astype(F32)
            table[pl.ds(c0 + BLOCK, BLOCK), :] = x[LANES:].T.astype(F32)
            return carry

        lax.fori_loop(0, (cells - plane) // (2 * BLOCK), build, 0, unroll=BUILD_UNROLL)
        gather(0, 0, rows.at[0])

    def turn(j, pair):
        near = pair[pl.ds(0, BLOCK, stride=2), :].astype(BF16)
        far = pair[pl.ds(1, BLOCK, stride=2), :].astype(BF16)
        t = dot_nt(unit(), jnp.concatenate([near, far], axis=1)).astype(BF16)
        out_ref[2 * j] = t[:, :LANES]
        out_ref[2 * j + 1] = t[:, LANES:]

    for j in range(blocks):
        ahead = rows.at[(j + 1) % DEPTH]
        if j + 1 < blocks:
            gather(step, j + 1, ahead)
        else:
            gather(jnp.minimum(step + 1, steps - 1), 0, ahead)
        turn(j, rows.at[j % DEPTH])


def gather_corners(cells, grid, parts):
    width = cells.shape[0] // parts
    features, total = grid.shape
    return pl.pallas_call(
        gather_kernel,
        grid=(parts,),
        out_shape=jax.ShapeDtypeStruct((parts * width // LANES, 8 * features, LANES), BF16),
        in_specs=[
            pl.BlockSpec(memory_space=pltpu.SMEM),
            pl.BlockSpec((features, total), lambda q: (0, 0), pipeline_mode=pl.Buffered(1)),
        ],
        out_specs=pl.BlockSpec((width // LANES, 8 * features, LANES), lambda q: (q, 0, 0)),
        scratch_shapes=[
            pltpu.VMEM((total, LANES), F32),
            pltpu.VMEM((features, total), BF16),
        ]
        + [pltpu.VMEM((DEPTH, 2 * BLOCK, LANES), F32)]
        + [pltpu.VMEM((2, BLOCK, LANES), BF16)],
        compiler_params=pltpu.CompilerParams(vmem_limit_bytes=60 * 1024 * 1024),
        name="gather_corners",
    )(cells, grid)


def lane_fold(x, cap):
    shift = LANES // 2
    while shift >= cap:
        x = x + pltpu.roll(x, shift, 1)
        shift //= 2
    return x


def running(pieces, cap):
    lane = lax.broadcasted_iota(jnp.int32, pieces[0].shape, 1)
    carry = jnp.zeros_like(pieces[0])
    out = []
    for x in pieces:
        y = x
        shift = cap
        while shift < LANES:
            y = y + jnp.where(lane >= shift, pltpu.roll(y, shift, 1), 0.0)
            shift *= 2
        out.append(carry + y)
        carry = carry + lane_fold(x, cap)
    return out, carry


def trailing(pieces, cap):
    lane = lax.broadcasted_iota(jnp.int32, pieces[0].shape, 1)
    carry = jnp.zeros_like(pieces[0])
    out = []
    for x in reversed(pieces):
        y = x
        shift = cap
        while shift < LANES:
            y = y + jnp.where(lane < LANES - shift, pltpu.roll(y, LANES - shift, 1), 0.0)
            shift *= 2
        out.append(carry + y)
        carry = carry + lane_fold(x, cap)
    return out[::-1]


def softplus(x):
    return jnp.maximum(x, 0.0) + jnp.log1p(jnp.exp(-jnp.abs(x)))


def pieces_of(x):
    return [x[:, v * LANES : (v + 1) * LANES] for v in range(x.shape[1] // LANES)]


def forward_kernel(
    cap, corners_ref, arrived_ref, fine_in_ref, prop_in_ref, mid_ref, fine_out_ref, prop_out_ref,
    saved_ref, dense_ref, summary_ref, weights, spacing, first, head, fine_logit, prop_logit,
):
    step = pl.program_id(0)
    features = corners_ref.shape[1] // 8
    hidden = mid_ref.shape[1]
    prop_hidden = prop_in_ref.shape[0]
    width = corners_ref.shape[0] * LANES

    @pl.when(step == 0)
    def _():
        parts = arrived_ref.shape[0]
        blocks = [arrived_ref[q].astype(F32) for q in range(parts)]
        g = [stack_rows(blocks, j) for j in range(4)]
        spacing[...] = g[3]
        first[:hidden, :] = fine_in_ref[...].astype(F32).T.astype(BF16)
        first[hidden:, :] = prop_in_ref[...]
        zero_f = jnp.zeros((1, prop_hidden), F32)
        zero_p = jnp.zeros((1, hidden), F32)
        top = jnp.concatenate([fine_out_ref[...].astype(F32), zero_f], axis=1)
        low = jnp.concatenate([zero_p, prop_out_ref[...].astype(F32)], axis=1)
        rest = jnp.zeros((6, hidden + prop_hidden), F32)
        head[...] = jnp.concatenate([top, low, rest], axis=0).astype(BF16)
        for corner in range(8):
            bits = (corner // 4, corner // 2 % 2, corner % 2)
            w = [x if bit else 1.0 - x for x, bit in zip(g, bits)]
            weights[corner] = w[0] * w[1] * w[2]

    feats = []
    row = [weights[corner, pl.ds(step, 1), :] for corner in range(8)]
    for v in range(width // LANES):
        at = v * LANES
        total = jnp.zeros((features, LANES), F32)
        for corner in range(8):
            place = (corner % 2) * 4 + corner // 2
            x = corners_ref[v, place * features : (place + 1) * features, :].astype(F32)
            total = total + x * row[corner][:, at : at + LANES]
        feats.append(total.astype(BF16))
    feat = jnp.concatenate(feats, axis=1)
    both = jnp.maximum(dot(first[...], feat), 0.0).astype(BF16)
    h = both[:hidden]
    ph = both[hidden:]
    for layer in range(mid_ref.shape[0]):
        h = jnp.maximum(dot(mid_ref[layer], h), 0.0).astype(BF16)
    logits = dot(head[...], jnp.concatenate([h, ph], axis=0))
    fine_logit[pl.ds(step, 1), :] = logits[0:1]
    prop_logit[pl.ds(step, 1), :] = logits[1:2]
    saved_ref[:features, :] = feat
    saved_ref[features:, :] = ph

    @pl.when(step == pl.num_programs(0) - 1)
    def _():
        space = pieces_of(spacing[...])
        results = []
        for k, ref in enumerate((prop_logit, fine_logit)):
            logit = pieces_of(ref[...])
            optical = [softplus(x) * s for x, s in zip(logit, space)]
            depth, whole = running(optical, cap)
            early = [jnp.exp(o - d) for o, d in zip(optical, depth)]
            absorb = [e - jnp.exp(-d) for e, d in zip(early, depth)]
            results.append((absorb, whole))
            if k == 0:
                slope = [s * jax.nn.sigmoid(x) for x, s in zip(logit, space)]
                dense_ref[0] = jnp.concatenate(early, axis=1)
                dense_ref[3] = jnp.concatenate(slope, axis=1)
        (a, log_prop), (b, log_fine) = results
        dense_ref[1] = jnp.concatenate(a, axis=1)
        dense_ref[2] = jnp.concatenate(b, axis=1)
        sums = [lane_fold(sum(x * y for x, y in zip(s, t)), cap) for s, t in ((a, a), (a, b), (b, b))]
        stats = [-log_prop, -log_fine] + sums
        per = LANES // cap
        group = lax.broadcasted_iota(jnp.int32, stats[0].shape, 1) // cap
        slabs = []
        for s in range(-(-len(stats) // per)):
            slab = jnp.zeros_like(stats[0])
            for k, x in enumerate(stats[s * per : (s + 1) * per]):
                slab = jnp.where(group == k, x, slab)
            slabs.append(slab)
        summary_ref[...] = jnp.concatenate(slabs, axis=1)


def forward(corners, arrived, fine_in, prop_in, mid, fine_out, prop_out, cap):
    rows = corners.shape[1]
    total = corners.shape[0] * LANES
    parts, _, width = arrived.shape
    features = rows // 8
    hidden = mid.shape[1]
    prop_hidden = prop_in.shape[0]
    kept = features + prop_hidden
    stat_lanes = -(-5 // (LANES // cap)) * LANES
    whole = lambda shape: pl.BlockSpec(shape, lambda q: (0,) * len(shape))
    small = (arrived, fine_in, prop_in, mid, fine_out, prop_out)
    return pl.pallas_call(
        functools.partial(forward_kernel, cap),
        grid=(parts,),
        out_shape=(
            jax.ShapeDtypeStruct((kept, total), BF16),
            jax.ShapeDtypeStruct((4, parts, width), F32),
            jax.ShapeDtypeStruct((parts, stat_lanes), F32),
        ),
        in_specs=[pl.BlockSpec((width // LANES, rows, LANES), lambda q: (q, 0, 0))]
        + [whole(x.shape) for x in small],
        out_specs=(
            pl.BlockSpec((kept, width), lambda q: (0, q)),
            whole((4, parts, width)),
            whole((parts, stat_lanes)),
        ),
        scratch_shapes=[
            pltpu.VMEM((8, parts, width), F32),
            pltpu.VMEM((parts, width), F32),
            pltpu.VMEM((hidden + prop_hidden, features), BF16),
            pltpu.VMEM((8, hidden + prop_hidden), BF16),
            pltpu.VMEM((parts, width), F32),
            pltpu.VMEM((parts, width), F32),
        ],
        compiler_params=pltpu.CompilerParams(vmem_limit_bytes=60 * 1024 * 1024),
        name="forward",
    )(corners, *small)


def backward_kernel(
    cap, me_ref, stats_ref, key_ref, hot_ref, dense_ref, saved_ref, prop_out_ref, *rest,
):
    masks, (loss_ref, grad_ref, slope_ref, *keys_t) = rest[:-3], rest[-3:]
    if stats_ref.shape[0] * cap > 256:
        masks, (loss_ref, grad_ref, slope_ref, *keys_t) = (), rest
    me = me_ref[0]
    parts = stats_ref.shape[0]
    slots = key_ref.shape[1]
    per = LANES // cap
    width = dense_ref.shape[2]
    prop_hidden = prop_out_ref.shape[1]
    key = key_ref[...]
    live = (key >= 0).astype(F32)
    sub = lax.broadcasted_iota(jnp.int32, (parts, slots), 0)
    if not masks:
        keys_t[0][...] = key.T

    def mask_of(q):
        lane = lax.broadcasted_iota(jnp.int32, (slots, parts), 1)
        col = jnp.sum(jnp.where(lane == q, keys_t[0][...], 0.0), axis=1, keepdims=True)
        row = jnp.sum(jnp.where(sub == q, key, 0.0), axis=0, keepdims=True)
        gap = row - col
        return ((gap > 0) & (gap < parts)).astype(BF16)

    def over(body, init):
        if masks:
            for q in range(parts):
                init = body(q, init)
            return init
        return lax.fori_loop(0, parts, body, init)

    group = lax.broadcasted_iota(jnp.int32, (parts, LANES), 1) // cap

    def flat(j):
        slab = slice((j // per) * LANES, (j // per + 1) * LANES)
        out = []
        for half in range(slots // LANES):
            x = jnp.zeros((parts, LANES), F32)
            for k in range(per):
                piece = stats_ref[half * per + k, :, slab]
                shift = ((k - j % per) * cap) % LANES
                x = jnp.where(group == k, pltpu.roll(piece, shift, 1) if shift else piece, x)
            out.append(x)
        return jnp.concatenate(out, axis=1)

    log_prop, log_fine, sum_aa, sum_ab, sum_bb = [flat(j) for j in range(5)]
    terms = split3(log_prop * live) + split3(log_fine * live)
    stacked = jnp.concatenate(terms, axis=0)

    def lead(q, acc):
        m = masks[0][q] if masks else mask_of(q)
        y = dot(stacked, m)
        return tuple(
            jnp.where(sub == q, y[k * parts : (k + 1) * parts], x) for k, x in enumerate(acc)
        )

    zero = jnp.zeros((parts, slots), F32)
    lead_sums = over(lead, (zero,) * 6)
    entry_prop = jnp.exp(lead_sums[0] + lead_sums[1] + lead_sums[2]) * live
    entry_fine = jnp.exp(lead_sums[3] + lead_sums[4] + lead_sums[5]) * live
    seg_loss = (
        entry_prop * entry_prop * sum_aa
        - 2.0 * entry_prop * entry_fine * sum_ab
        + entry_fine * entry_fine * sum_bb
    )
    slot_grad = distill_weight * (entry_prop * sum_aa - entry_fine * sum_ab) * entry_prop
    mine = pl.ds(pl.multiple_of(me * cap, cap), cap)
    grads = jnp.concatenate(split3(slot_grad), axis=0)
    sub_cap = lax.broadcasted_iota(jnp.int32, (parts, cap), 0)

    def tail(q, acc):
        if masks:
            m = masks[0][q, mine, :]
            y = dot_nt(grads, m)
        else:
            y = dot_nt(grads, mask_of(q))
            y = own_lanes(y)
        y = y[:parts] + y[parts : 2 * parts] + y[2 * parts :]
        return jnp.where(sub_cap == q, y, acc)

    def own_lanes(x):
        out = x[:, :cap]
        for p in range(1, parts):
            out = jnp.where(me == p, x[:, p * cap : (p + 1) * cap], out)
        return out

    carried = over(tail, jnp.zeros((parts, cap), F32)) * own_lanes(live)
    coef_aa = own_lanes(0.5 * distill_weight * entry_prop * entry_prop)
    coef_ab = own_lanes(-distill_weight * entry_prop * entry_fine)

    spread = dot(jnp.concatenate(split3(seg_loss), axis=0), hot_ref[...])
    spread = spread[:parts] + spread[parts : 2 * parts] + spread[2 * parts :]
    sub_ray = lax.broadcasted_iota(jnp.int32, (parts, RAY_DEV), 0)
    loss_ref[...] = (0.5 * distill_weight) * jnp.sum(
        jnp.where(sub_ray == me, spread, 0.0), axis=0, keepdims=True
    )

    tile = lambda x: jnp.concatenate([x] * per, axis=1)
    c_aa, c_ab, c_log = tile(2.0 * coef_aa), tile(coef_ab), tile(carried)
    early, a, b, slope = [pieces_of(dense_ref[k]) for k in range(4)]
    d_absorb = [c_aa * x + c_ab * y for x, y in zip(a, b)]
    back = trailing([d * x for d, x in zip(d_absorb, a)], cap)
    logit_grad = [
        ((d * e - c_log - r) * s).astype(BF16).astype(F32)
        for d, e, r, s in zip(d_absorb, early, back, slope)
    ]
    slope_ref[...] = jnp.concatenate(logit_grad, axis=1)
    features = saved_ref.shape[0] - prop_hidden
    wide = jnp.broadcast_to(prop_out_ref[...].astype(F32), (prop_hidden, prop_hidden))
    same = lax.broadcasted_iota(jnp.int32, wide.shape, 0) == lax.broadcasted_iota(
        jnp.int32, wide.shape, 1
    )
    out_col = jnp.sum(jnp.where(same, wide, 0.0), axis=1, keepdims=True)
    first_row = lax.broadcasted_iota(jnp.int32, (prop_hidden, width), 0) == 0

    def accumulate(q, total):
        at = pl.ds(pl.multiple_of(q * width, width), width)
        row = slope_ref[pl.ds(q, 1), :]
        kept = saved_ref[:, at]
        hidden_grad = jnp.where(kept[features:].astype(F32) > 0, out_col * row, 0.0).astype(BF16)
        alone = jnp.where(first_row, row, 0.0).astype(BF16)
        return total + dot_nt(jnp.concatenate([hidden_grad, alone], axis=0), kept)

    total = jnp.zeros((2 * prop_hidden, saved_ref.shape[0]), F32)
    total = lax.fori_loop(0, parts, accumulate, total)
    grad_ref[...] = total


def backward(me, stats, dense, saved, prop_out, marks, cap):
    key, hot, *masks = marks
    parts, slots = key.shape
    width = dense.shape[2]
    prop_hidden = prop_out.shape[1]
    vmem = pl.BlockSpec(memory_space=pltpu.VMEM)
    return pl.pallas_call(
        functools.partial(backward_kernel, cap),
        out_shape=(
            jax.ShapeDtypeStruct((1, RAY_DEV), F32),
            jax.ShapeDtypeStruct((2 * prop_hidden, saved.shape[0]), F32),
        ),
        in_specs=[pl.BlockSpec(memory_space=pltpu.SMEM)] + [vmem] * (6 + len(masks)),
        out_specs=(vmem, vmem),
        scratch_shapes=[pltpu.VMEM((parts, width), F32)]
        + ([] if masks else [pltpu.VMEM((slots, parts), F32)]),
        compiler_params=pltpu.CompilerParams(vmem_limit_bytes=48 * 1024 * 1024),
        name="backward",
    )(me, stats, key, hot, dense, saved, prop_out, *masks)


def sum_replicas(x):
    count = lax.axis_size("rep")
    if count != 4:
        return lax.psum(x, "rep")
    other = [lax.ppermute(x, "rep", [(i, i ^ s) for i in range(count)]) for s in (1, 2, 3)]
    return (x + other[0]) + (other[1] + other[2])


def on_device(
    feature_grid,
    fine_in,
    fine_mid,
    fine_out,
    prop_in,
    prop_out,
    sample_cells,
    sample_geometry,
    slot_ray,
    slot_rank,
    bucket_count,
):
    parts = lax.axis_size("dom")
    cap = slot_ray.shape[3]
    features = feature_grid.shape[1]
    prop_hidden = prop_in.shape[1]
    outgoing = pack(
        sample_geometry[:, 0, 0], slot_ray[0, 0], slot_rank[0, 0], bucket_count.reshape(-1, 1)
    )
    arrived = lax.all_to_all(outgoing, "dom", split_axis=0, concat_axis=0, tiled=True)
    corners = gather_corners(sample_cells.reshape(-1), feature_grid[0], parts)
    saved, dense, summary = forward(
        corners, arrived, fine_in[0].T, prop_in[0], fine_mid[0], fine_out, prop_out, cap
    )
    stats = lax.all_to_all(
        jnp.broadcast_to(summary[None], (parts,) + summary.shape),
        "dom", split_axis=0, concat_axis=0, tiled=True,
    )
    me = lax.axis_index("dom").reshape(1).astype(jnp.int32)
    marks = slot_marks(me, arrived, cap)
    ray_loss, grads = backward(me, stats, dense, saved, prop_out, marks, cap)
    sums = sum_replicas(grads)
    in_sum = sums[:prop_hidden, :features]
    out_sum = sums[prop_hidden, features:]
    return (ray_loss.reshape(1, 1, -1), in_sum[None], out_sum[None])


def solution(mesh):
    return jax.shard_map(
        on_device,
        mesh=mesh,
        in_specs=(
            P("dom", None, None),
            P("dom", None, None),
            P("dom", None, None, None),
            P("dom", None),
            P("dom", None, None),
            P("dom", None),
            P("dom", "rep", None, None),
            P(None, "dom", "rep", None, None),
            P("dom", "rep", None, None),
            P("dom", "rep", None, None),
            P("dom", "rep", None),
        ),
        out_specs=(P("dom", "rep", None), P("dom", None, None), P("dom", None)),
        check_vma=False,
    )
```

```python
import functools

import jax
import jax.numpy as jnp
from jax import lax
from jax.experimental import pallas as pl
from jax.experimental.pallas import tpu as pltpu
from jax.sharding import PartitionSpec as P

GR = 32
RAY_DEV = 256
LANES = 128
BLOCK = 256
BUILD_UNROLL = 31
DEPTH = 4

distill_weight = 50.0
F32 = jnp.float32
BF16 = jnp.bfloat16


def dot(a, b):
    return lax.dot_general(a, b, (((1,), (0,)), ((), ())), preferred_element_type=F32)


def dot_nt(a, b):
    return lax.dot_general(a, b, (((1,), (1,)), ((), ())), preferred_element_type=F32)


def split3(x):
    hi = x.astype(BF16)
    rest = x - hi.astype(F32)
    mid = rest.astype(BF16)
    low = (rest - mid.astype(F32)).astype(BF16)
    return [hi, mid, low]


def stack_rows(arrays, row):
    return jnp.concatenate([x[row : row + 1] for x in arrays], axis=0)


def flatten_slots(x, cap):
    parts = x.shape[0]
    per = LANES // cap
    lane = lax.broadcasted_iota(jnp.int32, (1, LANES), 1)
    wide = jnp.concatenate([x] * per, axis=1)
    out = []
    for first in range(0, parts, per):
        row = wide[first : first + 1]
        for k in range(1, per):
            row = jnp.where(lane // cap == k, wide[first + k : first + k + 1], row)
        out.append(row)
    return jnp.concatenate(out, axis=1)


def pack_kernel(geometry_ref, ray_ref, rank_ref, count_ref, out_ref):
    parts, cap = ray_ref.shape
    width = geometry_ref.shape[2]
    extra = out_ref.shape[1] - 4
    sub = lax.broadcasted_iota(jnp.int32, (parts, cap), 0)
    count = jnp.zeros((parts, cap), jnp.int32)
    for p in range(parts):
        count = jnp.where(sub == p, count_ref[p], count)
    live = lax.broadcasted_iota(jnp.int32, (parts, cap), 1) < count
    ray = jnp.where(live, ray_ref[...], -1).astype(F32)
    marks = jnp.concatenate(
        [flatten_slots(ray, cap), flatten_slots(rank_ref[...].astype(F32), cap)], axis=1
    )
    spare = extra * width - marks.shape[1]
    if spare:
        marks = jnp.concatenate([marks, jnp.zeros((1, spare), F32)], axis=1)
    marks = [marks[:, e * width : (e + 1) * width] for e in range(extra)]
    g = [geometry_ref[j].astype(F32) for j in range(4)]
    for p in range(parts):
        block = [x[p : p + 1] for x in g] + marks
        out_ref[p] = jnp.concatenate(block, axis=0).astype(BF16)


def pack(geometry, ray, rank, count):
    parts, width = geometry.shape[1:]
    extra = -(-2 * ray.size // width)
    vmem = pl.BlockSpec(memory_space=pltpu.VMEM)
    return pl.pallas_call(
        pack_kernel,
        out_shape=jax.ShapeDtypeStruct((parts, 4 + extra, width), BF16),
        in_specs=[vmem] * 3 + [pl.BlockSpec(memory_space=pltpu.SMEM)],
        out_specs=vmem,
        name="pack",
    )(geometry, ray, rank, count)


def marks_kernel(cap, me_ref, arrived_ref, key_ref, hot_ref, *mask_ref):
    me = me_ref[0]
    parts = arrived_ref.shape[0]
    slots = parts * cap
    width = arrived_ref.shape[2]
    extra = arrived_ref.shape[1] - 4
    ray, rank = [], []
    for q in range(parts):
        marks = [arrived_ref[q].astype(F32)[4 + e : 5 + e] for e in range(extra)]
        marks = marks[0] if extra == 1 else jnp.concatenate(marks, axis=1)
        ray.append(marks[:, :slots])
        rank.append(marks[:, slots : 2 * slots])
    key = jnp.concatenate(ray, axis=0) * (2.0 * parts) + jnp.concatenate(rank, axis=0)
    key_ref[...] = key
    key_t = key.T
    mine = lax.broadcasted_iota(jnp.int32, (slots, parts), 1) == me
    key_col = jnp.sum(jnp.where(mine, key_t, 0.0), axis=1, keepdims=True)
    ray = lax.broadcasted_iota(jnp.int32, (slots, RAY_DEV), 1).astype(F32)
    rest = key_col - ray * (2.0 * parts)
    hot_ref[...] = ((rest >= 0) & (rest < 2 * parts)).astype(BF16)
    if mask_ref:
        for q in range(parts):
            gap = key[q : q + 1] - key_t[:, q : q + 1]
            mask_ref[0][q] = ((gap > 0) & (gap < parts)).astype(BF16)


def slot_marks(me, arrived, cap):
    parts = arrived.shape[0]
    slots = parts * cap
    vmem = pl.BlockSpec(memory_space=pltpu.VMEM)
    shapes = [
        jax.ShapeDtypeStruct((parts, slots), F32),
        jax.ShapeDtypeStruct((slots, RAY_DEV), BF16),
    ]
    if slots <= 256:
        shapes.append(jax.ShapeDtypeStruct((parts, slots, slots), BF16))
    return pl.pallas_call(
        functools.partial(marks_kernel, cap),
        out_shape=tuple(shapes),
        in_specs=[pl.BlockSpec(memory_space=pltpu.SMEM), vmem],
        out_specs=(vmem,) * len(shapes),
        cost_estimate=pl.CostEstimate(
            flops=parts * slots * slots * 8, bytes_accessed=4 << 20, transcendentals=0
        ),
        name="slot_marks",
    )(me, arrived)


def lane_fold(x, cap):
    shift = LANES // 2
    while shift >= cap:
        x = x + pltpu.roll(x, shift, 1)
        shift //= 2
    return x


def running(pieces, cap):
    lane = lax.broadcasted_iota(jnp.int32, pieces[0].shape, 1)
    carry = jnp.zeros_like(pieces[0])
    out = []
    for x in pieces:
        y = x
        shift = cap
        while shift < LANES:
            y = y + jnp.where(lane >= shift, pltpu.roll(y, shift, 1), 0.0)
            shift *= 2
        out.append(carry + y)
        carry = carry + lane_fold(x, cap)
    return out, carry


def trailing(pieces, cap):
    lane = lax.broadcasted_iota(jnp.int32, pieces[0].shape, 1)
    carry = jnp.zeros_like(pieces[0])
    out = []
    for x in reversed(pieces):
        y = x
        shift = cap
        while shift < LANES:
            y = y + jnp.where(lane < LANES - shift, pltpu.roll(y, LANES - shift, 1), 0.0)
            shift *= 2
        out.append(carry + y)
        carry = carry + lane_fold(x, cap)
    return out[::-1]


def softplus(x):
    return jnp.maximum(x, 0.0) + jnp.log1p(jnp.exp(-jnp.abs(x)))


def pieces_of(x):
    return [x[:, v * LANES : (v + 1) * LANES] for v in range(x.shape[1] // LANES)]


def build_table(grid_ref, table, shifted):
    cells = grid_ref.shape[1]
    plane = GR * GR
    span = 2048

    def shift(b, carry):
        c0 = pl.multiple_of(b * span, span)
        x = grid_ref[:, pl.ds(c0, span + LANES)]
        shifted[:, pl.ds(c0, span)] = x[:, GR : GR + span]
        return carry

    lax.fori_loop(0, cells // span - 1, shift, 0)
    last = grid_ref[:, cells - span :]
    shifted[:, cells - span :] = jnp.concatenate([last[:, GR:], last[:, :GR]], axis=1)

    def build(b, carry):
        c0 = pl.multiple_of(b * 2 * BLOCK, 2 * BLOCK)
        for half in range(2):
            x = [
                ref[:, pl.ds(c0 + half * BLOCK + across, BLOCK)]
                for across in (0, plane)
                for ref in (grid_ref, shifted)
            ]
            rows = jnp.concatenate(x, axis=0).T.astype(F32)
            table[pl.ds(c0 + half * BLOCK, BLOCK), :] = rows
        return carry

    lax.fori_loop(0, (cells - plane) // (2 * BLOCK), build, 0, unroll=BUILD_UNROLL)


def forward_kernel(
    cap, idx_ref, grid_ref, arrived_ref, fine_in_ref, prop_in_ref, mid_ref, fine_out_ref,
    prop_out_ref, saved_ref, dense_ref, summary_ref,
    table, shifted, rows, eye, feats, weights, spacing, first, head, fine_logit, prop_logit,
):
    step = pl.program_id(0)
    parts = arrived_ref.shape[0]
    width = arrived_ref.shape[2]
    blocks = width // BLOCK
    features = grid_ref.shape[0]
    hidden = mid_ref.shape[1]
    prop_hidden = prop_in_ref.shape[0]

    def gather(row, block, pair):
        start = row * width
        for u in range(BLOCK):
            k = idx_ref.at[pl.ds(block * BLOCK + u, idx_ref.shape[0] - width + 1)][start]
            pair[2 * u : 2 * u + 2, :] = table[pl.ds(k, 2), :]

    def interpolate(block, pair, slot):
        near = pair[pl.ds(0, BLOCK, stride=2), :].astype(BF16)
        far = pair[pl.ds(1, BLOCK, stride=2), :].astype(BF16)
        unit = jnp.concatenate([eye[0], eye[1]], axis=1)
        t = dot_nt(unit, jnp.concatenate([near, far], axis=1))
        at = slice(block * BLOCK, (block + 1) * BLOCK)
        total = jnp.zeros((features, BLOCK), F32)
        for corner in range(8):
            place = (corner % 2) * 4 + corner // 2
            w = weights[corner, pl.ds(step, 1), at]
            total = total + t[place * features : (place + 1) * features] * w
        feats[slot, :, at] = total.astype(BF16)

    def networks(row, slot):
        feat = feats[slot]
        both = jnp.maximum(dot(first[...], feat), 0.0).astype(BF16)
        h = both[:hidden]
        ph = both[hidden:]
        for layer in range(mid_ref.shape[0]):
            h = jnp.maximum(dot(mid_ref[layer], h), 0.0).astype(BF16)
        logits = dot(head[...], jnp.concatenate([h, ph], axis=0))
        fine_logit[pl.ds(row, 1), :] = logits[0:1]
        prop_logit[pl.ds(row, 1), :] = logits[1:2]
        saved_ref[:features, :] = feat
        saved_ref[features:, :] = ph

    @pl.when(step == 0)
    def _():
        down = lax.broadcasted_iota(jnp.int32, (BLOCK, BLOCK), 0)
        across = lax.broadcasted_iota(jnp.int32, (BLOCK, BLOCK), 1)
        same = (down == across).astype(BF16)
        eye[0] = same[:, :LANES]
        eye[1] = same[:, LANES:]
        feats[...] = jnp.zeros(feats.shape, BF16)
        whole = [arrived_ref[q].astype(F32) for q in range(parts)]
        g = [stack_rows(whole, j) for j in range(4)]
        spacing[...] = g[3]
        first[:hidden, :] = fine_in_ref[...].astype(F32).T.astype(BF16)
        first[hidden:, :] = prop_in_ref[...]
        zero_f = jnp.zeros((1, prop_hidden), F32)
        zero_p = jnp.zeros((1, hidden), F32)
        top = jnp.concatenate([fine_out_ref[...].astype(F32), zero_f], axis=1)
        low = jnp.concatenate([zero_p, prop_out_ref[...].astype(F32)], axis=1)
        rest = jnp.zeros((6, hidden + prop_hidden), F32)
        head[...] = jnp.concatenate([top, low, rest], axis=0).astype(BF16)
        for corner in range(8):
            bits = (corner // 4, corner // 2 % 2, corner % 2)
            w = [x if bit else 1.0 - x for x, bit in zip(g, bits)]
            weights[corner] = w[0] * w[1] * w[2]
        build_table(grid_ref, table, shifted)
        gather(0, 0, rows.at[0])

    @pl.when(step < parts)
    def _():
        networks(jnp.maximum(step - 1, 0), (step + 1) % 2)
        for j in range(blocks):
            ahead = rows.at[(j + 1) % DEPTH]
            if j + 1 < blocks:
                gather(step, j + 1, ahead)
            else:
                gather(jnp.minimum(step + 1, parts - 1), 0, ahead)
            interpolate(j, rows.at[j % DEPTH], step % 2)

    @pl.when(step == parts)
    def _():
        networks(parts - 1, (parts - 1) % 2)
        space = pieces_of(spacing[...])
        results = []
        for k, ref in enumerate((prop_logit, fine_logit)):
            logit = pieces_of(ref[...])
            optical = [softplus(x) * s for x, s in zip(logit, space)]
            depth, whole = running(optical, cap)
            early = [jnp.exp(o - d) for o, d in zip(optical, depth)]
            absorb = [e - jnp.exp(-d) for e, d in zip(early, depth)]
            results.append((absorb, whole))
            if k == 0:
                slope = [s * jax.nn.sigmoid(x) for x, s in zip(logit, space)]
                dense_ref[0] = jnp.concatenate(early, axis=1)
                dense_ref[3] = jnp.concatenate(slope, axis=1)
        (a, log_prop), (b, log_fine) = results
        dense_ref[1] = jnp.concatenate(a, axis=1)
        dense_ref[2] = jnp.concatenate(b, axis=1)
        sums = [lane_fold(sum(x * y for x, y in zip(s, t)), cap) for s, t in ((a, a), (a, b), (b, b))]
        stats = [-log_prop, -log_fine] + sums
        per = LANES // cap
        group = lax.broadcasted_iota(jnp.int32, stats[0].shape, 1) // cap
        slabs = []
        for s in range(-(-len(stats) // per)):
            slab = jnp.zeros_like(stats[0])
            for k, x in enumerate(stats[s * per : (s + 1) * per]):
                slab = jnp.where(group == k, x, slab)
            slabs.append(slab)
        summary = jnp.concatenate(slabs, axis=1)
        for p in range(parts):
            summary_ref[p] = summary


def forward(cells, grid, arrived, fine_in, prop_in, mid, fine_out, prop_out, cap):
    parts, _, width = arrived.shape
    features, total = grid.shape
    hidden = mid.shape[1]
    prop_hidden = prop_in.shape[0]
    kept = features + prop_hidden
    stat_lanes = -(-5 // (LANES // cap)) * LANES
    whole = lambda shape: pl.BlockSpec(shape, lambda q: (0,) * len(shape))
    small = (arrived, fine_in, prop_in, mid, fine_out, prop_out)
    return pl.pallas_call(
        functools.partial(forward_kernel, cap),
        grid=(parts + 1,),
        out_shape=(
            jax.ShapeDtypeStruct((kept, parts * width), BF16),
            jax.ShapeDtypeStruct((4, parts, width), F32),
            jax.ShapeDtypeStruct((parts, parts, stat_lanes), F32),
        ),
        in_specs=[
            pl.BlockSpec(memory_space=pltpu.SMEM),
            pl.BlockSpec((features, total), lambda q: (0, 0), pipeline_mode=pl.Buffered(1)),
        ]
        + [whole(x.shape) for x in small],
        out_specs=(
            pl.BlockSpec((kept, width), lambda q: (0, jnp.maximum(q - 1, 0))),
            whole((4, parts, width)),
            whole((parts, parts, stat_lanes)),
        ),
        scratch_shapes=[
            pltpu.VMEM((total, LANES), F32),
            pltpu.VMEM((features, total), BF16),
            pltpu.VMEM((DEPTH, 2 * BLOCK, LANES), F32),
            pltpu.VMEM((2, BLOCK, LANES), BF16),
            pltpu.VMEM((2, features, width), BF16),
            pltpu.VMEM((8, parts, width), F32),
            pltpu.VMEM((parts, width), F32),
            pltpu.VMEM((hidden + prop_hidden, features), BF16),
            pltpu.VMEM((8, hidden + prop_hidden), BF16),
            pltpu.VMEM((parts, width), F32),
            pltpu.VMEM((parts, width), F32),
        ],
        compiler_params=pltpu.CompilerParams(vmem_limit_bytes=40 * 1024 * 1024),
        name="forward",
    )(cells, grid, *small)


def backward_kernel(
    cap, me_ref, stats_ref, key_ref, hot_ref, dense_ref, saved_ref, prop_out_ref, *rest,
):
    masks, (loss_ref, grad_ref, slope_ref, *keys_t) = rest[:-3], rest[-3:]
    if stats_ref.shape[0] * cap > 256:
        masks, (loss_ref, grad_ref, slope_ref, *keys_t) = (), rest
    me = me_ref[0]
    parts = stats_ref.shape[0]
    slots = key_ref.shape[1]
    per = LANES // cap
    width = dense_ref.shape[2]
    prop_hidden = prop_out_ref.shape[1]
    key = key_ref[...]
    live = (key >= 0).astype(F32)
    sub = lax.broadcasted_iota(jnp.int32, (parts, slots), 0)
    if not masks:
        keys_t[0][...] = key.T

    def mask_of(q):
        lane = lax.broadcasted_iota(jnp.int32, (slots, parts), 1)
        col = jnp.sum(jnp.where(lane == q, keys_t[0][...], 0.0), axis=1, keepdims=True)
        row = jnp.sum(jnp.where(sub == q, key, 0.0), axis=0, keepdims=True)
        gap = row - col
        return ((gap > 0) & (gap < parts)).astype(BF16)

    def over(body, init):
        if masks:
            for q in range(parts):
                init = body(q, init)
            return init
        return lax.fori_loop(0, parts, body, init)

    group = lax.broadcasted_iota(jnp.int32, (parts, LANES), 1) // cap

    def flat(j):
        slab = slice((j // per) * LANES, (j // per + 1) * LANES)
        out = []
        for half in range(slots // LANES):
            x = jnp.zeros((parts, LANES), F32)
            for k in range(per):
                piece = stats_ref[half * per + k, :, slab]
                shift = ((k - j % per) * cap) % LANES
                x = jnp.where(group == k, pltpu.roll(piece, shift, 1) if shift else piece, x)
            out.append(x)
        return jnp.concatenate(out, axis=1)

    log_prop, log_fine, sum_aa, sum_ab, sum_bb = [flat(j) for j in range(5)]
    terms = split3(log_prop * live) + split3(log_fine * live)
    stacked = jnp.concatenate(terms, axis=0)

    def lead(q, acc):
        m = masks[0][q] if masks else mask_of(q)
        y = dot(stacked, m)
        return tuple(
            jnp.where(sub == q, y[k * parts : (k + 1) * parts], x) for k, x in enumerate(acc)
        )

    zero = jnp.zeros((parts, slots), F32)
    lead_sums = over(lead, (zero,) * 6)
    entry_prop = jnp.exp(lead_sums[0] + lead_sums[1] + lead_sums[2]) * live
    entry_fine = jnp.exp(lead_sums[3] + lead_sums[4] + lead_sums[5]) * live
    seg_loss = (
        entry_prop * entry_prop * sum_aa
        - 2.0 * entry_prop * entry_fine * sum_ab
        + entry_fine * entry_fine * sum_bb
    )
    slot_grad = distill_weight * (entry_prop * sum_aa - entry_fine * sum_ab) * entry_prop
    mine = pl.ds(pl.multiple_of(me * cap, cap), cap)
    grads = jnp.concatenate(split3(slot_grad), axis=0)
    sub_cap = lax.broadcasted_iota(jnp.int32, (parts, cap), 0)

    def tail(q, acc):
        if masks:
            m = masks[0][q, mine, :]
            y = dot_nt(grads, m)
        else:
            y = dot_nt(grads, mask_of(q))
            y = own_lanes(y)
        y = y[:parts] + y[parts : 2 * parts] + y[2 * parts :]
        return jnp.where(sub_cap == q, y, acc)

    def own_lanes(x):
        out = x[:, :cap]
        for p in range(1, parts):
            out = jnp.where(me == p, x[:, p * cap : (p + 1) * cap], out)
        return out

    carried = over(tail, jnp.zeros((parts, cap), F32)) * own_lanes(live)
    coef_aa = own_lanes(0.5 * distill_weight * entry_prop * entry_prop)
    coef_ab = own_lanes(-distill_weight * entry_prop * entry_fine)

    spread = dot(jnp.concatenate(split3(seg_loss), axis=0), hot_ref[...])
    spread = spread[:parts] + spread[parts : 2 * parts] + spread[2 * parts :]
    sub_ray = lax.broadcasted_iota(jnp.int32, (parts, RAY_DEV), 0)
    loss_ref[...] = (0.5 * distill_weight) * jnp.sum(
        jnp.where(sub_ray == me, spread, 0.0), axis=0, keepdims=True
    )

    tile = lambda x: jnp.concatenate([x] * per, axis=1)
    c_aa, c_ab, c_log = tile(2.0 * coef_aa), tile(coef_ab), tile(carried)
    early, a, b, slope = [pieces_of(dense_ref[k]) for k in range(4)]
    d_absorb = [c_aa * x + c_ab * y for x, y in zip(a, b)]
    back = trailing([d * x for d, x in zip(d_absorb, a)], cap)
    logit_grad = [
        ((d * e - c_log - r) * s).astype(BF16).astype(F32)
        for d, e, r, s in zip(d_absorb, early, back, slope)
    ]
    slope_ref[...] = jnp.concatenate(logit_grad, axis=1)
    features = saved_ref.shape[0] - prop_hidden
    wide = jnp.broadcast_to(prop_out_ref[...].astype(F32), (prop_hidden, prop_hidden))
    same = lax.broadcasted_iota(jnp.int32, wide.shape, 0) == lax.broadcasted_iota(
        jnp.int32, wide.shape, 1
    )
    out_col = jnp.sum(jnp.where(same, wide, 0.0), axis=1, keepdims=True)
    first_row = lax.broadcasted_iota(jnp.int32, (prop_hidden, width), 0) == 0

    def accumulate(q, total):
        at = pl.ds(pl.multiple_of(q * width, width), width)
        row = slope_ref[pl.ds(q, 1), :]
        kept = saved_ref[:, at]
        hidden_grad = jnp.where(kept[features:].astype(F32) > 0, out_col * row, 0.0).astype(BF16)
        alone = jnp.where(first_row, row, 0.0).astype(BF16)
        return total + dot_nt(jnp.concatenate([hidden_grad, alone], axis=0), kept)

    total = jnp.zeros((2 * prop_hidden, saved_ref.shape[0]), F32)
    total = lax.fori_loop(0, parts, accumulate, total)
    grad_ref[...] = total


def backward(me, stats, dense, saved, prop_out, marks, cap):
    key, hot, *masks = marks
    parts, slots = key.shape
    width = dense.shape[2]
    prop_hidden = prop_out.shape[1]
    vmem = pl.BlockSpec(memory_space=pltpu.VMEM)
    return pl.pallas_call(
        functools.partial(backward_kernel, cap),
        out_shape=(
            jax.ShapeDtypeStruct((1, RAY_DEV), F32),
            jax.ShapeDtypeStruct((2 * prop_hidden, saved.shape[0]), F32),
        ),
        in_specs=[pl.BlockSpec(memory_space=pltpu.SMEM)] + [vmem] * (6 + len(masks)),
        out_specs=(vmem, vmem),
        scratch_shapes=[pltpu.VMEM((parts, width), F32)]
        + ([] if masks else [pltpu.VMEM((slots, parts), F32)]),
        compiler_params=pltpu.CompilerParams(vmem_limit_bytes=(16 if masks else 48) * 1024 * 1024),
        name="backward",
    )(me, stats, key, hot, dense, saved, prop_out, *masks)


def sum_replicas(x):
    count = lax.axis_size("rep")
    if count != 4:
        return lax.psum(x, "rep")
    other = [lax.ppermute(x, "rep", [(i, i ^ s) for i in range(count)]) for s in (1, 2, 3)]
    return (x + other[0]) + (other[1] + other[2])


def on_device(
    feature_grid,
    fine_in,
    fine_mid,
    fine_out,
    prop_in,
    prop_out,
    sample_cells,
    sample_geometry,
    slot_ray,
    slot_rank,
    bucket_count,
):
    parts = lax.axis_size("dom")
    cap = slot_ray.shape[3]
    features = feature_grid.shape[1]
    prop_hidden = prop_in.shape[1]
    outgoing = pack(
        sample_geometry[:, 0, 0], slot_ray[0, 0], slot_rank[0, 0], bucket_count.reshape(-1)
    )
    arrived = lax.all_to_all(outgoing, "dom", split_axis=0, concat_axis=0, tiled=True)
    saved, dense, summary = forward(
        sample_cells.reshape(-1), feature_grid[0], arrived,
        fine_in[0].T, prop_in[0], fine_mid[0], fine_out, prop_out, cap,
    )
    stats = lax.all_to_all(summary, "dom", split_axis=0, concat_axis=0, tiled=True)
    me = lax.axis_index("dom").reshape(1).astype(jnp.int32)
    marks = slot_marks(me, arrived, cap)
    ray_loss, grads = backward(me, stats, dense, saved, prop_out, marks, cap)
    sums = sum_replicas(grads)
    in_sum = sums[:prop_hidden, :features]
    out_sum = sums[prop_hidden, features:]
    return (ray_loss.reshape(1, 1, -1), in_sum[None], out_sum[None])


def solution(mesh):
    return jax.shard_map(
        on_device,
        mesh=mesh,
        in_specs=(
            P("dom", None, None),
            P("dom", None, None),
            P("dom", None, None, None),
            P("dom", None),
            P("dom", None, None),
            P("dom", None),
            P("dom", "rep", None, None),
            P(None, "dom", "rep", None, None),
            P("dom", "rep", None, None),
            P("dom", "rep", None, None),
            P("dom", "rep", None),
        ),
        out_specs=(P("dom", "rep", None), P("dom", None, None), P("dom", None)),
        check_vma=False,
    )
```

```python
import functools

import jax
import jax.numpy as jnp
from jax import lax
from jax.experimental import pallas as pl
from jax.experimental.pallas import tpu as pltpu
from jax.sharding import PartitionSpec as P

GR = 32
RAY_DEV = 256
LANES = 128
BLOCK = 256
CHUNKS = 8
DEPTH = 4

distill_weight = 50.0
F32 = jnp.float32
BF16 = jnp.bfloat16


def dot(a, b):
    return lax.dot_general(a, b, (((1,), (0,)), ((), ())), preferred_element_type=F32)


def dot_nt(a, b):
    return lax.dot_general(a, b, (((1,), (1,)), ((), ())), preferred_element_type=F32)


def split3(x):
    hi = x.astype(BF16)
    rest = x - hi.astype(F32)
    mid = rest.astype(BF16)
    low = (rest - mid.astype(F32)).astype(BF16)
    return [hi, mid, low]


def in_hbm(x):
    return pltpu.with_memory_space_constraint(x, pltpu.HBM)


def stack_rows(arrays, row):
    return jnp.concatenate([x[row : row + 1] for x in arrays], axis=0)


def flatten_slots(x, cap):
    parts = x.shape[0]
    per = LANES // cap
    lane = lax.broadcasted_iota(jnp.int32, (1, LANES), 1)
    wide = jnp.concatenate([x] * per, axis=1)
    out = []
    for first in range(0, parts, per):
        row = wide[first : first + 1]
        for k in range(1, per):
            row = jnp.where(lane // cap == k, wide[first + k : first + k + 1], row)
        out.append(row)
    return jnp.concatenate(out, axis=1)


def pack_kernel(geometry_ref, ray_ref, rank_ref, count_ref, out_ref):
    parts, cap = ray_ref.shape
    sub = lax.broadcasted_iota(jnp.int32, (parts, cap), 0)
    count = jnp.zeros((parts, cap), jnp.int32)
    for p in range(parts):
        count = jnp.where(sub == p, count_ref[p], count)
    live = lax.broadcasted_iota(jnp.int32, (parts, cap), 1) < count
    ray = jnp.where(live, ray_ref[...], -1).astype(F32)
    marks = jnp.concatenate(
        [flatten_slots(ray, cap), flatten_slots(rank_ref[...].astype(F32), cap)], axis=1
    )
    quarter = marks.shape[1] // 4
    g = [geometry_ref[j].astype(F32) for j in range(4)]
    for p in range(parts):
        rows = [
            jnp.concatenate([x[p : p + 1], marks[:, j * quarter : (j + 1) * quarter]], axis=1)
            for j, x in enumerate(g)
        ]
        out_ref[p] = jnp.concatenate(rows, axis=0).astype(BF16)


def pack(geometry, ray, rank, count):
    parts, width = geometry.shape[1:]
    vmem = pl.BlockSpec(memory_space=pltpu.VMEM)
    return pl.pallas_call(
        pack_kernel,
        out_shape=jax.ShapeDtypeStruct((parts, 4, width + ray.size // 2), BF16),
        in_specs=[vmem] * 3 + [pl.BlockSpec(memory_space=pltpu.SMEM)],
        out_specs=vmem,
        name="pack",
    )(geometry, ray, rank, count)


def marks_kernel(cap, me_ref, arrived_ref, key_ref, hot_ref, *mask_ref):
    me = me_ref[0]
    parts = arrived_ref.shape[0]
    slots = parts * cap
    width = arrived_ref.shape[2] - slots // 2
    ray, rank = [], []
    for q in range(parts):
        marks = arrived_ref[q, :, width:].astype(F32)
        ray.append(jnp.concatenate([marks[0:1], marks[1:2]], axis=1))
        rank.append(jnp.concatenate([marks[2:3], marks[3:4]], axis=1))
    key = jnp.concatenate(ray, axis=0) * (2.0 * parts) + jnp.concatenate(rank, axis=0)
    key_ref[...] = key
    key_t = key.T
    mine = lax.broadcasted_iota(jnp.int32, (slots, parts), 1) == me
    key_col = jnp.sum(jnp.where(mine, key_t, 0.0), axis=1, keepdims=True)
    ray = lax.broadcasted_iota(jnp.int32, (slots, RAY_DEV), 1).astype(F32)
    rest = key_col - ray * (2.0 * parts)
    hot_ref[...] = ((rest >= 0) & (rest < 2 * parts)).astype(BF16)
    if mask_ref:
        for q in range(parts):
            gap = key[q : q + 1] - key_t[:, q : q + 1]
            mask_ref[0][q] = ((gap > 0) & (gap < parts)).astype(BF16)


def slot_marks(me, arrived, cap):
    parts = arrived.shape[0]
    slots = parts * cap
    vmem = pl.BlockSpec(memory_space=pltpu.VMEM)
    shapes = [
        jax.ShapeDtypeStruct((parts, slots), F32),
        jax.ShapeDtypeStruct((slots, RAY_DEV), BF16),
    ]
    if slots <= 256:
        shapes.append(jax.ShapeDtypeStruct((parts, slots, slots), BF16))
    return pl.pallas_call(
        functools.partial(marks_kernel, cap),
        out_shape=tuple(shapes),
        in_specs=[pl.BlockSpec(memory_space=pltpu.SMEM), vmem],
        out_specs=(vmem,) * len(shapes),
        cost_estimate=pl.CostEstimate(
            flops=parts * slots * slots * 8, bytes_accessed=4 << 20, transcendentals=0
        ),
        compiler_params=pltpu.CompilerParams(vmem_limit_bytes=12 * 1024 * 1024),
        name="slot_marks",
    )(me, arrived)


def lane_fold(x, cap):
    shift = LANES // 2
    while shift >= cap:
        x = x + pltpu.roll(x, shift, 1)
        shift //= 2
    return x


def running(pieces, cap):
    lane = lax.broadcasted_iota(jnp.int32, pieces[0].shape, 1)
    carry = jnp.zeros_like(pieces[0])
    out = []
    for x in pieces:
        y = x
        shift = cap
        while shift < LANES:
            y = y + jnp.where(lane >= shift, pltpu.roll(y, shift, 1), 0.0)
            shift *= 2
        out.append(carry + y)
        carry = carry + lane_fold(x, cap)
    return out, carry


def trailing(pieces, cap):
    lane = lax.broadcasted_iota(jnp.int32, pieces[0].shape, 1)
    carry = jnp.zeros_like(pieces[0])
    out = []
    for x in reversed(pieces):
        y = x
        shift = cap
        while shift < LANES:
            y = y + jnp.where(lane < LANES - shift, pltpu.roll(y, LANES - shift, 1), 0.0)
            shift *= 2
        out.append(carry + y)
        carry = carry + lane_fold(x, cap)
    return out[::-1]


def softplus(x):
    return jnp.maximum(x, 0.0) + jnp.log1p(jnp.exp(-jnp.abs(x)))


def pieces_of(x):
    return [x[:, v * LANES : (v + 1) * LANES] for v in range(x.shape[1] // LANES)]


def fetch_grid(grid_hbm, grid_ref, sem, c):
    chunk = grid_ref.shape[1] // CHUNKS
    at = pl.ds(c * chunk, chunk)
    return pltpu.make_async_copy(grid_hbm.at[:, at], grid_ref.at[:, at], sem.at[c])


def build_table(grid_hbm, grid_ref, sem, table):
    features, cells = grid_ref.shape
    plane = GR * GR
    span = 2 * BLOCK
    chunk = cells // CHUNKS
    upper = lax.broadcasted_iota(jnp.int32, (span, LANES), 1) // features % 2 == 1

    def build(i, carry, top):
        c0 = pl.multiple_of(top - (i + 1) * span, span)
        base = grid_ref[:, pl.ds(c0, span)]
        across = grid_ref[:, pl.ds(c0 + plane, span)]
        rows = jnp.concatenate([base, base, across, across], axis=0).T.astype(F32)
        table[pl.ds(c0, span), :] = jnp.where(
            upper, jnp.concatenate([rows[GR:], carry], axis=0), rows
        )
        return rows[:GR]

    carry = jnp.zeros((GR, LANES), F32)
    for c in reversed(range(CHUNKS)):
        fetch_grid(grid_hbm, grid_ref, sem, c).wait()
        top = cells - plane if c == CHUNKS - 1 else (c + 1) * chunk
        body = functools.partial(build, top=top)
        carry = lax.fori_loop(0, (top - c * chunk) // span, body, carry, unroll=True)


def forward_kernel(
    cap, idx_ref, grid_hbm, arrived_ref, fine_in_ref, prop_in_ref, mid_ref, fine_out_ref,
    prop_out_ref, saved_ref, dense_ref, summary_ref,
    table, grid_ref, grid_sem, rows, eye, feats, weights, spacing, first, head, fine_logit, prop_logit,
):
    step = pl.program_id(0)
    parts = arrived_ref.shape[0]
    width = idx_ref.shape[0] // parts
    blocks = width // BLOCK
    features = prop_in_ref.shape[1]
    hidden = mid_ref.shape[1]
    prop_hidden = prop_in_ref.shape[0]

    def gather(row, block, pair):
        start = row * width
        for u in range(BLOCK):
            k = idx_ref.at[pl.ds(block * BLOCK + u, idx_ref.shape[0] - width + 1)][start]
            pair[2 * u : 2 * u + 2, :] = table[pl.ds(k, 2), :]

    def interpolate(block, pair, slot):
        near = pair[pl.ds(0, BLOCK, stride=2), :].astype(BF16)
        far = pair[pl.ds(1, BLOCK, stride=2), :].astype(BF16)
        unit = jnp.concatenate([eye[0], eye[1]], axis=1)
        t = dot_nt(unit, jnp.concatenate([near, far], axis=1))
        at = slice(block * BLOCK, (block + 1) * BLOCK)
        total = jnp.zeros((features, BLOCK), F32)
        for corner in range(8):
            place = (corner % 2) * 4 + corner // 2
            w = weights[corner, pl.ds(step, 1), at]
            total = total + t[place * features : (place + 1) * features] * w
        feats[slot, :, at] = total.astype(BF16)

    def networks(row, slot):
        feat = feats[slot]
        both = jnp.maximum(dot(first[...], feat), 0.0).astype(BF16)
        h = both[:hidden]
        ph = both[hidden:]
        for layer in range(mid_ref.shape[0]):
            h = jnp.maximum(dot(mid_ref[layer], h), 0.0).astype(BF16)
        logits = dot(head[...], jnp.concatenate([h, ph], axis=0))
        fine_logit[pl.ds(row, 1), :] = logits[0:1]
        prop_logit[pl.ds(row, 1), :] = logits[1:2]
        saved_ref[:features, :] = feat
        saved_ref[features:, :] = ph

    @pl.when(step == 0)
    def _():
        for c in reversed(range(CHUNKS)):
            fetch_grid(grid_hbm, grid_ref, grid_sem, c).start()
        down = lax.broadcasted_iota(jnp.int32, (BLOCK, BLOCK), 0)
        across = lax.broadcasted_iota(jnp.int32, (BLOCK, BLOCK), 1)
        same = (down == across).astype(BF16)
        eye[0] = same[:, :LANES]
        eye[1] = same[:, LANES:]
        feats[...] = jnp.zeros(feats.shape, BF16)
        whole = [arrived_ref[q, :, :width].astype(F32) for q in range(parts)]
        g = [stack_rows(whole, j) for j in range(4)]
        spacing[...] = g[3]
        first[:hidden, :] = fine_in_ref[...].astype(F32).T.astype(BF16)
        first[hidden:, :] = prop_in_ref[...]
        zero_f = jnp.zeros((1, prop_hidden), F32)
        zero_p = jnp.zeros((1, hidden), F32)
        top = jnp.concatenate([fine_out_ref[...].astype(F32), zero_f], axis=1)
        low = jnp.concatenate([zero_p, prop_out_ref[...].astype(F32)], axis=1)
        rest = jnp.zeros((6, hidden + prop_hidden), F32)
        head[...] = jnp.concatenate([top, low, rest], axis=0).astype(BF16)
        for corner in range(8):
            bits = (corner // 4, corner // 2 % 2, corner % 2)
            w = [x if bit else 1.0 - x for x, bit in zip(g, bits)]
            weights[corner] = w[0] * w[1] * w[2]
        build_table(grid_hbm, grid_ref, grid_sem, table)
        gather(0, 0, rows.at[0])

    @pl.when(step < parts)
    def _():
        networks(jnp.maximum(step - 1, 0), (step + 1) % 2)
        for j in range(blocks):
            ahead = rows.at[(j + 1) % DEPTH]
            if j + 1 < blocks:
                gather(step, j + 1, ahead)
            else:
                gather(jnp.minimum(step + 1, parts - 1), 0, ahead)
            interpolate(j, rows.at[j % DEPTH], step % 2)

    @pl.when(step == parts)
    def _():
        networks(parts - 1, (parts - 1) % 2)
        space = pieces_of(spacing[...])
        results = []
        for k, ref in enumerate((prop_logit, fine_logit)):
            logit = pieces_of(ref[...])
            optical = [softplus(x) * s for x, s in zip(logit, space)]
            depth, whole = running(optical, cap)
            early = [jnp.exp(o - d) for o, d in zip(optical, depth)]
            absorb = [e - jnp.exp(-d) for e, d in zip(early, depth)]
            results.append((absorb, whole))
            if k == 0:
                slope = [s * jax.nn.sigmoid(x) for x, s in zip(logit, space)]
                dense_ref[0] = jnp.concatenate(early, axis=1)
                dense_ref[3] = jnp.concatenate(slope, axis=1)
        (a, log_prop), (b, log_fine) = results
        dense_ref[1] = jnp.concatenate(a, axis=1)
        dense_ref[2] = jnp.concatenate(b, axis=1)
        sums = [lane_fold(sum(x * y for x, y in zip(s, t)), cap) for s, t in ((a, a), (a, b), (b, b))]
        stats = [-log_prop, -log_fine] + sums
        per = LANES // cap
        group = lax.broadcasted_iota(jnp.int32, stats[0].shape, 1) // cap
        slabs = []
        for s in range(-(-len(stats) // per)):
            slab = jnp.zeros_like(stats[0])
            for k, x in enumerate(stats[s * per : (s + 1) * per]):
                slab = jnp.where(group == k, x, slab)
            slabs.append(slab)
        summary = jnp.concatenate(slabs, axis=1)
        for p in range(parts):
            summary_ref[p] = summary


def forward(cells, grid, arrived, fine_in, prop_in, mid, fine_out, prop_out, cap):
    parts = arrived.shape[0]
    width = cells.shape[0] // parts
    features, total = grid.shape
    hidden = mid.shape[1]
    prop_hidden = prop_in.shape[0]
    kept = features + prop_hidden
    stat_lanes = -(-5 // (LANES // cap)) * LANES
    whole = lambda shape: pl.BlockSpec(shape, lambda q: (0,) * len(shape))
    small = (arrived, fine_in, prop_in, mid, fine_out, prop_out)
    return pl.pallas_call(
        functools.partial(forward_kernel, cap),
        grid=(parts + 1,),
        out_shape=(
            jax.ShapeDtypeStruct((kept, parts * width), BF16),
            jax.ShapeDtypeStruct((4, parts, width), F32),
            jax.ShapeDtypeStruct((parts, parts, stat_lanes), F32),
        ),
        in_specs=[
            pl.BlockSpec(memory_space=pltpu.SMEM),
            pl.BlockSpec(memory_space=pltpu.HBM),
        ]
        + [whole(x.shape) for x in small],
        out_specs=(
            pl.BlockSpec((kept, width), lambda q: (0, jnp.maximum(q - 1, 0))),
            whole((4, parts, width)),
            whole((parts, parts, stat_lanes)),
        ),
        scratch_shapes=[
            pltpu.VMEM((total, LANES), F32),
            pltpu.VMEM((features, total), BF16),
            pltpu.SemaphoreType.DMA((CHUNKS,)),
            pltpu.VMEM((DEPTH, 2 * BLOCK, LANES), F32),
            pltpu.VMEM((2, BLOCK, LANES), BF16),
            pltpu.VMEM((2, features, width), BF16),
            pltpu.VMEM((8, parts, width), F32),
            pltpu.VMEM((parts, width), F32),
            pltpu.VMEM((hidden + prop_hidden, features), BF16),
            pltpu.VMEM((8, hidden + prop_hidden), BF16),
            pltpu.VMEM((parts, width), F32),
            pltpu.VMEM((parts, width), F32),
        ],
        compiler_params=pltpu.CompilerParams(vmem_limit_bytes=(32 + parts // 2) * 1024 * 1024),
        name="forward",
    )(cells, in_hbm(grid), arrived, *[in_hbm(x) for x in small[1:]])


def backward_kernel(
    cap, me_ref, stats_ref, key_ref, hot_ref, dense_ref, saved_ref, prop_out_ref, *rest,
):
    masks, (loss_ref, grad_ref, slope_ref, *keys_t) = rest[:-3], rest[-3:]
    if stats_ref.shape[0] * cap > 256:
        masks, (loss_ref, grad_ref, slope_ref, *keys_t) = (), rest
    me = me_ref[0]
    parts = stats_ref.shape[0]
    slots = key_ref.shape[1]
    per = LANES // cap
    width = dense_ref.shape[2]
    prop_hidden = prop_out_ref.shape[1]
    key = key_ref[...]
    live = (key >= 0).astype(F32)
    sub = lax.broadcasted_iota(jnp.int32, (parts, slots), 0)
    if not masks:
        keys_t[0][...] = key.T

    def mask_of(q):
        lane = lax.broadcasted_iota(jnp.int32, (slots, parts), 1)
        col = jnp.sum(jnp.where(lane == q, keys_t[0][...], 0.0), axis=1, keepdims=True)
        row = jnp.sum(jnp.where(sub == q, key, 0.0), axis=0, keepdims=True)
        gap = row - col
        return ((gap > 0) & (gap < parts)).astype(BF16)

    def over(body, init):
        if masks:
            for q in range(parts):
                init = body(q, init)
            return init
        return lax.fori_loop(0, parts, body, init)

    group = lax.broadcasted_iota(jnp.int32, (parts, LANES), 1) // cap

    def flat(j):
        slab = slice((j // per) * LANES, (j // per + 1) * LANES)
        out = []
        for half in range(slots // LANES):
            x = jnp.zeros((parts, LANES), F32)
            for k in range(per):
                piece = stats_ref[half * per + k, :, slab]
                shift = ((k - j % per) * cap) % LANES
                x = jnp.where(group == k, pltpu.roll(piece, shift, 1) if shift else piece, x)
            out.append(x)
        return jnp.concatenate(out, axis=1)

    log_prop, log_fine, sum_aa, sum_ab, sum_bb = [flat(j) for j in range(5)]
    terms = split3(log_prop * live) + split3(log_fine * live)
    stacked = jnp.concatenate(terms, axis=0)

    def lead(q, acc):
        m = masks[0][q] if masks else mask_of(q)
        y = dot(stacked, m)
        return tuple(
            jnp.where(sub == q, y[k * parts : (k + 1) * parts], x) for k, x in enumerate(acc)
        )

    zero = jnp.zeros((parts, slots), F32)
    lead_sums = over(lead, (zero,) * 6)
    entry_prop = jnp.exp(lead_sums[0] + lead_sums[1] + lead_sums[2]) * live
    entry_fine = jnp.exp(lead_sums[3] + lead_sums[4] + lead_sums[5]) * live
    seg_loss = (
        entry_prop * entry_prop * sum_aa
        - 2.0 * entry_prop * entry_fine * sum_ab
        + entry_fine * entry_fine * sum_bb
    )
    slot_grad = distill_weight * (entry_prop * sum_aa - entry_fine * sum_ab) * entry_prop
    mine = pl.ds(pl.multiple_of(me * cap, cap), cap)
    grads = jnp.concatenate(split3(slot_grad), axis=0)
    sub_cap = lax.broadcasted_iota(jnp.int32, (parts, cap), 0)

    def tail(q, acc):
        if masks:
            m = masks[0][q, mine, :]
            y = dot_nt(grads, m)
        else:
            y = dot_nt(grads, mask_of(q))
            y = own_lanes(y)
        y = y[:parts] + y[parts : 2 * parts] + y[2 * parts :]
        return jnp.where(sub_cap == q, y, acc)

    def own_lanes(x):
        out = x[:, :cap]
        for p in range(1, parts):
            out = jnp.where(me == p, x[:, p * cap : (p + 1) * cap], out)
        return out

    carried = over(tail, jnp.zeros((parts, cap), F32)) * own_lanes(live)
    coef_aa = own_lanes(0.5 * distill_weight * entry_prop * entry_prop)
    coef_ab = own_lanes(-distill_weight * entry_prop * entry_fine)

    spread = dot(jnp.concatenate(split3(seg_loss), axis=0), hot_ref[...])
    spread = spread[:parts] + spread[parts : 2 * parts] + spread[2 * parts :]
    sub_ray = lax.broadcasted_iota(jnp.int32, (parts, RAY_DEV), 0)
    loss_ref[...] = (0.5 * distill_weight) * jnp.sum(
        jnp.where(sub_ray == me, spread, 0.0), axis=0, keepdims=True
    )

    tile = lambda x: jnp.concatenate([x] * per, axis=1)
    c_aa, c_ab, c_log = tile(2.0 * coef_aa), tile(coef_ab), tile(carried)
    early, a, b, slope = [pieces_of(dense_ref[k]) for k in range(4)]
    d_absorb = [c_aa * x + c_ab * y for x, y in zip(a, b)]
    back = trailing([d * x for d, x in zip(d_absorb, a)], cap)
    logit_grad = [
        ((d * e - c_log - r) * s).astype(BF16).astype(F32)
        for d, e, r, s in zip(d_absorb, early, back, slope)
    ]
    slope_ref[...] = jnp.concatenate(logit_grad, axis=1)
    features = saved_ref.shape[0] - prop_hidden
    wide = jnp.broadcast_to(prop_out_ref[...].astype(F32), (prop_hidden, prop_hidden))
    same = lax.broadcasted_iota(jnp.int32, wide.shape, 0) == lax.broadcasted_iota(
        jnp.int32, wide.shape, 1
    )
    out_col = jnp.sum(jnp.where(same, wide, 0.0), axis=1, keepdims=True)
    first_row = lax.broadcasted_iota(jnp.int32, (prop_hidden, width), 0) == 0

    def accumulate(q, total):
        at = pl.ds(pl.multiple_of(q * width, width), width)
        row = slope_ref[pl.ds(q, 1), :]
        kept = saved_ref[:, at]
        hidden_grad = jnp.where(kept[features:].astype(F32) > 0, out_col * row, 0.0).astype(BF16)
        alone = jnp.where(first_row, row, 0.0).astype(BF16)
        return total + dot_nt(jnp.concatenate([hidden_grad, alone], axis=0), kept)

    total = jnp.zeros((2 * prop_hidden, saved_ref.shape[0]), F32)
    total = lax.fori_loop(0, parts, accumulate, total)
    grad_ref[...] = total


def backward(me, stats, dense, saved, prop_out, marks, cap):
    key, hot, *masks = marks
    parts, slots = key.shape
    width = dense.shape[2]
    prop_hidden = prop_out.shape[1]
    vmem = pl.BlockSpec(memory_space=pltpu.VMEM)
    return pl.pallas_call(
        functools.partial(backward_kernel, cap),
        out_shape=(
            jax.ShapeDtypeStruct((1, RAY_DEV), F32),
            jax.ShapeDtypeStruct((2 * prop_hidden, saved.shape[0]), F32),
        ),
        in_specs=[pl.BlockSpec(memory_space=pltpu.SMEM)] + [vmem] * (6 + len(masks)),
        out_specs=(vmem, vmem),
        scratch_shapes=[pltpu.VMEM((parts, width), F32)]
        + ([] if masks else [pltpu.VMEM((slots, parts), F32)]),
        compiler_params=pltpu.CompilerParams(vmem_limit_bytes=(12 if masks else 48) * 1024 * 1024),
        name="backward",
    )(me, stats, key, hot, dense, saved, prop_out, *masks)


def sum_replicas(x):
    count = lax.axis_size("rep")
    if count != 4:
        return lax.psum(x, "rep")
    other = [lax.ppermute(x, "rep", [(i, i ^ s) for i in range(count)]) for s in (1, 2, 3)]
    return (x + other[0]) + (other[1] + other[2])


def on_device(
    feature_grid,
    fine_in,
    fine_mid,
    fine_out,
    prop_in,
    prop_out,
    sample_cells,
    sample_geometry,
    slot_ray,
    slot_rank,
    bucket_count,
):
    parts = lax.axis_size("dom")
    cap = slot_ray.shape[3]
    features = feature_grid.shape[1]
    prop_hidden = prop_in.shape[1]
    outgoing = pack(
        sample_geometry[:, 0, 0], slot_ray[0, 0], slot_rank[0, 0], bucket_count.reshape(-1)
    )
    arrived = lax.all_to_all(outgoing, "dom", split_axis=0, concat_axis=0, tiled=True)
    saved, dense, summary = forward(
        sample_cells.reshape(-1), feature_grid[0], arrived,
        fine_in[0].T, prop_in[0], fine_mid[0], fine_out, prop_out, cap,
    )
    stats = lax.all_to_all(summary, "dom", split_axis=0, concat_axis=0, tiled=True)
    me = lax.axis_index("dom").reshape(1).astype(jnp.int32)
    marks = slot_marks(me, arrived, cap)
    ray_loss, grads = backward(me, stats, dense, saved, prop_out, marks, cap)
    sums = sum_replicas(grads)
    in_sum = sums[:prop_hidden, :features]
    out_sum = sums[prop_hidden, features:]
    return (ray_loss.reshape(1, 1, -1), in_sum[None], out_sum[None])


def solution(mesh):
    return jax.shard_map(
        on_device,
        mesh=mesh,
        in_specs=(
            P("dom", None, None),
            P("dom", None, None),
            P("dom", None, None, None),
            P("dom", None),
            P("dom", None, None),
            P("dom", None),
            P("dom", "rep", None, None),
            P(None, "dom", "rep", None, None),
            P("dom", "rep", None, None),
            P("dom", "rep", None, None),
            P("dom", "rep", None),
        ),
        out_specs=(P("dom", "rep", None), P("dom", None, None), P("dom", None)),
        check_vma=False,
    )
```

```python
import functools

import jax
import jax.numpy as jnp
from jax import lax
from jax.experimental import pallas as pl
from jax.experimental.pallas import tpu as pltpu
from jax.sharding import PartitionSpec as P

GR = 32
RAY_DEV = 256
LANES = 128
BLOCK = 256
CHUNKS = 8
TABLE_PAD = 8
NET_SPLIT = 4
DEPTH = 4

distill_weight = 50.0
F32 = jnp.float32
BF16 = jnp.bfloat16


def dot(a, b):
    return lax.dot_general(a, b, (((1,), (0,)), ((), ())), preferred_element_type=F32)


def dot_nt(a, b):
    return lax.dot_general(a, b, (((1,), (1,)), ((), ())), preferred_element_type=F32)


def split3(x):
    hi = x.astype(BF16)
    rest = x - hi.astype(F32)
    mid = rest.astype(BF16)
    low = (rest - mid.astype(F32)).astype(BF16)
    return [hi, mid, low]


def in_hbm(x):
    return pltpu.with_memory_space_constraint(x, pltpu.HBM)


def stack_rows(arrays, row):
    return jnp.concatenate([x[row : row + 1] for x in arrays], axis=0)


def flatten_slots(x, cap):
    parts = x.shape[0]
    per = LANES // cap
    lane = lax.broadcasted_iota(jnp.int32, (1, LANES), 1)
    wide = jnp.concatenate([x] * per, axis=1)
    out = []
    for first in range(0, parts, per):
        row = wide[first : first + 1]
        for k in range(1, per):
            row = jnp.where(lane // cap == k, wide[first + k : first + k + 1], row)
        out.append(row)
    return jnp.concatenate(out, axis=1)


def pack_kernel(geometry_ref, ray_ref, rank_ref, count_ref, out_ref):
    parts, cap = ray_ref.shape
    sub = lax.broadcasted_iota(jnp.int32, (parts, cap), 0)
    count = jnp.zeros((parts, cap), jnp.int32)
    for p in range(parts):
        count = jnp.where(sub == p, count_ref[p], count)
    live = lax.broadcasted_iota(jnp.int32, (parts, cap), 1) < count
    ray = jnp.where(live, ray_ref[...], -1).astype(F32)
    marks = jnp.concatenate(
        [flatten_slots(ray, cap), flatten_slots(rank_ref[...].astype(F32), cap)], axis=1
    )
    quarter = marks.shape[1] // 4
    g = [geometry_ref[j].astype(F32) for j in range(4)]
    for p in range(parts):
        rows = [
            jnp.concatenate([x[p : p + 1], marks[:, j * quarter : (j + 1) * quarter]], axis=1)
            for j, x in enumerate(g)
        ]
        out_ref[p] = jnp.concatenate(rows, axis=0).astype(BF16)


def pack(geometry, ray, rank, count):
    parts, width = geometry.shape[1:]
    vmem = pl.BlockSpec(memory_space=pltpu.VMEM)
    return pl.pallas_call(
        pack_kernel,
        out_shape=jax.ShapeDtypeStruct((parts, 4, width + ray.size // 2), BF16),
        in_specs=[vmem] * 3 + [pl.BlockSpec(memory_space=pltpu.SMEM)],
        out_specs=vmem,
        name="pack",
    )(geometry, ray, rank, count)


def marks_kernel(cap, me_ref, arrived_ref, key_ref, hot_ref, *mask_ref):
    me = me_ref[0]
    parts = arrived_ref.shape[0]
    slots = parts * cap
    width = arrived_ref.shape[2] - slots // 2
    ray, rank = [], []
    for q in range(parts):
        marks = arrived_ref[q, :, width:].astype(F32)
        ray.append(jnp.concatenate([marks[0:1], marks[1:2]], axis=1))
        rank.append(jnp.concatenate([marks[2:3], marks[3:4]], axis=1))
    key = jnp.concatenate(ray, axis=0) * (2.0 * parts) + jnp.concatenate(rank, axis=0)
    key_ref[...] = key
    key_t = key.T
    mine = lax.broadcasted_iota(jnp.int32, (slots, parts), 1) == me
    key_col = jnp.sum(jnp.where(mine, key_t, 0.0), axis=1, keepdims=True)
    ray = lax.broadcasted_iota(jnp.int32, (slots, RAY_DEV), 1).astype(F32)
    rest = key_col - ray * (2.0 * parts)
    hot_ref[...] = ((rest >= 0) & (rest < 2 * parts)).astype(BF16)
    if mask_ref:
        for q in range(parts):
            gap = key[q : q + 1] - key_t[:, q : q + 1]
            mask_ref[0][q] = ((gap > 0) & (gap < parts)).astype(BF16)


def slot_marks(me, arrived, cap):
    parts = arrived.shape[0]
    slots = parts * cap
    vmem = pl.BlockSpec(memory_space=pltpu.VMEM)
    shapes = [
        jax.ShapeDtypeStruct((parts, slots), F32),
        jax.ShapeDtypeStruct((slots, RAY_DEV), BF16),
    ]
    if slots <= 256:
        shapes.append(jax.ShapeDtypeStruct((parts, slots, slots), BF16))
    return pl.pallas_call(
        functools.partial(marks_kernel, cap),
        out_shape=tuple(shapes),
        in_specs=[pl.BlockSpec(memory_space=pltpu.SMEM), vmem],
        out_specs=(vmem,) * len(shapes),
        cost_estimate=pl.CostEstimate(
            flops=parts * slots * slots * 8, bytes_accessed=4 << 20, transcendentals=0
        ),
        compiler_params=pltpu.CompilerParams(vmem_limit_bytes=12 * 1024 * 1024),
        name="slot_marks",
    )(me, arrived)


def lane_fold(x, cap):
    shift = LANES // 2
    while shift >= cap:
        x = x + pltpu.roll(x, shift, 1)
        shift //= 2
    return x


def running(pieces, cap):
    lane = lax.broadcasted_iota(jnp.int32, pieces[0].shape, 1)
    carry = jnp.zeros_like(pieces[0])
    out = []
    for x in pieces:
        y = x
        shift = cap
        while shift < LANES:
            y = y + jnp.where(lane >= shift, pltpu.roll(y, shift, 1), 0.0)
            shift *= 2
        out.append(carry + y)
        carry = carry + lane_fold(x, cap)
    return out, carry


def trailing(pieces, cap):
    lane = lax.broadcasted_iota(jnp.int32, pieces[0].shape, 1)
    carry = jnp.zeros_like(pieces[0])
    out = []
    for x in reversed(pieces):
        y = x
        shift = cap
        while shift < LANES:
            y = y + jnp.where(lane < LANES - shift, pltpu.roll(y, LANES - shift, 1), 0.0)
            shift *= 2
        out.append(carry + y)
        carry = carry + lane_fold(x, cap)
    return out[::-1]


def softplus(x):
    return jnp.maximum(x, 0.0) + jnp.log1p(jnp.exp(-jnp.abs(x)))


def pieces_of(x):
    return [x[:, v * LANES : (v + 1) * LANES] for v in range(x.shape[1] // LANES)]


def fetch_grid(grid_hbm, grid_ref, sem, c):
    chunk = grid_ref.shape[1] // CHUNKS
    at = pl.ds(c * chunk, chunk)
    return pltpu.make_async_copy(grid_hbm.at[:, at], grid_ref.at[:, at], sem.at[c])


def build_table(grid_hbm, grid_ref, sem, table):
    features, cells = grid_ref.shape
    plane = GR * GR
    span = 2 * BLOCK
    chunk = cells // CHUNKS
    upper = lax.broadcasted_iota(jnp.int32, (span, LANES), 1) // features % 2 == 1

    def build(i, carry, top):
        c0 = pl.multiple_of(top - (i + 1) * span, span)
        base = grid_ref[:, pl.ds(c0, span)]
        across = grid_ref[:, pl.ds(c0 + plane, span)]
        rows = jnp.concatenate([base, base, across, across], axis=0).T.astype(F32)
        table[pl.ds(c0 + TABLE_PAD, span), :] = jnp.where(
            upper, jnp.concatenate([rows[GR:], carry], axis=0), rows
        )
        return rows[:GR]

    carry = jnp.zeros((GR, LANES), F32)
    for c in reversed(range(CHUNKS)):
        fetch_grid(grid_hbm, grid_ref, sem, c).wait()
        top = cells - plane if c == CHUNKS - 1 else (c + 1) * chunk
        body = functools.partial(build, top=top)
        carry = lax.fori_loop(0, (top - c * chunk) // span, body, carry, unroll=True)


def forward_kernel(
    cap, idx_hbm, grid_hbm, arrived_ref, fine_in_ref, prop_in_ref, mid_ref, fine_out_ref,
    prop_out_ref, saved_ref, dense_ref, summary_ref,
    idx_ref, idx_sem, table, grid_ref, grid_sem, rows, feats, hidden_rows, weights, spacing, first, head, fine_logit, prop_logit,
):
    step = pl.program_id(0)
    parts = arrived_ref.shape[0]
    width = idx_ref.shape[0] // parts
    blocks = width // BLOCK
    features = prop_in_ref.shape[1]
    hidden = mid_ref.shape[1]
    prop_hidden = prop_in_ref.shape[0]

    def gather(row, block, pair):
        start = row * width
        sub = lax.broadcasted_iota(jnp.int32, (8, LANES), 0)
        for u in range(0, BLOCK, 4):
            merged = None
            for e in range(4):
                at = pl.ds(block * BLOCK + u + e, idx_ref.shape[0] - width + 1)
                k = idx_ref.at[at][start]
                loaded = table[pl.ds(k + (TABLE_PAD - 2 * e), 8), :]
                merged = loaded if merged is None else jnp.where(sub < 2 * e, merged, loaded)
            pair[2 * u : 2 * u + 8, :] = merged

    def interpolate(block, pair, slot):
        near = pair[pl.ds(0, BLOCK, stride=2), :].astype(BF16)
        far = pair[pl.ds(1, BLOCK, stride=2), :].astype(BF16)
        t = jnp.concatenate([near, far], axis=1).T.astype(F32)
        at = slice(block * BLOCK, (block + 1) * BLOCK)
        total = jnp.zeros((features, BLOCK), F32)
        for corner in range(8):
            place = (corner % 2) * 4 + corner // 2
            w = weights[corner, pl.ds(step, 1), at]
            total = total + t[place * features : (place + 1) * features] * w
        feats[slot, :, at] = total.astype(BF16)

    layers = mid_ref.shape[0]

    def stage(row, slot, layer, lanes):
        if layer == 0:
            feat = feats[slot, :, lanes]
            saved_ref[:features, lanes] = feat
            both = jnp.maximum(dot(first[...], feat), 0.0).astype(BF16)
            hidden_rows[:, lanes] = both
            saved_ref[features:, lanes] = both[hidden:]
        elif layer <= layers:
            h = dot(mid_ref[layer - 1], hidden_rows[:hidden, lanes])
            hidden_rows[:hidden, lanes] = jnp.maximum(h, 0.0).astype(BF16)
        else:
            logits = dot(head[...], hidden_rows[:, lanes])
            fine_logit[pl.ds(row, 1), lanes] = logits[0:1]
            prop_logit[pl.ds(row, 1), lanes] = logits[1:2]

    def stages(row, slot):
        parts_of = NET_SPLIT
        size = width // parts_of
        return [
            functools.partial(stage, row, slot, layer, slice(h * size, (h + 1) * size))
            for layer in range(layers + 2)
            for h in range(parts_of)
        ]

    @pl.when(step == 0)
    def _():
        fetch_idx = pltpu.make_async_copy(idx_hbm, idx_ref, idx_sem)
        fetch_idx.start()
        for c in reversed(range(CHUNKS)):
            fetch_grid(grid_hbm, grid_ref, grid_sem, c).start()
        feats[...] = jnp.zeros(feats.shape, BF16)
        whole = [arrived_ref[q, :, :width].astype(F32) for q in range(parts)]
        g = [stack_rows(whole, j) for j in range(4)]
        spacing[...] = g[3]
        first[:hidden, :] = fine_in_ref[...].astype(F32).T.astype(BF16)
        first[hidden:, :] = prop_in_ref[...]
        zero_f = jnp.zeros((1, prop_hidden), F32)
        zero_p = jnp.zeros((1, hidden), F32)
        top = jnp.concatenate([fine_out_ref[...].astype(F32), zero_f], axis=1)
        low = jnp.concatenate([zero_p, prop_out_ref[...].astype(F32)], axis=1)
        rest = jnp.zeros((6, hidden + prop_hidden), F32)
        head[...] = jnp.concatenate([top, low, rest], axis=0).astype(BF16)
        for corner in range(8):
            bits = (corner // 4, corner // 2 % 2, corner % 2)
            w = [x if bit else 1.0 - x for x, bit in zip(g, bits)]
            weights[corner] = w[0] * w[1] * w[2]
        build_table(grid_hbm, grid_ref, grid_sem, table)
        fetch_idx.wait()
        gather(0, 0, rows.at[0])

    @pl.when(step < parts)
    def _():
        todo = stages(jnp.maximum(step - 1, 0), (step + 1) % 2)
        for j in range(blocks):
            for run in todo[j * len(todo) // blocks : (j + 1) * len(todo) // blocks]:
                run()
            interpolate(j, rows.at[j % DEPTH], step % 2)
            ahead = rows.at[(j + 1) % DEPTH]
            if j + 1 < blocks:
                gather(step, j + 1, ahead)
            else:
                gather(jnp.minimum(step + 1, parts - 1), 0, ahead)

    @pl.when(step == parts)
    def _():
        for run in stages(parts - 1, (parts - 1) % 2):
            run()
        space = pieces_of(spacing[...])
        results = []
        for k, ref in enumerate((prop_logit, fine_logit)):
            logit = pieces_of(ref[...])
            optical = [softplus(x) * s for x, s in zip(logit, space)]
            depth, whole = running(optical, cap)
            early = [jnp.exp(o - d) for o, d in zip(optical, depth)]
            absorb = [e - jnp.exp(-d) for e, d in zip(early, depth)]
            results.append((absorb, whole))
            if k == 0:
                slope = [s * jax.nn.sigmoid(x) for x, s in zip(logit, space)]
                dense_ref[0] = jnp.concatenate(early, axis=1)
                dense_ref[3] = jnp.concatenate(slope, axis=1)
        (a, log_prop), (b, log_fine) = results
        dense_ref[1] = jnp.concatenate(a, axis=1)
        dense_ref[2] = jnp.concatenate(b, axis=1)
        sums = [lane_fold(sum(x * y for x, y in zip(s, t)), cap) for s, t in ((a, a), (a, b), (b, b))]
        stats = [-log_prop, -log_fine] + sums
        per = LANES // cap
        group = lax.broadcasted_iota(jnp.int32, stats[0].shape, 1) // cap
        slabs = []
        for s in range(-(-len(stats) // per)):
            slab = jnp.zeros_like(stats[0])
            for k, x in enumerate(stats[s * per : (s + 1) * per]):
                slab = jnp.where(group == k, x, slab)
            slabs.append(slab)
        summary = jnp.concatenate(slabs, axis=1)
        for p in range(parts):
            summary_ref[p] = summary


def forward(cells, grid, arrived, fine_in, prop_in, mid, fine_out, prop_out, cap):
    parts = arrived.shape[0]
    width = cells.shape[0] // parts
    features, total = grid.shape
    hidden = mid.shape[1]
    prop_hidden = prop_in.shape[0]
    kept = features + prop_hidden
    stat_lanes = -(-5 // (LANES // cap)) * LANES
    whole = lambda shape: pl.BlockSpec(shape, lambda q: (0,) * len(shape))
    small = (arrived, fine_in, prop_in, mid, fine_out, prop_out)
    return pl.pallas_call(
        functools.partial(forward_kernel, cap),
        grid=(parts + 1,),
        out_shape=(
            jax.ShapeDtypeStruct((kept, parts * width), BF16),
            jax.ShapeDtypeStruct((4, parts, width), F32),
            jax.ShapeDtypeStruct((parts, parts, stat_lanes), F32),
        ),
        in_specs=[
            pl.BlockSpec(memory_space=pltpu.HBM),
            pl.BlockSpec(memory_space=pltpu.HBM),
        ]
        + [whole(x.shape) for x in small],
        out_specs=(
            pl.BlockSpec((kept, width), lambda q: (0, jnp.maximum(q - 1, 0))),
            whole((4, parts, width)),
            whole((parts, parts, stat_lanes)),
        ),
        scratch_shapes=[
            pltpu.SMEM(cells.shape, jnp.int32),
            pltpu.SemaphoreType.DMA,
            pltpu.VMEM((total + 2 * TABLE_PAD, LANES), F32),
            pltpu.VMEM((features, total), BF16),
            pltpu.SemaphoreType.DMA((CHUNKS,)),
            pltpu.VMEM((DEPTH, 2 * BLOCK, LANES), F32),
            pltpu.VMEM((2, features, width), BF16),
            pltpu.VMEM((hidden + prop_hidden, width), BF16),
            pltpu.VMEM((8, parts, width), F32),
            pltpu.VMEM((parts, width), F32),
            pltpu.VMEM((hidden + prop_hidden, features), BF16),
            pltpu.VMEM((8, hidden + prop_hidden), BF16),
            pltpu.VMEM((parts, width), F32),
            pltpu.VMEM((parts, width), F32),
        ],
        compiler_params=pltpu.CompilerParams(vmem_limit_bytes=(32 + parts // 2) * 1024 * 1024),
        name="forward",
    )(in_hbm(cells), in_hbm(grid), arrived, *[in_hbm(x) for x in small[1:]])


def backward_kernel(
    cap, me_ref, stats_ref, key_ref, hot_ref, dense_ref, saved_ref, prop_out_ref, *rest,
):
    masks, (loss_ref, grad_ref, slope_ref, *keys_t) = rest[:-3], rest[-3:]
    if stats_ref.shape[0] * cap > 256:
        masks, (loss_ref, grad_ref, slope_ref, *keys_t) = (), rest
    me = me_ref[0]
    parts = stats_ref.shape[0]
    slots = key_ref.shape[1]
    per = LANES // cap
    width = dense_ref.shape[2]
    prop_hidden = prop_out_ref.shape[1]
    key = key_ref[...]
    live = (key >= 0).astype(F32)
    sub = lax.broadcasted_iota(jnp.int32, (parts, slots), 0)
    if not masks:
        keys_t[0][...] = key.T

    def mask_of(q):
        lane = lax.broadcasted_iota(jnp.int32, (slots, parts), 1)
        col = jnp.sum(jnp.where(lane == q, keys_t[0][...], 0.0), axis=1, keepdims=True)
        row = jnp.sum(jnp.where(sub == q, key, 0.0), axis=0, keepdims=True)
        gap = row - col
        return ((gap > 0) & (gap < parts)).astype(BF16)

    def over(body, init):
        if masks:
            for q in range(parts):
                init = body(q, init)
            return init
        return lax.fori_loop(0, parts, body, init)

    group = lax.broadcasted_iota(jnp.int32, (parts, LANES), 1) // cap

    def flat(j):
        slab = slice((j // per) * LANES, (j // per + 1) * LANES)
        out = []
        for half in range(slots // LANES):
            x = jnp.zeros((parts, LANES), F32)
            for k in range(per):
                piece = stats_ref[half * per + k, :, slab]
                shift = ((k - j % per) * cap) % LANES
                x = jnp.where(group == k, pltpu.roll(piece, shift, 1) if shift else piece, x)
            out.append(x)
        return jnp.concatenate(out, axis=1)

    log_prop, log_fine, sum_aa, sum_ab, sum_bb = [flat(j) for j in range(5)]
    terms = split3(log_prop * live) + split3(log_fine * live)
    stacked = jnp.concatenate(terms, axis=0)

    def lead(q, acc):
        m = masks[0][q] if masks else mask_of(q)
        y = dot(stacked, m)
        return tuple(
            jnp.where(sub == q, y[k * parts : (k + 1) * parts], x) for k, x in enumerate(acc)
        )

    zero = jnp.zeros((parts, slots), F32)
    lead_sums = over(lead, (zero,) * 6)
    entry_prop = jnp.exp(lead_sums[0] + lead_sums[1] + lead_sums[2]) * live
    entry_fine = jnp.exp(lead_sums[3] + lead_sums[4] + lead_sums[5]) * live
    seg_loss = (
        entry_prop * entry_prop * sum_aa
        - 2.0 * entry_prop * entry_fine * sum_ab
        + entry_fine * entry_fine * sum_bb
    )
    slot_grad = distill_weight * (entry_prop * sum_aa - entry_fine * sum_ab) * entry_prop
    mine = pl.ds(pl.multiple_of(me * cap, cap), cap)
    grads = jnp.concatenate(split3(slot_grad), axis=0)
    sub_cap = lax.broadcasted_iota(jnp.int32, (parts, cap), 0)

    def tail(q, acc):
        if masks:
            m = masks[0][q, mine, :]
            y = dot_nt(grads, m)
        else:
            y = dot_nt(grads, mask_of(q))
            y = own_lanes(y)
        y = y[:parts] + y[parts : 2 * parts] + y[2 * parts :]
        return jnp.where(sub_cap == q, y, acc)

    def own_lanes(x):
        out = x[:, :cap]
        for p in range(1, parts):
            out = jnp.where(me == p, x[:, p * cap : (p + 1) * cap], out)
        return out

    carried = over(tail, jnp.zeros((parts, cap), F32)) * own_lanes(live)
    coef_aa = own_lanes(0.5 * distill_weight * entry_prop * entry_prop)
    coef_ab = own_lanes(-distill_weight * entry_prop * entry_fine)

    spread = dot(jnp.concatenate(split3(seg_loss), axis=0), hot_ref[...])
    spread = spread[:parts] + spread[parts : 2 * parts] + spread[2 * parts :]
    sub_ray = lax.broadcasted_iota(jnp.int32, (parts, RAY_DEV), 0)
    loss_ref[...] = (0.5 * distill_weight) * jnp.sum(
        jnp.where(sub_ray == me, spread, 0.0), axis=0, keepdims=True
    )

    tile = lambda x: jnp.concatenate([x] * per, axis=1)
    c_aa, c_ab, c_log = tile(2.0 * coef_aa), tile(coef_ab), tile(carried)
    early, a, b, slope = [pieces_of(dense_ref[k]) for k in range(4)]
    d_absorb = [c_aa * x + c_ab * y for x, y in zip(a, b)]
    back = trailing([d * x for d, x in zip(d_absorb, a)], cap)
    logit_grad = [
        ((d * e - c_log - r) * s).astype(BF16).astype(F32)
        for d, e, r, s in zip(d_absorb, early, back, slope)
    ]
    slope_ref[...] = jnp.concatenate(logit_grad, axis=1)
    features = saved_ref.shape[0] - prop_hidden
    wide = jnp.broadcast_to(prop_out_ref[...].astype(F32), (prop_hidden, prop_hidden))
    same = lax.broadcasted_iota(jnp.int32, wide.shape, 0) == lax.broadcasted_iota(
        jnp.int32, wide.shape, 1
    )
    out_col = jnp.sum(jnp.where(same, wide, 0.0), axis=1, keepdims=True)
    first_row = lax.broadcasted_iota(jnp.int32, (prop_hidden, width), 0) == 0

    def accumulate(q, total):
        at = pl.ds(pl.multiple_of(q * width, width), width)
        row = slope_ref[pl.ds(q, 1), :]
        kept = saved_ref[:, at]
        hidden_grad = jnp.where(kept[features:].astype(F32) > 0, out_col * row, 0.0).astype(BF16)
        alone = jnp.where(first_row, row, 0.0).astype(BF16)
        return total + dot_nt(jnp.concatenate([hidden_grad, alone], axis=0), kept)

    total = jnp.zeros((2 * prop_hidden, saved_ref.shape[0]), F32)
    total = lax.fori_loop(0, parts, accumulate, total)
    grad_ref[...] = total


def backward(me, stats, dense, saved, prop_out, marks, cap):
    key, hot, *masks = marks
    parts, slots = key.shape
    width = dense.shape[2]
    prop_hidden = prop_out.shape[1]
    vmem = pl.BlockSpec(memory_space=pltpu.VMEM)
    return pl.pallas_call(
        functools.partial(backward_kernel, cap),
        out_shape=(
            jax.ShapeDtypeStruct((1, RAY_DEV), F32),
            jax.ShapeDtypeStruct((2 * prop_hidden, saved.shape[0]), F32),
        ),
        in_specs=[pl.BlockSpec(memory_space=pltpu.SMEM)] + [vmem] * (6 + len(masks)),
        out_specs=(vmem, vmem),
        scratch_shapes=[pltpu.VMEM((parts, width), F32)]
        + ([] if masks else [pltpu.VMEM((slots, parts), F32)]),
        compiler_params=pltpu.CompilerParams(vmem_limit_bytes=(12 if masks else 48) * 1024 * 1024),
        name="backward",
    )(me, stats, key, hot, dense, saved, prop_out, *masks)


def sum_replicas(x):
    count = lax.axis_size("rep")
    if count != 4:
        return lax.psum(x, "rep")
    other = [lax.ppermute(x, "rep", [(i, i ^ s) for i in range(count)]) for s in (1, 2, 3)]
    return (x + other[0]) + (other[1] + other[2])


def on_device(
    feature_grid,
    fine_in,
    fine_mid,
    fine_out,
    prop_in,
    prop_out,
    sample_cells,
    sample_geometry,
    slot_ray,
    slot_rank,
    bucket_count,
):
    parts = lax.axis_size("dom")
    cap = slot_ray.shape[3]
    features = feature_grid.shape[1]
    prop_hidden = prop_in.shape[1]
    outgoing = pack(
        sample_geometry[:, 0, 0], slot_ray[0, 0], slot_rank[0, 0], bucket_count.reshape(-1)
    )
    arrived = lax.all_to_all(outgoing, "dom", split_axis=0, concat_axis=0, tiled=True)
    saved, dense, summary = forward(
        sample_cells.reshape(-1), feature_grid[0], arrived,
        fine_in[0].T, prop_in[0], fine_mid[0], fine_out, prop_out, cap,
    )
    stats = lax.all_to_all(summary, "dom", split_axis=0, concat_axis=0, tiled=True)
    me = lax.axis_index("dom").reshape(1).astype(jnp.int32)
    marks = slot_marks(me, arrived, cap)
    ray_loss, grads = backward(me, stats, dense, saved, prop_out, marks, cap)
    sums = sum_replicas(grads)
    in_sum = sums[:prop_hidden, :features]
    out_sum = sums[prop_hidden, features:]
    return (ray_loss.reshape(1, 1, -1), in_sum[None], out_sum[None])


def solution(mesh):
    return jax.shard_map(
        on_device,
        mesh=mesh,
        in_specs=(
            P("dom", None, None),
            P("dom", None, None),
            P("dom", None, None, None),
            P("dom", None),
            P("dom", None, None),
            P("dom", None),
            P("dom", "rep", None, None),
            P(None, "dom", "rep", None, None),
            P("dom", "rep", None, None),
            P("dom", "rep", None, None),
            P("dom", "rep", None),
        ),
        out_specs=(P("dom", "rep", None), P("dom", None, None), P("dom", None)),
        check_vma=False,
    )
```

```python
import functools

import jax
import jax.numpy as jnp
from jax import lax
from jax.experimental import pallas as pl
from jax.experimental.pallas import tpu as pltpu
from jax.sharding import PartitionSpec as P

GR = 32
RAY_DEV = 256
LANES = 128
BLOCK = 256
CHUNKS = 8
TABLE_PAD = 8
NET_SPLIT = 4
DEPTH = 4

distill_weight = 50.0
F32 = jnp.float32
BF16 = jnp.bfloat16


def dot(a, b):
    return lax.dot_general(a, b, (((1,), (0,)), ((), ())), preferred_element_type=F32)


def dot_nt(a, b):
    return lax.dot_general(a, b, (((1,), (1,)), ((), ())), preferred_element_type=F32)


def split3(x):
    hi = x.astype(BF16)
    rest = x - hi.astype(F32)
    mid = rest.astype(BF16)
    low = (rest - mid.astype(F32)).astype(BF16)
    return [hi, mid, low]


def in_hbm(x):
    return pltpu.with_memory_space_constraint(x, pltpu.HBM)


def stack_rows(arrays, row):
    return jnp.concatenate([x[row : row + 1] for x in arrays], axis=0)


def flatten_slots(x, cap):
    parts = x.shape[0]
    per = LANES // cap
    lane = lax.broadcasted_iota(jnp.int32, (1, LANES), 1)
    wide = jnp.concatenate([x] * per, axis=1)
    out = []
    for first in range(0, parts, per):
        row = wide[first : first + 1]
        for k in range(1, per):
            row = jnp.where(lane // cap == k, wide[first + k : first + k + 1], row)
        out.append(row)
    return jnp.concatenate(out, axis=1)


def pack_kernel(geometry_ref, ray_ref, rank_ref, count_ref, out_ref):
    parts, cap = ray_ref.shape
    sub = lax.broadcasted_iota(jnp.int32, (parts, cap), 0)
    count = jnp.zeros((parts, cap), jnp.int32)
    for p in range(parts):
        count = jnp.where(sub == p, count_ref[p], count)
    live = lax.broadcasted_iota(jnp.int32, (parts, cap), 1) < count
    ray = jnp.where(live, ray_ref[...], -1).astype(F32)
    marks = jnp.concatenate(
        [flatten_slots(ray, cap), flatten_slots(rank_ref[...].astype(F32), cap)], axis=1
    )
    quarter = marks.shape[1] // 4
    g = [geometry_ref[j].astype(F32) for j in range(4)]
    for p in range(parts):
        rows = [
            jnp.concatenate([x[p : p + 1], marks[:, j * quarter : (j + 1) * quarter]], axis=1)
            for j, x in enumerate(g)
        ]
        out_ref[p] = jnp.concatenate(rows, axis=0).astype(BF16)


def pack(geometry, ray, rank, count):
    parts, width = geometry.shape[1:]
    vmem = pl.BlockSpec(memory_space=pltpu.VMEM)
    return pl.pallas_call(
        pack_kernel,
        out_shape=jax.ShapeDtypeStruct((parts, 4, width + ray.size // 2), BF16),
        in_specs=[vmem] * 3 + [pl.BlockSpec(memory_space=pltpu.SMEM)],
        out_specs=vmem,
        name="pack",
    )(geometry, ray, rank, count)


def marks_kernel(cap, me_ref, arrived_ref, key_ref, hot_ref, *mask_ref):
    me = me_ref[0]
    parts = arrived_ref.shape[0]
    slots = parts * cap
    width = arrived_ref.shape[2] - slots // 2
    ray, rank = [], []
    for q in range(parts):
        marks = arrived_ref[q, :, width:].astype(F32)
        ray.append(jnp.concatenate([marks[0:1], marks[1:2]], axis=1))
        rank.append(jnp.concatenate([marks[2:3], marks[3:4]], axis=1))
    key = jnp.concatenate(ray, axis=0) * (2.0 * parts) + jnp.concatenate(rank, axis=0)
    key_ref[...] = key
    key_t = key.T
    mine = lax.broadcasted_iota(jnp.int32, (slots, parts), 1) == me
    key_col = jnp.sum(jnp.where(mine, key_t, 0.0), axis=1, keepdims=True)
    ray = lax.broadcasted_iota(jnp.int32, (slots, RAY_DEV), 1).astype(F32)
    rest = key_col - ray * (2.0 * parts)
    hot_ref[...] = ((rest >= 0) & (rest < 2 * parts)).astype(BF16)
    if mask_ref:
        for q in range(parts):
            gap = key[q : q + 1] - key_t[:, q : q + 1]
            mask_ref[0][q] = ((gap > 0) & (gap < parts)).astype(BF16)


def slot_marks(me, arrived, cap):
    parts = arrived.shape[0]
    slots = parts * cap
    vmem = pl.BlockSpec(memory_space=pltpu.VMEM)
    shapes = [
        jax.ShapeDtypeStruct((parts, slots), F32),
        jax.ShapeDtypeStruct((slots, RAY_DEV), BF16),
    ]
    if slots <= 256:
        shapes.append(jax.ShapeDtypeStruct((parts, slots, slots), BF16))
    return pl.pallas_call(
        functools.partial(marks_kernel, cap),
        out_shape=tuple(shapes),
        in_specs=[pl.BlockSpec(memory_space=pltpu.SMEM), vmem],
        out_specs=(vmem,) * len(shapes),
        cost_estimate=pl.CostEstimate(
            flops=parts * slots * slots * 8, bytes_accessed=4 << 20, transcendentals=0
        ),
        compiler_params=pltpu.CompilerParams(vmem_limit_bytes=12 * 1024 * 1024),
        name="slot_marks",
    )(me, arrived)


def lane_fold(x, cap):
    shift = LANES // 2
    while shift >= cap:
        x = x + pltpu.roll(x, shift, 1)
        shift //= 2
    return x


def running(pieces, cap):
    lane = lax.broadcasted_iota(jnp.int32, pieces[0].shape, 1)
    carry = jnp.zeros_like(pieces[0])
    out = []
    for x in pieces:
        y = x
        shift = cap
        while shift < LANES:
            y = y + jnp.where(lane >= shift, pltpu.roll(y, shift, 1), 0.0)
            shift *= 2
        out.append(carry + y)
        carry = carry + lane_fold(x, cap)
    return out, carry


def trailing(pieces, cap):
    lane = lax.broadcasted_iota(jnp.int32, pieces[0].shape, 1)
    carry = jnp.zeros_like(pieces[0])
    out = []
    for x in reversed(pieces):
        y = x
        shift = cap
        while shift < LANES:
            y = y + jnp.where(lane < LANES - shift, pltpu.roll(y, LANES - shift, 1), 0.0)
            shift *= 2
        out.append(carry + y)
        carry = carry + lane_fold(x, cap)
    return out[::-1]


def softplus(x):
    return jnp.maximum(x, 0.0) + jnp.log1p(jnp.exp(-jnp.abs(x)))


def pieces_of(x):
    return [x[:, v * LANES : (v + 1) * LANES] for v in range(x.shape[1] // LANES)]


def fetch_grid(grid_hbm, grid_ref, sem, c):
    chunk = grid_ref.shape[1] // CHUNKS
    at = pl.ds(c * chunk, chunk)
    return pltpu.make_async_copy(grid_hbm.at[:, at], grid_ref.at[:, at], sem.at[c])


def build_table(grid_hbm, grid_ref, sem, table):
    features, cells = grid_ref.shape
    plane = GR * GR
    span = 2 * BLOCK
    chunk = cells // CHUNKS
    upper = lax.broadcasted_iota(jnp.int32, (span, LANES), 1) // features % 2 == 1

    def build(i, carry, top):
        c0 = pl.multiple_of(top - (i + 1) * span, span)
        base = grid_ref[:, pl.ds(c0, span)]
        across = grid_ref[:, pl.ds(c0 + plane, span)]
        rows = jnp.concatenate([base, base, across, across], axis=0).T.astype(F32)
        table[pl.ds(c0 + TABLE_PAD, span), :] = jnp.where(
            upper, jnp.concatenate([rows[GR:], carry], axis=0), rows
        )
        return rows[:GR]

    carry = jnp.zeros((GR, LANES), F32)
    for c in reversed(range(CHUNKS)):
        fetch_grid(grid_hbm, grid_ref, sem, c).wait()
        top = cells - plane if c == CHUNKS - 1 else (c + 1) * chunk
        body = functools.partial(build, top=top)
        carry = lax.fori_loop(0, (top - c * chunk) // span, body, carry, unroll=True)


def forward_kernel(
    cap, idx_hbm, grid_hbm, arrived_ref, fine_in_ref, prop_in_ref, mid_ref, fine_out_ref,
    prop_out_ref, saved_ref, dense_ref, summary_ref,
    idx_ref, idx_sem, table, grid_ref, grid_sem, rows, feats, hidden_rows, weights, spacing, first, head, fine_logit, prop_logit,
):
    parts = arrived_ref.shape[0]
    width = idx_ref.shape[0] // parts
    blocks = width // BLOCK
    features = prop_in_ref.shape[1]
    hidden = mid_ref.shape[1]
    prop_hidden = prop_in_ref.shape[0]

    def gather(row, block, pair):
        start = row * width
        sub = lax.broadcasted_iota(jnp.int32, (8, LANES), 0)
        for u in range(0, BLOCK, 4):
            merged = None
            for e in range(4):
                at = pl.ds(block * BLOCK + u + e, idx_ref.shape[0] - width + 1)
                k = idx_ref.at[at][start]
                loaded = table[pl.ds(k + (TABLE_PAD - 2 * e), 8), :]
                merged = loaded if merged is None else jnp.where(sub < 2 * e, merged, loaded)
            pair[2 * u : 2 * u + 8, :] = merged

    def interpolate(step, block, pair, slot):
        near = pair[pl.ds(0, BLOCK, stride=2), :].astype(BF16)
        far = pair[pl.ds(1, BLOCK, stride=2), :].astype(BF16)
        t = jnp.concatenate([near, far], axis=1).T.astype(F32)
        at = slice(block * BLOCK, (block + 1) * BLOCK)
        total = jnp.zeros((features, BLOCK), F32)
        for corner in range(8):
            place = (corner % 2) * 4 + corner // 2
            w = weights[corner, pl.ds(step, 1), at]
            total = total + t[place * features : (place + 1) * features] * w
        feats[slot, :, at] = total.astype(BF16)

    layers = mid_ref.shape[0]

    def stage(row, slot, layer, lanes):
        if layer == 0:
            feat = feats[slot, :, lanes]
            saved_ref[row, :features, lanes] = feat
            both = jnp.maximum(dot(first[...], feat), 0.0).astype(BF16)
            hidden_rows[:, lanes] = both
            saved_ref[row, features:, lanes] = both[hidden:]
        elif layer <= layers:
            h = dot(mid_ref[layer - 1], hidden_rows[:hidden, lanes])
            hidden_rows[:hidden, lanes] = jnp.maximum(h, 0.0).astype(BF16)
        else:
            logits = dot(head[...], hidden_rows[:, lanes])
            fine_logit[pl.ds(row, 1), lanes] = logits[0:1]
            prop_logit[pl.ds(row, 1), lanes] = logits[1:2]

    def stages(row, slot):
        parts_of = NET_SPLIT
        size = width // parts_of
        return [
            functools.partial(stage, row, slot, layer, slice(h * size, (h + 1) * size))
            for layer in range(layers + 2)
            for h in range(parts_of)
        ]

    fetch_idx = pltpu.make_async_copy(idx_hbm, idx_ref, idx_sem)
    fetch_idx.start()
    for c in reversed(range(CHUNKS)):
        fetch_grid(grid_hbm, grid_ref, grid_sem, c).start()
    feats[...] = jnp.zeros(feats.shape, BF16)
    whole = [arrived_ref[q, :, :width].astype(F32) for q in range(parts)]
    g = [stack_rows(whole, j) for j in range(4)]
    spacing[...] = g[3]
    first[:hidden, :] = fine_in_ref[...].astype(F32).T.astype(BF16)
    first[hidden:, :] = prop_in_ref[...]
    zero_f = jnp.zeros((1, prop_hidden), F32)
    zero_p = jnp.zeros((1, hidden), F32)
    top = jnp.concatenate([fine_out_ref[...].astype(F32), zero_f], axis=1)
    low = jnp.concatenate([zero_p, prop_out_ref[...].astype(F32)], axis=1)
    rest = jnp.zeros((6, hidden + prop_hidden), F32)
    head[...] = jnp.concatenate([top, low, rest], axis=0).astype(BF16)
    for corner in range(8):
        bits = (corner // 4, corner // 2 % 2, corner % 2)
        w = [x if bit else 1.0 - x for x, bit in zip(g, bits)]
        weights[corner] = w[0] * w[1] * w[2]
    build_table(grid_hbm, grid_ref, grid_sem, table)
    fetch_idx.wait()
    gather(0, 0, rows.at[0])

    def turn(step, carry):
        todo = stages(jnp.maximum(step - 1, 0), (step + 1) % 2)
        for j in range(blocks):
            for run in todo[j * len(todo) // blocks : (j + 1) * len(todo) // blocks]:
                run()
            interpolate(step, j, rows.at[j % DEPTH], step % 2)
            ahead = rows.at[(j + 1) % DEPTH]
            if j + 1 < blocks:
                gather(step, j + 1, ahead)
            else:
                gather(jnp.minimum(step + 1, parts - 1), 0, ahead)
        return carry

    lax.fori_loop(0, parts, turn, 0)

    for run in stages(parts - 1, (parts - 1) % 2):
        run()
    space = pieces_of(spacing[...])
    results = []
    for k, ref in enumerate((prop_logit, fine_logit)):
        logit = pieces_of(ref[...])
        optical = [softplus(x) * s for x, s in zip(logit, space)]
        depth, whole = running(optical, cap)
        early = [jnp.exp(o - d) for o, d in zip(optical, depth)]
        absorb = [e - jnp.exp(-d) for e, d in zip(early, depth)]
        results.append((absorb, whole))
        if k == 0:
            slope = [s * jax.nn.sigmoid(x) for x, s in zip(logit, space)]
            dense_ref[0] = jnp.concatenate(early, axis=1)
            dense_ref[3] = jnp.concatenate(slope, axis=1)
    (a, log_prop), (b, log_fine) = results
    dense_ref[1] = jnp.concatenate(a, axis=1)
    dense_ref[2] = jnp.concatenate(b, axis=1)
    sums = [lane_fold(sum(x * y for x, y in zip(s, t)), cap) for s, t in ((a, a), (a, b), (b, b))]
    stats = [-log_prop, -log_fine] + sums
    per = LANES // cap
    group = lax.broadcasted_iota(jnp.int32, stats[0].shape, 1) // cap
    slabs = []
    for s in range(-(-len(stats) // per)):
        slab = jnp.zeros_like(stats[0])
        for k, x in enumerate(stats[s * per : (s + 1) * per]):
            slab = jnp.where(group == k, x, slab)
        slabs.append(slab)
    summary = jnp.concatenate(slabs, axis=1)
    for p in range(parts):
        summary_ref[p] = summary


def forward(cells, grid, arrived, fine_in, prop_in, mid, fine_out, prop_out, cap):
    parts = arrived.shape[0]
    width = cells.shape[0] // parts
    features, total = grid.shape
    hidden = mid.shape[1]
    prop_hidden = prop_in.shape[0]
    kept = features + prop_hidden
    stat_lanes = -(-5 // (LANES // cap)) * LANES
    vmem = pl.BlockSpec(memory_space=pltpu.VMEM)
    small = (arrived, fine_in, prop_in, mid, fine_out, prop_out)
    return pl.pallas_call(
        functools.partial(forward_kernel, cap),
        out_shape=(
            jax.ShapeDtypeStruct((parts, kept, width), BF16),
            jax.ShapeDtypeStruct((4, parts, width), F32),
            jax.ShapeDtypeStruct((parts, parts, stat_lanes), F32),
        ),
        in_specs=[
            pl.BlockSpec(memory_space=pltpu.HBM),
            pl.BlockSpec(memory_space=pltpu.HBM),
        ]
        + [vmem] * len(small),
        out_specs=(vmem,) * 3,
        scratch_shapes=[
            pltpu.SMEM(cells.shape, jnp.int32),
            pltpu.SemaphoreType.DMA,
            pltpu.VMEM((total + 2 * TABLE_PAD, LANES), F32),
            pltpu.VMEM((features, total), BF16),
            pltpu.SemaphoreType.DMA((CHUNKS,)),
            pltpu.VMEM((DEPTH, 2 * BLOCK, LANES), F32),
            pltpu.VMEM((2, features, width), BF16),
            pltpu.VMEM((hidden + prop_hidden, width), BF16),
            pltpu.VMEM((8, parts, width), F32),
            pltpu.VMEM((parts, width), F32),
            pltpu.VMEM((hidden + prop_hidden, features), BF16),
            pltpu.VMEM((8, hidden + prop_hidden), BF16),
            pltpu.VMEM((parts, width), F32),
            pltpu.VMEM((parts, width), F32),
        ],
        compiler_params=pltpu.CompilerParams(vmem_limit_bytes=(32 + parts // 2) * 1024 * 1024),
        name="forward",
    )(in_hbm(cells), in_hbm(grid), arrived, *[in_hbm(x) for x in small[1:]])


def backward_kernel(
    cap, me_ref, stats_ref, key_ref, hot_ref, dense_ref, saved_ref, prop_out_ref, *rest,
):
    masks, (loss_ref, grad_ref, slope_ref, *keys_t) = rest[:-3], rest[-3:]
    if stats_ref.shape[0] * cap > 256:
        masks, (loss_ref, grad_ref, slope_ref, *keys_t) = (), rest
    me = me_ref[0]
    parts = stats_ref.shape[0]
    slots = key_ref.shape[1]
    per = LANES // cap
    width = dense_ref.shape[2]
    prop_hidden = prop_out_ref.shape[1]
    key = key_ref[...]
    live = (key >= 0).astype(F32)
    sub = lax.broadcasted_iota(jnp.int32, (parts, slots), 0)
    if not masks:
        keys_t[0][...] = key.T

    def mask_of(q):
        lane = lax.broadcasted_iota(jnp.int32, (slots, parts), 1)
        col = jnp.sum(jnp.where(lane == q, keys_t[0][...], 0.0), axis=1, keepdims=True)
        row = jnp.sum(jnp.where(sub == q, key, 0.0), axis=0, keepdims=True)
        gap = row - col
        return ((gap > 0) & (gap < parts)).astype(BF16)

    def over(body, init):
        if masks:
            for q in range(parts):
                init = body(q, init)
            return init
        return lax.fori_loop(0, parts, body, init)

    group = lax.broadcasted_iota(jnp.int32, (parts, LANES), 1) // cap

    def flat(j):
        slab = slice((j // per) * LANES, (j // per + 1) * LANES)
        out = []
        for half in range(slots // LANES):
            x = jnp.zeros((parts, LANES), F32)
            for k in range(per):
                piece = stats_ref[half * per + k, :, slab]
                shift = ((k - j % per) * cap) % LANES
                x = jnp.where(group == k, pltpu.roll(piece, shift, 1) if shift else piece, x)
            out.append(x)
        return jnp.concatenate(out, axis=1)

    log_prop, log_fine, sum_aa, sum_ab, sum_bb = [flat(j) for j in range(5)]
    terms = split3(log_prop * live) + split3(log_fine * live)
    stacked = jnp.concatenate(terms, axis=0)

    def lead(q, acc):
        m = masks[0][q] if masks else mask_of(q)
        y = dot(stacked, m)
        return tuple(
            jnp.where(sub == q, y[k * parts : (k + 1) * parts], x) for k, x in enumerate(acc)
        )

    zero = jnp.zeros((parts, slots), F32)
    lead_sums = over(lead, (zero,) * 6)
    entry_prop = jnp.exp(lead_sums[0] + lead_sums[1] + lead_sums[2]) * live
    entry_fine = jnp.exp(lead_sums[3] + lead_sums[4] + lead_sums[5]) * live
    seg_loss = (
        entry_prop * entry_prop * sum_aa
        - 2.0 * entry_prop * entry_fine * sum_ab
        + entry_fine * entry_fine * sum_bb
    )
    slot_grad = distill_weight * (entry_prop * sum_aa - entry_fine * sum_ab) * entry_prop
    mine = pl.ds(pl.multiple_of(me * cap, cap), cap)
    grads = jnp.concatenate(split3(slot_grad), axis=0)
    sub_cap = lax.broadcasted_iota(jnp.int32, (parts, cap), 0)

    def tail(q, acc):
        if masks:
            m = masks[0][q, mine, :]
            y = dot_nt(grads, m)
        else:
            y = dot_nt(grads, mask_of(q))
            y = own_lanes(y)
        y = y[:parts] + y[parts : 2 * parts] + y[2 * parts :]
        return jnp.where(sub_cap == q, y, acc)

    def own_lanes(x):
        out = x[:, :cap]
        for p in range(1, parts):
            out = jnp.where(me == p, x[:, p * cap : (p + 1) * cap], out)
        return out

    carried = over(tail, jnp.zeros((parts, cap), F32)) * own_lanes(live)
    coef_aa = own_lanes(0.5 * distill_weight * entry_prop * entry_prop)
    coef_ab = own_lanes(-distill_weight * entry_prop * entry_fine)

    spread = dot(jnp.concatenate(split3(seg_loss), axis=0), hot_ref[...])
    spread = spread[:parts] + spread[parts : 2 * parts] + spread[2 * parts :]
    sub_ray = lax.broadcasted_iota(jnp.int32, (parts, RAY_DEV), 0)
    loss_ref[...] = (0.5 * distill_weight) * jnp.sum(
        jnp.where(sub_ray == me, spread, 0.0), axis=0, keepdims=True
    )

    tile = lambda x: jnp.concatenate([x] * per, axis=1)
    c_aa, c_ab, c_log = tile(2.0 * coef_aa), tile(coef_ab), tile(carried)
    early, a, b, slope = [pieces_of(dense_ref[k]) for k in range(4)]
    d_absorb = [c_aa * x + c_ab * y for x, y in zip(a, b)]
    back = trailing([d * x for d, x in zip(d_absorb, a)], cap)
    logit_grad = [
        ((d * e - c_log - r) * s).astype(BF16).astype(F32)
        for d, e, r, s in zip(d_absorb, early, back, slope)
    ]
    slope_ref[...] = jnp.concatenate(logit_grad, axis=1)
    features = saved_ref.shape[1] - prop_hidden
    wide = jnp.broadcast_to(prop_out_ref[...].astype(F32), (prop_hidden, prop_hidden))
    same = lax.broadcasted_iota(jnp.int32, wide.shape, 0) == lax.broadcasted_iota(
        jnp.int32, wide.shape, 1
    )
    out_col = jnp.sum(jnp.where(same, wide, 0.0), axis=1, keepdims=True)
    first_row = lax.broadcasted_iota(jnp.int32, (prop_hidden, width), 0) == 0

    def accumulate(q, total):
        row = slope_ref[pl.ds(q, 1), :]
        kept = saved_ref[q]
        hidden_grad = jnp.where(kept[features:].astype(F32) > 0, out_col * row, 0.0).astype(BF16)
        alone = jnp.where(first_row, row, 0.0).astype(BF16)
        return total + dot_nt(jnp.concatenate([hidden_grad, alone], axis=0), kept)

    total = jnp.zeros((2 * prop_hidden, saved_ref.shape[1]), F32)
    if masks:
        for q in range(parts):
            total = accumulate(q, total)
    else:
        total = lax.fori_loop(0, parts, accumulate, total)
    grad_ref[...] = total


def backward(me, stats, dense, saved, prop_out, marks, cap):
    key, hot, *masks = marks
    parts, slots = key.shape
    width = dense.shape[2]
    prop_hidden = prop_out.shape[1]
    vmem = pl.BlockSpec(memory_space=pltpu.VMEM)
    return pl.pallas_call(
        functools.partial(backward_kernel, cap),
        out_shape=(
            jax.ShapeDtypeStruct((1, RAY_DEV), F32),
            jax.ShapeDtypeStruct((2 * prop_hidden, saved.shape[1]), F32),
        ),
        in_specs=[pl.BlockSpec(memory_space=pltpu.SMEM)] + [vmem] * (6 + len(masks)),
        out_specs=(vmem, vmem),
        scratch_shapes=[pltpu.VMEM((parts, width), F32)]
        + ([] if masks else [pltpu.VMEM((slots, parts), F32)]),
        compiler_params=pltpu.CompilerParams(vmem_limit_bytes=(12 if masks else 48) * 1024 * 1024),
        name="backward",
    )(me, stats, key, hot, dense, saved, prop_out, *masks)


def sum_replicas(x):
    count = lax.axis_size("rep")
    if count != 4:
        return lax.psum(x, "rep")
    other = [lax.ppermute(x, "rep", [(i, i ^ s) for i in range(count)]) for s in (1, 2, 3)]
    return (x + other[0]) + (other[1] + other[2])


def on_device(
    feature_grid,
    fine_in,
    fine_mid,
    fine_out,
    prop_in,
    prop_out,
    sample_cells,
    sample_geometry,
    slot_ray,
    slot_rank,
    bucket_count,
):
    parts = lax.axis_size("dom")
    cap = slot_ray.shape[3]
    features = feature_grid.shape[1]
    prop_hidden = prop_in.shape[1]
    outgoing = pack(
        sample_geometry[:, 0, 0], slot_ray[0, 0], slot_rank[0, 0], bucket_count.reshape(-1)
    )
    arrived = lax.all_to_all(outgoing, "dom", split_axis=0, concat_axis=0, tiled=True)
    saved, dense, summary = forward(
        sample_cells.reshape(-1), feature_grid[0], arrived,
        fine_in[0].T, prop_in[0], fine_mid[0], fine_out, prop_out, cap,
    )
    stats = lax.all_to_all(summary, "dom", split_axis=0, concat_axis=0, tiled=True)
    me = lax.axis_index("dom").reshape(1).astype(jnp.int32)
    marks = slot_marks(me, arrived, cap)
    ray_loss, grads = backward(me, stats, dense, saved, prop_out, marks, cap)
    sums = sum_replicas(grads)
    in_sum = sums[:prop_hidden, :features]
    out_sum = sums[prop_hidden, features:]
    return (ray_loss.reshape(1, 1, -1), in_sum[None], out_sum[None])


def solution(mesh):
    return jax.shard_map(
        on_device,
        mesh=mesh,
        in_specs=(
            P("dom", None, None),
            P("dom", None, None),
            P("dom", None, None, None),
            P("dom", None),
            P("dom", None, None),
            P("dom", None),
            P("dom", "rep", None, None),
            P(None, "dom", "rep", None, None),
            P("dom", "rep", None, None),
            P("dom", "rep", None, None),
            P("dom", "rep", None),
        ),
        out_specs=(P("dom", "rep", None), P("dom", None, None), P("dom", None)),
        check_vma=False,
    )
```

```python
import functools

import jax
import jax.numpy as jnp
from jax import lax
from jax.experimental import pallas as pl
from jax.experimental.pallas import tpu as pltpu
from jax.sharding import PartitionSpec as P

GR = 32
RAY_DEV = 256
LANES = 128
BLOCK = 256
CHUNKS = 8
TABLE_PAD = 8
NET_SPLIT = 4
DEPTH = 4
AHEAD = 3

distill_weight = 50.0
F32 = jnp.float32
BF16 = jnp.bfloat16


def dot(a, b):
    return lax.dot_general(a, b, (((1,), (0,)), ((), ())), preferred_element_type=F32)


def dot_nt(a, b):
    return lax.dot_general(a, b, (((1,), (1,)), ((), ())), preferred_element_type=F32)


def split3(x):
    hi = x.astype(BF16)
    rest = x - hi.astype(F32)
    mid = rest.astype(BF16)
    low = (rest - mid.astype(F32)).astype(BF16)
    return [hi, mid, low]


def in_hbm(x):
    return pltpu.with_memory_space_constraint(x, pltpu.HBM)


def stack_rows(arrays, row):
    return jnp.concatenate([x[row : row + 1] for x in arrays], axis=0)


def flatten_slots(x, cap):
    parts = x.shape[0]
    per = LANES // cap
    lane = lax.broadcasted_iota(jnp.int32, (1, LANES), 1)
    wide = jnp.concatenate([x] * per, axis=1)
    out = []
    for first in range(0, parts, per):
        row = wide[first : first + 1]
        for k in range(1, per):
            row = jnp.where(lane // cap == k, wide[first + k : first + k + 1], row)
        out.append(row)
    return jnp.concatenate(out, axis=1)


def pack_kernel(geometry_ref, ray_ref, rank_ref, count_ref, out_ref):
    parts, cap = ray_ref.shape
    sub = lax.broadcasted_iota(jnp.int32, (parts, cap), 0)
    count = jnp.zeros((parts, cap), jnp.int32)
    for p in range(parts):
        count = jnp.where(sub == p, count_ref[p], count)
    live = lax.broadcasted_iota(jnp.int32, (parts, cap), 1) < count
    ray = jnp.where(live, ray_ref[...], -1).astype(F32)
    marks = jnp.concatenate(
        [flatten_slots(ray, cap), flatten_slots(rank_ref[...].astype(F32), cap)], axis=1
    )
    quarter = marks.shape[1] // 4
    g = [geometry_ref[j].astype(F32) for j in range(4)]
    for p in range(parts):
        rows = [
            jnp.concatenate([x[p : p + 1], marks[:, j * quarter : (j + 1) * quarter]], axis=1)
            for j, x in enumerate(g)
        ]
        out_ref[p] = jnp.concatenate(rows, axis=0).astype(BF16)


def pack(geometry, ray, rank, count):
    parts, width = geometry.shape[1:]
    vmem = pl.BlockSpec(memory_space=pltpu.VMEM)
    return pl.pallas_call(
        pack_kernel,
        out_shape=jax.ShapeDtypeStruct((parts, 4, width + ray.size // 2), BF16),
        in_specs=[vmem] * 3 + [pl.BlockSpec(memory_space=pltpu.SMEM)],
        out_specs=vmem,
        name="pack",
    )(geometry, ray, rank, count)


def marks_kernel(cap, me_ref, arrived_ref, key_ref, hot_ref, *mask_ref):
    me = me_ref[0]
    parts = arrived_ref.shape[0]
    slots = parts * cap
    width = arrived_ref.shape[2] - slots // 2
    ray, rank = [], []
    for q in range(parts):
        marks = arrived_ref[q, :, width:].astype(F32)
        ray.append(jnp.concatenate([marks[0:1], marks[1:2]], axis=1))
        rank.append(jnp.concatenate([marks[2:3], marks[3:4]], axis=1))
    key = jnp.concatenate(ray, axis=0) * (2.0 * parts) + jnp.concatenate(rank, axis=0)
    key_ref[...] = key
    key_t = key.T
    mine = lax.broadcasted_iota(jnp.int32, (slots, parts), 1) == me
    key_col = jnp.sum(jnp.where(mine, key_t, 0.0), axis=1, keepdims=True)
    ray = lax.broadcasted_iota(jnp.int32, (slots, RAY_DEV), 1).astype(F32)
    rest = key_col - ray * (2.0 * parts)
    hot_ref[...] = ((rest >= 0) & (rest < 2 * parts)).astype(BF16)
    if mask_ref:
        for q in range(parts):
            gap = key[q : q + 1] - key_t[:, q : q + 1]
            mask_ref[0][q] = ((gap > 0) & (gap < parts)).astype(BF16)


def slot_marks(me, arrived, cap):
    parts = arrived.shape[0]
    slots = parts * cap
    vmem = pl.BlockSpec(memory_space=pltpu.VMEM)
    shapes = [
        jax.ShapeDtypeStruct((parts, slots), F32),
        jax.ShapeDtypeStruct((slots, RAY_DEV), BF16),
    ]
    if slots <= 256:
        shapes.append(jax.ShapeDtypeStruct((parts, slots, slots), BF16))
    return pl.pallas_call(
        functools.partial(marks_kernel, cap),
        out_shape=tuple(shapes),
        in_specs=[pl.BlockSpec(memory_space=pltpu.SMEM), vmem],
        out_specs=(vmem,) * len(shapes),
        cost_estimate=pl.CostEstimate(
            flops=parts * slots * slots * 8, bytes_accessed=4 << 20, transcendentals=0
        ),
        compiler_params=pltpu.CompilerParams(vmem_limit_bytes=12 * 1024 * 1024),
        name="slot_marks",
    )(me, arrived)


def lane_fold(x, cap):
    shift = LANES // 2
    while shift >= cap:
        x = x + pltpu.roll(x, shift, 1)
        shift //= 2
    return x


def running(pieces, cap):
    lane = lax.broadcasted_iota(jnp.int32, pieces[0].shape, 1)
    carry = jnp.zeros_like(pieces[0])
    out = []
    for x in pieces:
        y = x
        shift = cap
        while shift < LANES:
            y = y + jnp.where(lane >= shift, pltpu.roll(y, shift, 1), 0.0)
            shift *= 2
        out.append(carry + y)
        carry = carry + lane_fold(x, cap)
    return out, carry


def trailing(pieces, cap):
    lane = lax.broadcasted_iota(jnp.int32, pieces[0].shape, 1)
    carry = jnp.zeros_like(pieces[0])
    out = []
    for x in reversed(pieces):
        y = x
        shift = cap
        while shift < LANES:
            y = y + jnp.where(lane < LANES - shift, pltpu.roll(y, LANES - shift, 1), 0.0)
            shift *= 2
        out.append(carry + y)
        carry = carry + lane_fold(x, cap)
    return out[::-1]


def softplus(x):
    return jnp.maximum(x, 0.0) + jnp.log1p(jnp.exp(-jnp.abs(x)))


def pieces_of(x):
    return [x[:, v * LANES : (v + 1) * LANES] for v in range(x.shape[1] // LANES)]


def fetch_grid(grid_hbm, grid_ref, sem, c):
    chunk = grid_ref.shape[1] // CHUNKS
    at = pl.ds(c * chunk, chunk)
    return pltpu.make_async_copy(grid_hbm.at[:, at], grid_ref.at[:, at], sem.at[c])


def build_table(grid_hbm, grid_ref, sem, table):
    features, cells = grid_ref.shape
    plane = GR * GR
    span = 2 * BLOCK
    chunk = cells // CHUNKS
    upper = lax.broadcasted_iota(jnp.int32, (span, LANES), 1) // features % 2 == 1

    def build(i, carry, top):
        c0 = pl.multiple_of(top - (i + 1) * span, span)
        base = grid_ref[:, pl.ds(c0, span)]
        across = grid_ref[:, pl.ds(c0 + plane, span)]
        rows = jnp.concatenate([base, base, across, across], axis=0).T.astype(F32)
        table[pl.ds(c0 + TABLE_PAD, span), :] = jnp.where(
            upper, jnp.concatenate([rows[GR:], carry], axis=0), rows
        )
        return rows[:GR]

    carry = jnp.zeros((GR, LANES), F32)
    for c in reversed(range(CHUNKS)):
        fetch_grid(grid_hbm, grid_ref, sem, c).wait()
        top = cells - plane if c == CHUNKS - 1 else (c + 1) * chunk
        body = functools.partial(build, top=top)
        carry = lax.fori_loop(0, (top - c * chunk) // span, body, carry, unroll=True)


def forward_kernel(
    cap, idx_hbm, grid_hbm, arrived_ref, fine_in_ref, prop_in_ref, mid_ref, fine_out_ref,
    prop_out_ref, saved_ref, dense_ref, summary_ref,
    idx_ref, idx_sem, table, grid_ref, grid_sem, rows, feats, hidden_rows, weights, spacing, first, head, fine_logit, prop_logit,
):
    parts = arrived_ref.shape[0]
    width = idx_ref.shape[0] // parts
    blocks = width // BLOCK
    features = prop_in_ref.shape[1]
    hidden = mid_ref.shape[1]
    prop_hidden = prop_in_ref.shape[0]

    def gather(row, block, pair):
        start = row * width
        sub = lax.broadcasted_iota(jnp.int32, (8, LANES), 0)
        for u in range(0, BLOCK, 4):
            merged = None
            for e in range(4):
                at = pl.ds(block * BLOCK + u + e, idx_ref.shape[0] - width + 1)
                k = idx_ref.at[at][start]
                loaded = table[pl.ds(k + (TABLE_PAD - 2 * e), 8), :]
                merged = loaded if merged is None else jnp.where(sub < 2 * e, merged, loaded)
            pair[2 * u : 2 * u + 8, :] = merged

    def interpolate(step, block, pair, slot):
        near = pair[pl.ds(0, BLOCK, stride=2), :].astype(BF16)
        far = pair[pl.ds(1, BLOCK, stride=2), :].astype(BF16)
        t = jnp.concatenate([near, far], axis=1).T.astype(F32)
        at = slice(block * BLOCK, (block + 1) * BLOCK)
        total = jnp.zeros((features, BLOCK), F32)
        for corner in range(8):
            place = (corner % 2) * 4 + corner // 2
            w = weights[corner, pl.ds(step, 1), at]
            total = total + t[place * features : (place + 1) * features] * w
        feats[slot, :, at] = total.astype(BF16)

    layers = mid_ref.shape[0]

    def stage(row, slot, layer, lanes):
        if layer == 0:
            feat = feats[slot, :, lanes]
            saved_ref[row, :features, lanes] = feat
            both = jnp.maximum(dot(first[...], feat), 0.0).astype(BF16)
            hidden_rows[:, lanes] = both
            saved_ref[row, features:, lanes] = both[hidden:]
        elif layer <= layers:
            h = dot(mid_ref[layer - 1], hidden_rows[:hidden, lanes])
            hidden_rows[:hidden, lanes] = jnp.maximum(h, 0.0).astype(BF16)
        else:
            logits = dot(head[...], hidden_rows[:, lanes])
            fine_logit[pl.ds(row, 1), lanes] = logits[0:1]
            prop_logit[pl.ds(row, 1), lanes] = logits[1:2]

    def stages(row, slot):
        parts_of = NET_SPLIT
        size = width // parts_of
        return [
            functools.partial(stage, row, slot, layer, slice(h * size, (h + 1) * size))
            for layer in range(layers + 2)
            for h in range(parts_of)
        ]

    fetch_idx = pltpu.make_async_copy(idx_hbm, idx_ref, idx_sem)
    fetch_idx.start()
    for c in reversed(range(CHUNKS)):
        fetch_grid(grid_hbm, grid_ref, grid_sem, c).start()
    feats[...] = jnp.zeros(feats.shape, BF16)
    whole = [arrived_ref[q, :, :width].astype(F32) for q in range(parts)]
    g = [stack_rows(whole, j) for j in range(4)]
    spacing[...] = g[3]
    first[:hidden, :] = fine_in_ref[...].astype(F32).T.astype(BF16)
    first[hidden:, :] = prop_in_ref[...]
    zero_f = jnp.zeros((1, prop_hidden), F32)
    zero_p = jnp.zeros((1, hidden), F32)
    top = jnp.concatenate([fine_out_ref[...].astype(F32), zero_f], axis=1)
    low = jnp.concatenate([zero_p, prop_out_ref[...].astype(F32)], axis=1)
    rest = jnp.zeros((6, hidden + prop_hidden), F32)
    head[...] = jnp.concatenate([top, low, rest], axis=0).astype(BF16)
    for corner in range(8):
        bits = (corner // 4, corner // 2 % 2, corner % 2)
        w = [x if bit else 1.0 - x for x, bit in zip(g, bits)]
        weights[corner] = w[0] * w[1] * w[2]
    build_table(grid_hbm, grid_ref, grid_sem, table)
    fetch_idx.wait()
    for j in range(AHEAD):
        gather(0, j, rows.at[j])

    def turn(step, carry):
        todo = stages(jnp.maximum(step - 1, 0), (step + 1) % 2)
        for j in range(blocks):
            for run in todo[j * len(todo) // blocks : (j + 1) * len(todo) // blocks]:
                run()
            interpolate(step, j, rows.at[j % DEPTH], step % 2)
            row = step if j + AHEAD < blocks else jnp.minimum(step + 1, parts - 1)
            gather(row, (j + AHEAD) % blocks, rows.at[(j + AHEAD) % DEPTH])
        return carry

    lax.fori_loop(0, parts, turn, 0)

    for run in stages(parts - 1, (parts - 1) % 2):
        run()
    space = pieces_of(spacing[...])
    results = []
    for k, ref in enumerate((prop_logit, fine_logit)):
        logit = pieces_of(ref[...])
        optical = [softplus(x) * s for x, s in zip(logit, space)]
        depth, whole = running(optical, cap)
        early = [jnp.exp(o - d) for o, d in zip(optical, depth)]
        absorb = [e - jnp.exp(-d) for e, d in zip(early, depth)]
        results.append((absorb, whole))
        if k == 0:
            slope = [s * jax.nn.sigmoid(x) for x, s in zip(logit, space)]
            dense_ref[0] = jnp.concatenate(early, axis=1)
            dense_ref[3] = jnp.concatenate(slope, axis=1)
    (a, log_prop), (b, log_fine) = results
    dense_ref[1] = jnp.concatenate(a, axis=1)
    dense_ref[2] = jnp.concatenate(b, axis=1)
    sums = [lane_fold(sum(x * y for x, y in zip(s, t)), cap) for s, t in ((a, a), (a, b), (b, b))]
    stats = [-log_prop, -log_fine] + sums
    per = LANES // cap
    group = lax.broadcasted_iota(jnp.int32, stats[0].shape, 1) // cap
    slabs = []
    for s in range(-(-len(stats) // per)):
        slab = jnp.zeros_like(stats[0])
        for k, x in enumerate(stats[s * per : (s + 1) * per]):
            slab = jnp.where(group == k, x, slab)
        slabs.append(slab)
    summary = jnp.concatenate(slabs, axis=1)
    for p in range(parts):
        summary_ref[p] = summary


def forward(cells, grid, arrived, fine_in, prop_in, mid, fine_out, prop_out, cap):
    parts = arrived.shape[0]
    width = cells.shape[0] // parts
    features, total = grid.shape
    hidden = mid.shape[1]
    prop_hidden = prop_in.shape[0]
    kept = features + prop_hidden
    stat_lanes = -(-5 // (LANES // cap)) * LANES
    vmem = pl.BlockSpec(memory_space=pltpu.VMEM)
    small = (arrived, fine_in, prop_in, mid, fine_out, prop_out)
    return pl.pallas_call(
        functools.partial(forward_kernel, cap),
        out_shape=(
            jax.ShapeDtypeStruct((parts, kept, width), BF16),
            jax.ShapeDtypeStruct((4, parts, width), F32),
            jax.ShapeDtypeStruct((parts, parts, stat_lanes), F32),
        ),
        in_specs=[
            pl.BlockSpec(memory_space=pltpu.HBM),
            pl.BlockSpec(memory_space=pltpu.HBM),
        ]
        + [vmem] * len(small),
        out_specs=(vmem,) * 3,
        scratch_shapes=[
            pltpu.SMEM(cells.shape, jnp.int32),
            pltpu.SemaphoreType.DMA,
            pltpu.VMEM((total + 2 * TABLE_PAD, LANES), F32),
            pltpu.VMEM((features, total), BF16),
            pltpu.SemaphoreType.DMA((CHUNKS,)),
            pltpu.VMEM((DEPTH, 2 * BLOCK, LANES), F32),
            pltpu.VMEM((2, features, width), BF16),
            pltpu.VMEM((hidden + prop_hidden, width), BF16),
            pltpu.VMEM((8, parts, width), F32),
            pltpu.VMEM((parts, width), F32),
            pltpu.VMEM((hidden + prop_hidden, features), BF16),
            pltpu.VMEM((8, hidden + prop_hidden), BF16),
            pltpu.VMEM((parts, width), F32),
            pltpu.VMEM((parts, width), F32),
        ],
        compiler_params=pltpu.CompilerParams(vmem_limit_bytes=(32 + parts // 2) * 1024 * 1024),
        name="forward",
    )(in_hbm(cells), in_hbm(grid), arrived, *[in_hbm(x) for x in small[1:]])


def backward_kernel(
    cap, me_ref, stats_ref, key_ref, hot_ref, dense_ref, saved_ref, prop_out_ref, *rest,
):
    masks, (loss_ref, grad_ref, slope_ref, *keys_t) = rest[:-3], rest[-3:]
    if stats_ref.shape[0] * cap > 256:
        masks, (loss_ref, grad_ref, slope_ref, *keys_t) = (), rest
    me = me_ref[0]
    parts = stats_ref.shape[0]
    slots = key_ref.shape[1]
    per = LANES // cap
    width = dense_ref.shape[2]
    prop_hidden = prop_out_ref.shape[1]
    key = key_ref[...]
    live = (key >= 0).astype(F32)
    sub = lax.broadcasted_iota(jnp.int32, (parts, slots), 0)
    if not masks:
        keys_t[0][...] = key.T

    def mask_of(q):
        lane = lax.broadcasted_iota(jnp.int32, (slots, parts), 1)
        col = jnp.sum(jnp.where(lane == q, keys_t[0][...], 0.0), axis=1, keepdims=True)
        row = jnp.sum(jnp.where(sub == q, key, 0.0), axis=0, keepdims=True)
        gap = row - col
        return ((gap > 0) & (gap < parts)).astype(BF16)

    def over(body, init):
        if masks:
            for q in range(parts):
                init = body(q, init)
            return init
        return lax.fori_loop(0, parts, body, init)

    group = lax.broadcasted_iota(jnp.int32, (parts, LANES), 1) // cap

    def flat(j):
        slab = slice((j // per) * LANES, (j // per + 1) * LANES)
        out = []
        for half in range(slots // LANES):
            x = jnp.zeros((parts, LANES), F32)
            for k in range(per):
                piece = stats_ref[half * per + k, :, slab]
                shift = ((k - j % per) * cap) % LANES
                x = jnp.where(group == k, pltpu.roll(piece, shift, 1) if shift else piece, x)
            out.append(x)
        return jnp.concatenate(out, axis=1)

    log_prop, log_fine, sum_aa, sum_ab, sum_bb = [flat(j) for j in range(5)]
    terms = split3(log_prop * live) + split3(log_fine * live)
    stacked = jnp.concatenate(terms, axis=0)

    def lead(q, acc):
        m = masks[0][q] if masks else mask_of(q)
        y = dot(stacked, m)
        return tuple(
            jnp.where(sub == q, y[k * parts : (k + 1) * parts], x) for k, x in enumerate(acc)
        )

    zero = jnp.zeros((parts, slots), F32)
    lead_sums = over(lead, (zero,) * 6)
    entry_prop = jnp.exp(lead_sums[0] + lead_sums[1] + lead_sums[2]) * live
    entry_fine = jnp.exp(lead_sums[3] + lead_sums[4] + lead_sums[5]) * live
    seg_loss = (
        entry_prop * entry_prop * sum_aa
        - 2.0 * entry_prop * entry_fine * sum_ab
        + entry_fine * entry_fine * sum_bb
    )
    slot_grad = distill_weight * (entry_prop * sum_aa - entry_fine * sum_ab) * entry_prop
    mine = pl.ds(pl.multiple_of(me * cap, cap), cap)
    grads = jnp.concatenate(split3(slot_grad), axis=0)
    sub_cap = lax.broadcasted_iota(jnp.int32, (parts, cap), 0)

    def tail(q, acc):
        if masks:
            m = masks[0][q, mine, :]
            y = dot_nt(grads, m)
        else:
            y = dot_nt(grads, mask_of(q))
            y = own_lanes(y)
        y = y[:parts] + y[parts : 2 * parts] + y[2 * parts :]
        return jnp.where(sub_cap == q, y, acc)

    def own_lanes(x):
        out = x[:, :cap]
        for p in range(1, parts):
            out = jnp.where(me == p, x[:, p * cap : (p + 1) * cap], out)
        return out

    carried = over(tail, jnp.zeros((parts, cap), F32)) * own_lanes(live)
    coef_aa = own_lanes(0.5 * distill_weight * entry_prop * entry_prop)
    coef_ab = own_lanes(-distill_weight * entry_prop * entry_fine)

    spread = dot(jnp.concatenate(split3(seg_loss), axis=0), hot_ref[...])
    spread = spread[:parts] + spread[parts : 2 * parts] + spread[2 * parts :]
    sub_ray = lax.broadcasted_iota(jnp.int32, (parts, RAY_DEV), 0)
    loss_ref[...] = (0.5 * distill_weight) * jnp.sum(
        jnp.where(sub_ray == me, spread, 0.0), axis=0, keepdims=True
    )

    tile = lambda x: jnp.concatenate([x] * per, axis=1)
    c_aa, c_ab, c_log = tile(2.0 * coef_aa), tile(coef_ab), tile(carried)
    early, a, b, slope = [pieces_of(dense_ref[k]) for k in range(4)]
    d_absorb = [c_aa * x + c_ab * y for x, y in zip(a, b)]
    back = trailing([d * x for d, x in zip(d_absorb, a)], cap)
    logit_grad = [
        ((d * e - c_log - r) * s).astype(BF16).astype(F32)
        for d, e, r, s in zip(d_absorb, early, back, slope)
    ]
    slope_ref[...] = jnp.concatenate(logit_grad, axis=1)
    features = saved_ref.shape[1] - prop_hidden
    wide = jnp.broadcast_to(prop_out_ref[...].astype(F32), (prop_hidden, prop_hidden))
    same = lax.broadcasted_iota(jnp.int32, wide.shape, 0) == lax.broadcasted_iota(
        jnp.int32, wide.shape, 1
    )
    out_col = jnp.sum(jnp.where(same, wide, 0.0), axis=1, keepdims=True)
    first_row = lax.broadcasted_iota(jnp.int32, (prop_hidden, width), 0) == 0

    def accumulate(q, total):
        row = slope_ref[pl.ds(q, 1), :]
        kept = saved_ref[q]
        hidden_grad = jnp.where(kept[features:].astype(F32) > 0, out_col * row, 0.0).astype(BF16)
        alone = jnp.where(first_row, row, 0.0).astype(BF16)
        return total + dot_nt(jnp.concatenate([hidden_grad, alone], axis=0), kept)

    total = jnp.zeros((2 * prop_hidden, saved_ref.shape[1]), F32)
    if masks:
        for q in range(parts):
            total = accumulate(q, total)
    else:
        total = lax.fori_loop(0, parts, accumulate, total)
    grad_ref[...] = total


def backward(me, stats, dense, saved, prop_out, marks, cap):
    key, hot, *masks = marks
    parts, slots = key.shape
    width = dense.shape[2]
    prop_hidden = prop_out.shape[1]
    vmem = pl.BlockSpec(memory_space=pltpu.VMEM)
    return pl.pallas_call(
        functools.partial(backward_kernel, cap),
        out_shape=(
            jax.ShapeDtypeStruct((1, RAY_DEV), F32),
            jax.ShapeDtypeStruct((2 * prop_hidden, saved.shape[1]), F32),
        ),
        in_specs=[pl.BlockSpec(memory_space=pltpu.SMEM)] + [vmem] * (6 + len(masks)),
        out_specs=(vmem, vmem),
        scratch_shapes=[pltpu.VMEM((parts, width), F32)]
        + ([] if masks else [pltpu.VMEM((slots, parts), F32)]),
        compiler_params=pltpu.CompilerParams(vmem_limit_bytes=(12 if masks else 48) * 1024 * 1024),
        name="backward",
    )(me, stats, key, hot, dense, saved, prop_out, *masks)


def sum_replicas(x):
    count = lax.axis_size("rep")
    if count != 4:
        return lax.psum(x, "rep")
    other = [lax.ppermute(x, "rep", [(i, i ^ s) for i in range(count)]) for s in (1, 2, 3)]
    return (x + other[0]) + (other[1] + other[2])


def on_device(
    feature_grid,
    fine_in,
    fine_mid,
    fine_out,
    prop_in,
    prop_out,
    sample_cells,
    sample_geometry,
    slot_ray,
    slot_rank,
    bucket_count,
):
    parts = lax.axis_size("dom")
    cap = slot_ray.shape[3]
    features = feature_grid.shape[1]
    prop_hidden = prop_in.shape[1]
    outgoing = pack(
        sample_geometry[:, 0, 0], slot_ray[0, 0], slot_rank[0, 0], bucket_count.reshape(-1)
    )
    arrived = lax.all_to_all(outgoing, "dom", split_axis=0, concat_axis=0, tiled=True)
    saved, dense, summary = forward(
        sample_cells.reshape(-1), feature_grid[0], arrived,
        fine_in[0].T, prop_in[0], fine_mid[0], fine_out, prop_out, cap,
    )
    stats = lax.all_to_all(summary, "dom", split_axis=0, concat_axis=0, tiled=True)
    me = lax.axis_index("dom").reshape(1).astype(jnp.int32)
    marks = slot_marks(me, arrived, cap)
    ray_loss, grads = backward(me, stats, dense, saved, prop_out, marks, cap)
    sums = sum_replicas(grads)
    in_sum = sums[:prop_hidden, :features]
    out_sum = sums[prop_hidden, features:]
    return (ray_loss.reshape(1, 1, -1), in_sum[None], out_sum[None])


def solution(mesh):
    return jax.shard_map(
        on_device,
        mesh=mesh,
        in_specs=(
            P("dom", None, None),
            P("dom", None, None),
            P("dom", None, None, None),
            P("dom", None),
            P("dom", None, None),
            P("dom", None),
            P("dom", "rep", None, None),
            P(None, "dom", "rep", None, None),
            P("dom", "rep", None, None),
            P("dom", "rep", None, None),
            P("dom", "rep", None),
        ),
        out_specs=(P("dom", "rep", None), P("dom", None, None), P("dom", None)),
        check_vma=False,
    )
```

```python
import functools

import jax
import jax.numpy as jnp
from jax import lax
from jax.experimental import pallas as pl
from jax.experimental.pallas import tpu as pltpu
from jax.sharding import PartitionSpec as P

GR = 32
RAY_DEV = 256
LANES = 128
BLOCK = 256
CHUNKS = 8
TABLE_PAD = 8
NET_SPLIT = 4
DEPTH = 4
AHEAD = 3

distill_weight = 50.0
F32 = jnp.float32
BF16 = jnp.bfloat16


def dot(a, b):
    return lax.dot_general(a, b, (((1,), (0,)), ((), ())), preferred_element_type=F32)


def dot_nt(a, b):
    return lax.dot_general(a, b, (((1,), (1,)), ((), ())), preferred_element_type=F32)


def split3(x):
    hi = x.astype(BF16)
    rest = x - hi.astype(F32)
    mid = rest.astype(BF16)
    low = (rest - mid.astype(F32)).astype(BF16)
    return [hi, mid, low]


def in_hbm(x):
    return pltpu.with_memory_space_constraint(x, pltpu.HBM)


def stack_rows(arrays, row):
    return jnp.concatenate([x[row : row + 1] for x in arrays], axis=0)


def flatten_slots(x, cap):
    parts = x.shape[0]
    per = LANES // cap
    lane = lax.broadcasted_iota(jnp.int32, (1, LANES), 1)
    wide = jnp.concatenate([x] * per, axis=1)
    out = []
    for first in range(0, parts, per):
        row = wide[first : first + 1]
        for k in range(1, per):
            row = jnp.where(lane // cap == k, wide[first + k : first + k + 1], row)
        out.append(row)
    return jnp.concatenate(out, axis=1)


def pack_kernel(geometry_ref, ray_ref, rank_ref, count_ref, out_ref):
    parts, cap = ray_ref.shape
    sub = lax.broadcasted_iota(jnp.int32, (parts, cap), 0)
    count = jnp.zeros((parts, cap), jnp.int32)
    for p in range(parts):
        count = jnp.where(sub == p, count_ref[p], count)
    live = lax.broadcasted_iota(jnp.int32, (parts, cap), 1) < count
    ray = jnp.where(live, ray_ref[...], -1).astype(F32)
    marks = jnp.concatenate(
        [flatten_slots(ray, cap), flatten_slots(rank_ref[...].astype(F32), cap)], axis=1
    )
    quarter = marks.shape[1] // 4
    g = [geometry_ref[j].astype(F32) for j in range(4)]
    for p in range(parts):
        rows = [
            jnp.concatenate([x[p : p + 1], marks[:, j * quarter : (j + 1) * quarter]], axis=1)
            for j, x in enumerate(g)
        ]
        out_ref[p] = jnp.concatenate(rows, axis=0).astype(BF16)


def pack(geometry, ray, rank, count):
    parts, width = geometry.shape[1:]
    vmem = pl.BlockSpec(memory_space=pltpu.VMEM)
    return pl.pallas_call(
        pack_kernel,
        out_shape=jax.ShapeDtypeStruct((parts, 4, width + ray.size // 2), BF16),
        in_specs=[vmem] * 3 + [pl.BlockSpec(memory_space=pltpu.SMEM)],
        out_specs=vmem,
        name="pack",
    )(geometry, ray, rank, count)


def marks_kernel(cap, me_ref, arrived_ref, key_ref, hot_ref, *mask_ref):
    me = me_ref[0]
    parts = arrived_ref.shape[0]
    slots = parts * cap
    width = arrived_ref.shape[2] - slots // 2
    ray, rank = [], []
    for q in range(parts):
        marks = arrived_ref[q, :, width:].astype(F32)
        ray.append(jnp.concatenate([marks[0:1], marks[1:2]], axis=1))
        rank.append(jnp.concatenate([marks[2:3], marks[3:4]], axis=1))
    key = jnp.concatenate(ray, axis=0) * (2.0 * parts) + jnp.concatenate(rank, axis=0)
    key_ref[...] = key
    key_t = key.T
    mine = lax.broadcasted_iota(jnp.int32, (slots, parts), 1) == me
    key_col = jnp.sum(jnp.where(mine, key_t, 0.0), axis=1, keepdims=True)
    ray = lax.broadcasted_iota(jnp.int32, (slots, RAY_DEV), 1).astype(F32)
    rest = key_col - ray * (2.0 * parts)
    hot_ref[...] = ((rest >= 0) & (rest < 2 * parts)).astype(BF16)
    if mask_ref:
        for q in range(parts):
            gap = key[q : q + 1] - key_t[:, q : q + 1]
            mask_ref[0][q] = ((gap > 0) & (gap < parts)).astype(BF16)


def slot_marks(me, arrived, cap):
    parts = arrived.shape[0]
    slots = parts * cap
    vmem = pl.BlockSpec(memory_space=pltpu.VMEM)
    shapes = [
        jax.ShapeDtypeStruct((parts, slots), F32),
        jax.ShapeDtypeStruct((slots, RAY_DEV), BF16),
    ]
    if slots <= 256:
        shapes.append(jax.ShapeDtypeStruct((parts, slots, slots), BF16))
    return pl.pallas_call(
        functools.partial(marks_kernel, cap),
        out_shape=tuple(shapes),
        in_specs=[pl.BlockSpec(memory_space=pltpu.SMEM), vmem],
        out_specs=(vmem,) * len(shapes),
        cost_estimate=pl.CostEstimate(
            flops=parts * slots * slots * 8, bytes_accessed=4 << 20, transcendentals=0
        ),
        compiler_params=pltpu.CompilerParams(vmem_limit_bytes=12 * 1024 * 1024),
        name="slot_marks",
    )(me, arrived)


def lane_fold(x, cap):
    shift = LANES // 2
    while shift >= cap:
        x = x + pltpu.roll(x, shift, 1)
        shift //= 2
    return x


def running(pieces, cap):
    lane = lax.broadcasted_iota(jnp.int32, pieces[0].shape, 1)
    carry = jnp.zeros_like(pieces[0])
    out = []
    for x in pieces:
        y = x
        shift = cap
        while shift < LANES:
            y = y + jnp.where(lane >= shift, pltpu.roll(y, shift, 1), 0.0)
            shift *= 2
        out.append(carry + y)
        carry = carry + lane_fold(x, cap)
    return out, carry


def trailing(pieces, cap):
    lane = lax.broadcasted_iota(jnp.int32, pieces[0].shape, 1)
    carry = jnp.zeros_like(pieces[0])
    out = []
    for x in reversed(pieces):
        y = x
        shift = cap
        while shift < LANES:
            y = y + jnp.where(lane < LANES - shift, pltpu.roll(y, LANES - shift, 1), 0.0)
            shift *= 2
        out.append(carry + y)
        carry = carry + lane_fold(x, cap)
    return out[::-1]


def softplus(x):
    return jnp.maximum(x, 0.0) + jnp.log1p(jnp.exp(-jnp.abs(x)))


def pieces_of(x):
    return [x[:, v * LANES : (v + 1) * LANES] for v in range(x.shape[1] // LANES)]


def fetch_grid(grid_hbm, grid_ref, sem, c):
    chunk = grid_ref.shape[1] // CHUNKS
    at = pl.ds(c * chunk, chunk)
    return pltpu.make_async_copy(grid_hbm.at[:, at], grid_ref.at[:, at], sem.at[c])


def build_table(grid_hbm, grid_ref, sem, table):
    features, cells = grid_ref.shape
    plane = GR * GR
    span = 2 * BLOCK
    chunk = cells // CHUNKS
    upper = lax.broadcasted_iota(jnp.int32, (span, LANES), 1) // features % 2 == 1

    def build(i, carry, top):
        c0 = pl.multiple_of(top - (i + 1) * span, span)
        base = grid_ref[:, pl.ds(c0, span)]
        across = grid_ref[:, pl.ds(c0 + plane, span)]
        rows = jnp.concatenate([base, base, across, across], axis=0).T.astype(F32)
        table[pl.ds(c0 + TABLE_PAD, span), :] = jnp.where(
            upper, jnp.concatenate([rows[GR:], carry], axis=0), rows
        )
        return rows[:GR]

    carry = jnp.zeros((GR, LANES), F32)
    for c in reversed(range(CHUNKS)):
        fetch_grid(grid_hbm, grid_ref, sem, c).wait()
        top = cells - plane if c == CHUNKS - 1 else (c + 1) * chunk
        body = functools.partial(build, top=top)
        carry = lax.fori_loop(0, (top - c * chunk) // span, body, carry, unroll=True)


def forward_kernel(
    cap, idx_hbm, grid_hbm, arrived_ref, fine_in_ref, prop_in_ref, mid_ref, fine_out_ref,
    prop_out_ref, saved_ref, dense_ref, summary_ref,
    idx_ref, idx_sem, table, grid_ref, grid_sem, rows, feats, hidden_rows, weights, spacing, first, head, fine_logit, prop_logit,
):
    parts = arrived_ref.shape[0]
    width = idx_ref.shape[0] // parts
    blocks = width // BLOCK
    features = prop_in_ref.shape[1]
    hidden = mid_ref.shape[1]
    prop_hidden = prop_in_ref.shape[0]

    def gather(row, block, pair):
        start = row * width
        sub = lax.broadcasted_iota(jnp.int32, (8, LANES), 0)
        for u in range(0, BLOCK, 4):
            merged = None
            for e in range(4):
                at = pl.ds(block * BLOCK + u + e, idx_ref.shape[0] - width + 1)
                k = idx_ref.at[at][start]
                loaded = table[pl.ds(k + (TABLE_PAD - 2 * e), 8), :]
                merged = loaded if merged is None else jnp.where(sub < 2 * e, merged, loaded)
            pair[2 * u : 2 * u + 8, :] = merged

    def interpolate(step, block, pair, slot):
        near = pair[pl.ds(0, BLOCK, stride=2), :].astype(BF16)
        far = pair[pl.ds(1, BLOCK, stride=2), :].astype(BF16)
        t = jnp.concatenate([near, far], axis=1).T.astype(F32)
        at = slice(block * BLOCK, (block + 1) * BLOCK)
        total = jnp.zeros((features, BLOCK), F32)
        for corner in range(8):
            place = (corner % 2) * 4 + corner // 2
            w = weights[corner, pl.ds(step, 1), at]
            total = total + t[place * features : (place + 1) * features] * w
        feats[slot, :, at] = total.astype(BF16)

    layers = mid_ref.shape[0]

    def stage(row, slot, layer, lanes):
        if layer == 0:
            feat = feats[slot, :, lanes]
            saved_ref[row, :features, lanes] = feat
            both = jnp.maximum(dot(first[...], feat), 0.0).astype(BF16)
            hidden_rows[:, lanes] = both
            saved_ref[row, features:, lanes] = both[hidden:]
        elif layer <= layers:
            h = dot(mid_ref[layer - 1], hidden_rows[:hidden, lanes])
            hidden_rows[:hidden, lanes] = jnp.maximum(h, 0.0).astype(BF16)
        else:
            logits = dot(head[...], hidden_rows[:, lanes])
            fine_logit[pl.ds(row, 1), lanes] = logits[0:1]
            prop_logit[pl.ds(row, 1), lanes] = logits[1:2]

    def stages(row, slot):
        parts_of = NET_SPLIT
        size = width // parts_of
        return [
            functools.partial(stage, row, slot, layer, slice(h * size, (h + 1) * size))
            for layer in range(layers + 2)
            for h in range(parts_of)
        ]

    fetch_idx = pltpu.make_async_copy(idx_hbm, idx_ref, idx_sem)
    fetch_idx.start()
    for c in reversed(range(CHUNKS)):
        fetch_grid(grid_hbm, grid_ref, grid_sem, c).start()
    feats[...] = jnp.zeros(feats.shape, BF16)
    whole = [arrived_ref[q, :, :width].astype(F32) for q in range(parts)]
    g = [stack_rows(whole, j) for j in range(4)]
    spacing[...] = g[3]
    first[:hidden, :] = fine_in_ref[...].astype(F32).T.astype(BF16)
    first[hidden:, :] = prop_in_ref[...]
    zero_f = jnp.zeros((1, prop_hidden), F32)
    zero_p = jnp.zeros((1, hidden), F32)
    top = jnp.concatenate([fine_out_ref[...].astype(F32), zero_f], axis=1)
    low = jnp.concatenate([zero_p, prop_out_ref[...].astype(F32)], axis=1)
    rest = jnp.zeros((6, hidden + prop_hidden), F32)
    head[...] = jnp.concatenate([top, low, rest], axis=0).astype(BF16)
    for corner in range(8):
        bits = (corner // 4, corner // 2 % 2, corner % 2)
        w = [x if bit else 1.0 - x for x, bit in zip(g, bits)]
        weights[corner] = w[0] * w[1] * w[2]
    build_table(grid_hbm, grid_ref, grid_sem, table)
    fetch_idx.wait()
    for j in range(AHEAD):
        gather(0, j, rows.at[j])

    def turn(step, carry):
        todo = stages(jnp.maximum(step - 1, 0), (step + 1) % 2)
        for j in range(blocks):
            for run in todo[j * len(todo) // blocks : (j + 1) * len(todo) // blocks]:
                run()
            interpolate(step, j, rows.at[j % DEPTH], step % 2)
            row = step if j + AHEAD < blocks else jnp.minimum(step + 1, parts - 1)
            gather(row, (j + AHEAD) % blocks, rows.at[(j + AHEAD) % DEPTH])
        return carry

    lax.fori_loop(0, parts, turn, 0)

    for run in stages(parts - 1, (parts - 1) % 2):
        run()
    space = pieces_of(spacing[...])
    results = []
    for k, ref in enumerate((prop_logit, fine_logit)):
        logit = pieces_of(ref[...])
        optical = [softplus(x) * s for x, s in zip(logit, space)]
        depth, whole = running(optical, cap)
        early = [jnp.exp(o - d) for o, d in zip(optical, depth)]
        absorb = [e - jnp.exp(-d) for e, d in zip(early, depth)]
        results.append((absorb, whole))
        if k == 0:
            slope = [s * jax.nn.sigmoid(x) for x, s in zip(logit, space)]
            dense_ref[0] = jnp.concatenate(early, axis=1)
            dense_ref[3] = jnp.concatenate(slope, axis=1)
    (a, log_prop), (b, log_fine) = results
    dense_ref[1] = jnp.concatenate(a, axis=1)
    dense_ref[2] = jnp.concatenate(b, axis=1)
    sums = [lane_fold(sum(x * y for x, y in zip(s, t)), cap) for s, t in ((a, a), (a, b), (b, b))]
    stats = [-log_prop, -log_fine] + sums
    per = LANES // cap
    group = lax.broadcasted_iota(jnp.int32, stats[0].shape, 1) // cap
    slabs = []
    for s in range(-(-len(stats) // per)):
        slab = jnp.zeros_like(stats[0])
        for k, x in enumerate(stats[s * per : (s + 1) * per]):
            slab = jnp.where(group == k, x, slab)
        slabs.append(slab)
    summary = jnp.concatenate(slabs, axis=1)
    for p in range(parts):
        summary_ref[p] = summary


def forward(cells, grid, arrived, fine_in, prop_in, mid, fine_out, prop_out, cap):
    parts = arrived.shape[0]
    width = cells.shape[0] // parts
    features, total = grid.shape
    hidden = mid.shape[1]
    prop_hidden = prop_in.shape[0]
    kept = features + prop_hidden
    stat_lanes = -(-5 // (LANES // cap)) * LANES
    vmem = pl.BlockSpec(memory_space=pltpu.VMEM)
    small = (arrived, fine_in, prop_in, mid, fine_out, prop_out)
    return pl.pallas_call(
        functools.partial(forward_kernel, cap),
        out_shape=(
            jax.ShapeDtypeStruct((parts, kept, width), BF16),
            jax.ShapeDtypeStruct((4, parts, width), F32),
            jax.ShapeDtypeStruct((parts, parts, stat_lanes), F32),
        ),
        in_specs=[
            pl.BlockSpec(memory_space=pltpu.HBM),
            pl.BlockSpec(memory_space=pltpu.HBM),
        ]
        + [vmem] * len(small),
        out_specs=(vmem,) * 3,
        scratch_shapes=[
            pltpu.SMEM(cells.shape, jnp.int32),
            pltpu.SemaphoreType.DMA,
            pltpu.VMEM((total + 2 * TABLE_PAD, LANES), F32),
            pltpu.VMEM((features, total), BF16),
            pltpu.SemaphoreType.DMA((CHUNKS,)),
            pltpu.VMEM((DEPTH, 2 * BLOCK, LANES), F32),
            pltpu.VMEM((2, features, width), BF16),
            pltpu.VMEM((hidden + prop_hidden, width), BF16),
            pltpu.VMEM((8, parts, width), F32),
            pltpu.VMEM((parts, width), F32),
            pltpu.VMEM((hidden + prop_hidden, features), BF16),
            pltpu.VMEM((8, hidden + prop_hidden), BF16),
            pltpu.VMEM((parts, width), F32),
            pltpu.VMEM((parts, width), F32),
        ],
        compiler_params=pltpu.CompilerParams(vmem_limit_bytes=(32 + parts // 2) * 1024 * 1024),
        name="forward",
    )(in_hbm(cells), in_hbm(grid), arrived, *[in_hbm(x) for x in small[1:]])


def backward_kernel(
    cap, me_ref, stats_ref, key_ref, hot_ref, dense_ref, saved_ref, prop_out_ref, *rest,
):
    masks, (loss_ref, grad_ref, slope_ref, *keys_t) = rest[:-3], rest[-3:]
    if stats_ref.shape[0] * cap > 256:
        masks, (loss_ref, grad_ref, slope_ref, *keys_t) = (), rest
    me = me_ref[0]
    parts = stats_ref.shape[0]
    slots = key_ref.shape[1]
    per = LANES // cap
    width = dense_ref.shape[2]
    prop_hidden = prop_out_ref.shape[1]
    key = key_ref[...]
    live = (key >= 0).astype(F32)
    sub = lax.broadcasted_iota(jnp.int32, (parts, slots), 0)
    if not masks:
        keys_t[0][...] = key.T

    def mask_of(q):
        lane = lax.broadcasted_iota(jnp.int32, (slots, parts), 1)
        col = jnp.sum(jnp.where(lane == q, keys_t[0][...], 0.0), axis=1, keepdims=True)
        row = jnp.sum(jnp.where(sub == q, key, 0.0), axis=0, keepdims=True)
        gap = row - col
        return ((gap > 0) & (gap < parts)).astype(BF16)

    def over(body, init):
        if masks:
            for q in range(parts):
                init = body(q, init)
            return init
        return lax.fori_loop(0, parts, body, init)

    group = lax.broadcasted_iota(jnp.int32, (parts, LANES), 1) // cap

    def flat(j):
        slab = slice((j // per) * LANES, (j // per + 1) * LANES)
        out = []
        for half in range(slots // LANES):
            x = jnp.zeros((parts, LANES), F32)
            for k in range(per):
                piece = stats_ref[half * per + k, :, slab]
                shift = ((k - j % per) * cap) % LANES
                x = jnp.where(group == k, pltpu.roll(piece, shift, 1) if shift else piece, x)
            out.append(x)
        return jnp.concatenate(out, axis=1)

    log_prop, log_fine, sum_aa, sum_ab, sum_bb = [flat(j) for j in range(5)]
    terms = split3(log_prop * live) + split3(log_fine * live)
    stacked = jnp.concatenate(terms, axis=0)

    def lead(q, acc):
        m = masks[0][q] if masks else mask_of(q)
        y = dot(stacked, m)
        return tuple(
            jnp.where(sub == q, y[k * parts : (k + 1) * parts], x) for k, x in enumerate(acc)
        )

    zero = jnp.zeros((parts, slots), F32)
    lead_sums = over(lead, (zero,) * 6)
    entry_prop = jnp.exp(lead_sums[0] + lead_sums[1] + lead_sums[2]) * live
    entry_fine = jnp.exp(lead_sums[3] + lead_sums[4] + lead_sums[5]) * live
    seg_loss = (
        entry_prop * entry_prop * sum_aa
        - 2.0 * entry_prop * entry_fine * sum_ab
        + entry_fine * entry_fine * sum_bb
    )
    slot_grad = distill_weight * (entry_prop * sum_aa - entry_fine * sum_ab) * entry_prop
    mine = pl.ds(pl.multiple_of(me * cap, cap), cap)
    grads = jnp.concatenate(split3(slot_grad), axis=0)
    sub_cap = lax.broadcasted_iota(jnp.int32, (parts, cap), 0)

    def tail(q, acc):
        if masks:
            m = masks[0][q, mine, :]
            y = dot_nt(grads, m)
        else:
            y = dot_nt(grads, mask_of(q))
            y = own_lanes(y)
        y = y[:parts] + y[parts : 2 * parts] + y[2 * parts :]
        return jnp.where(sub_cap == q, y, acc)

    def own_lanes(x):
        out = x[:, :cap]
        for p in range(1, parts):
            out = jnp.where(me == p, x[:, p * cap : (p + 1) * cap], out)
        return out

    carried = over(tail, jnp.zeros((parts, cap), F32)) * own_lanes(live)
    coef_aa = own_lanes(0.5 * distill_weight * entry_prop * entry_prop)
    coef_ab = own_lanes(-distill_weight * entry_prop * entry_fine)

    spread = dot(jnp.concatenate(split3(seg_loss), axis=0), hot_ref[...])
    spread = spread[:parts] + spread[parts : 2 * parts] + spread[2 * parts :]
    sub_ray = lax.broadcasted_iota(jnp.int32, (parts, RAY_DEV), 0)
    loss_ref[...] = (0.5 * distill_weight) * jnp.sum(
        jnp.where(sub_ray == me, spread, 0.0), axis=0, keepdims=True
    )

    tile = lambda x: jnp.concatenate([x] * per, axis=1)
    c_aa, c_ab, c_log = tile(2.0 * coef_aa), tile(coef_ab), tile(carried)
    early, a, b, slope = [pieces_of(dense_ref[k]) for k in range(4)]
    d_absorb = [c_aa * x + c_ab * y for x, y in zip(a, b)]
    back = trailing([d * x for d, x in zip(d_absorb, a)], cap)
    logit_grad = [
        ((d * e - c_log - r) * s).astype(BF16).astype(F32)
        for d, e, r, s in zip(d_absorb, early, back, slope)
    ]
    slope_ref[...] = jnp.concatenate(logit_grad, axis=1)
    features = saved_ref.shape[1] - prop_hidden
    wide = jnp.broadcast_to(prop_out_ref[...].astype(F32), (prop_hidden, prop_hidden))
    same = lax.broadcasted_iota(jnp.int32, wide.shape, 0) == lax.broadcasted_iota(
        jnp.int32, wide.shape, 1
    )
    out_col = jnp.sum(jnp.where(same, wide, 0.0), axis=1, keepdims=True)
    first_row = lax.broadcasted_iota(jnp.int32, (prop_hidden, width), 0) == 0

    def accumulate(q, total):
        row = slope_ref[pl.ds(q, 1), :]
        kept = saved_ref[q]
        hidden_grad = jnp.where(kept[features:].astype(F32) > 0, out_col * row, 0.0).astype(BF16)
        alone = jnp.where(first_row, row, 0.0).astype(BF16)
        return total + dot_nt(jnp.concatenate([hidden_grad, alone], axis=0), kept)

    total = jnp.zeros((2 * prop_hidden, saved_ref.shape[1]), F32)
    if masks:
        for q in range(parts):
            total = accumulate(q, total)
    else:
        total = lax.fori_loop(0, parts, accumulate, total)
    grad_ref[...] = total


def backward(me, stats, dense, saved, prop_out, marks, cap):
    key, hot, *masks = marks
    parts, slots = key.shape
    width = dense.shape[2]
    prop_hidden = prop_out.shape[1]
    vmem = pl.BlockSpec(memory_space=pltpu.VMEM)
    return pl.pallas_call(
        functools.partial(backward_kernel, cap),
        out_shape=(
            jax.ShapeDtypeStruct((1, RAY_DEV), F32),
            jax.ShapeDtypeStruct((2 * prop_hidden, saved.shape[1]), F32),
        ),
        in_specs=[pl.BlockSpec(memory_space=pltpu.SMEM)] + [vmem] * (6 + len(masks)),
        out_specs=(vmem, vmem),
        scratch_shapes=[pltpu.VMEM((parts, width), F32)]
        + ([] if masks else [pltpu.VMEM((slots, parts), F32)]),
        compiler_params=pltpu.CompilerParams(vmem_limit_bytes=(12 if masks else 48) * 1024 * 1024),
        name="backward",
    )(me, stats, key, hot, dense, saved, prop_out, *masks)


def finish_kernel(own_ref, one_ref, two_ref, three_ref, in_ref, out_ref):
    total = (own_ref[...] + one_ref[...]) + (two_ref[...] + three_ref[...])
    prop_hidden, features = in_ref.shape
    in_ref[...] = total[:prop_hidden, :features]
    out_ref[...] = total[prop_hidden : prop_hidden + 1, features:]


def sum_replicas(x, prop_hidden, features):
    count = lax.axis_size("rep")
    if count != 4:
        x = lax.psum(x, "rep")
        return x[:prop_hidden, :features], x[prop_hidden : prop_hidden + 1, features:]
    other = [lax.ppermute(x, "rep", [(i, i ^ s) for i in range(count)]) for s in (1, 2, 3)]
    vmem = pl.BlockSpec(memory_space=pltpu.VMEM)
    return pl.pallas_call(
        finish_kernel,
        out_shape=(
            jax.ShapeDtypeStruct((prop_hidden, features), F32),
            jax.ShapeDtypeStruct((1, prop_hidden), F32),
        ),
        in_specs=[vmem] * 4,
        out_specs=(vmem, vmem),
        compiler_params=pltpu.CompilerParams(vmem_limit_bytes=4 * 1024 * 1024),
        name="finish",
    )(x, *other)


def on_device(
    feature_grid,
    fine_in,
    fine_mid,
    fine_out,
    prop_in,
    prop_out,
    sample_cells,
    sample_geometry,
    slot_ray,
    slot_rank,
    bucket_count,
):
    parts = lax.axis_size("dom")
    cap = slot_ray.shape[3]
    features = feature_grid.shape[1]
    prop_hidden = prop_in.shape[1]
    outgoing = pack(
        sample_geometry[:, 0, 0], slot_ray[0, 0], slot_rank[0, 0], bucket_count.reshape(-1)
    )
    arrived = lax.all_to_all(outgoing, "dom", split_axis=0, concat_axis=0, tiled=True)
    saved, dense, summary = forward(
        sample_cells.reshape(-1), feature_grid[0], arrived,
        fine_in[0].T, prop_in[0], fine_mid[0], fine_out, prop_out, cap,
    )
    stats = lax.all_to_all(summary, "dom", split_axis=0, concat_axis=0, tiled=True)
    me = lax.axis_index("dom").reshape(1).astype(jnp.int32)
    marks = slot_marks(me, arrived, cap)
    ray_loss, grads = backward(me, stats, dense, saved, prop_out, marks, cap)
    in_sum, out_sum = sum_replicas(grads, prop_hidden, features)
    return (ray_loss.reshape(1, 1, -1), in_sum[None], out_sum)


def solution(mesh):
    return jax.shard_map(
        on_device,
        mesh=mesh,
        in_specs=(
            P("dom", None, None),
            P("dom", None, None),
            P("dom", None, None, None),
            P("dom", None),
            P("dom", None, None),
            P("dom", None),
            P("dom", "rep", None, None),
            P(None, "dom", "rep", None, None),
            P("dom", "rep", None, None),
            P("dom", "rep", None, None),
            P("dom", "rep", None),
        ),
        out_specs=(P("dom", "rep", None), P("dom", None, None), P("dom", None)),
        check_vma=False,
    )
```
